32 devices in a mesh: dp: 8 (over z, y), tensor: 4 (over x, core).
Axes of the slice: x: 2, y: 2, z: 4, core: 2. Of those that a mesh axis runs over, the one named last changes fastest.
Arguments:
- tokens: bfloat16 [4096, 2048], P('dp'), may hold values from -6 to 6
- g_attn: float32 [2048], replicated, may hold values from 0.25 to 1.75
- w_query: bfloat16 [2048, 2048], P(None, 'tensor'), may hold values from -0.125 to 0.125
- w_key: bfloat16 [2048, 1024], P(None, 'tensor'), may hold values from -0.125 to 0.125
- w_value: bfloat16 [2048, 1024], P(None, 'tensor'), may hold values from -0.125 to 0.125
- q_gain: float32 [128], replicated, may hold values from 0.25 to 1.75
- k_gain: float32 [128], replicated, may hold values from 0.25 to 1.75
- w_out: bfloat16 [2048, 2048], P('tensor'), may hold values from -0.5 to 0.5
- g_mlp: float32 [2048], replicated, may hold values from 0.25 to 1.75
- w_gate: bfloat16 [2048, 6144], P(None, 'tensor'), may hold values from -0.125 to 0.125
- w_up: bfloat16 [2048, 6144], P(None, 'tensor'), may hold values from -0.125 to 0.125
- w_down: bfloat16 [6144, 2048], P('tensor'), may hold values from -0.078125 to 0.078125
- cotangent: bfloat16 [4096, 2048], P('dp'), may hold values from -6 to 6
Outputs:
- output: bfloat16 [4096, 2048], P('dp')
- grad_tokens: float32 [4096, 2048], P('dp')
- grad_g_attn: float32 [2048], replicated
- grad_query: float32 [2048, 2048], P('dp', 'tensor')
- grad_key: float32 [2048, 1024], P('dp', 'tensor')
- grad_value: float32 [2048, 1024], P('dp', 'tensor')
- grad_q_gain: float32 [128], replicated
- grad_k_gain: float32 [128], replicated
- grad_out: float32 [2048, 2048], P('tensor', 'dp')
- grad_g_mlp: float32 [2048], replicated
- grad_gate: float32 [2048, 6144], P('dp', 'tensor')
- grad_up: float32 [2048, 6144], P('dp', 'tensor')
- grad_down: float32 [6144, 2048], P('tensor', 'dp')
The draws below stay inside these ranges and needn't reach their ends.
All inputs are finite; a program needn't handle non-finite values.
Results may differ from the reference program's by a relative error of at most 0.014.
Values sent between devices are 32-bit elements; how exact they have to be, the bound alone decides.
No kernel may reach another device: no remote copies, remote signals or barrier semaphores. Data moves between devices by JAX's collectives and lax.ppermute only.
A program may use at most 256 MiB of HBM per device.

```python
import jax
import jax.numpy as jnp
from jax import lax

D = 2048
H = 16
KV = 8
HD = 128
FF = 6144
SEQ_LEN = 256
SEQ_DEV = 2
TOKENS = 4096
N_DP = 8


def spiked(array, rng, source, target, parts, factor):
    owner, partner = [(jnp.arange(array.shape[position]) // (array.shape[position] // parts)).reshape([-1 if axis == position else 1 for axis in range(array.ndim)]) for position in (source, target)]
    chosen = jax.random.permutation(rng, parts)[partner]
    strong = (owner == chosen) | (owner == (partner + parts // 2) % parts)
    return jnp.where(strong, factor * array, array)


def level_of(rng, dims, shards, low, largest):
    def one(axis_at, blocks):
        draws = jax.random.uniform(jax.random.fold_in(jax.random.fold_in(rng, 6), axis_at), (blocks,), jnp.float32, low / len(shards), largest / len(shards))
        return jnp.repeat(jnp.exp(draws), dims[axis_at] // blocks).reshape((-1,) + (1,) * (len(dims) - axis_at - 1))

    loudness = one(*shards[0])
    for cut in shards[1:]:
        loudness = loudness * one(*cut)
    return loudness


def centred(key, extent, scale, reach, shards=(), dtype=jnp.bfloat16):
    array = jax.random.normal(key, extent, jnp.float32) * scale
    if len(shards) > 0:
        array = level_of(key, extent, shards, -0.22, 0.18) * array
    return jnp.clip(array, min=-reach, max=reach).astype(dtype)


def heavy_noise(key, extent, scale, reach, cuts, heavy, kind=jnp.bfloat16):
    values = scale * jax.random.normal(key, extent, jnp.float32)
    if cuts:
        values = values * level_of(key, extent, cuts, -0.22, 0.18)
    return jnp.clip(spiked(values, jax.random.fold_in(key, 3), *heavy), -reach, reach).astype(kind)


def setup_inputs(seed: int = 0) -> dict:
    arg_keys = jax.random.split(jax.random.key(seed), 14)
    tokens = heavy_noise(arg_keys[0], (TOKENS, D), 1.0, 6.0, ((0, 8),), (0, 1, 8, 2.0))
    g_attn = jnp.clip(1.0 + 0.15 * jax.random.normal(arg_keys[1], (D,), jnp.float32), 0.25, 1.75)
    w_query = centred(arg_keys[2], (D, H * HD), D ** -0.5, 0.125, ((1, 4),))
    w_key = centred(arg_keys[3], (D, KV * HD), D ** -0.5, 0.125, ((1, 4),))
    w_value = centred(arg_keys[4], (D, KV * HD), D ** -0.5, 0.125, ((1, 4),))
    q_gain = jnp.clip(1.0 + 0.15 * jax.random.normal(arg_keys[5], (HD,), jnp.float32), 0.25, 1.75)
    k_gain = jnp.clip(1.0 + 0.15 * jax.random.normal(arg_keys[6], (HD,), jnp.float32), 0.25, 1.75)
    w_out = centred(arg_keys[7], (H * HD, D), (H * HD // 16) ** -0.5, 0.5, ((0, 4),))
    g_mlp = jnp.clip(1.0 + 0.15 * jax.random.normal(arg_keys[8], (D,), jnp.float32), 0.25, 1.75)
    w_gate = centred(arg_keys[9], (D, FF), D ** -0.5, 0.125, ((1, 4),))
    w_up = centred(arg_keys[10], (D, FF), D ** -0.5, 0.125, ((1, 4),))
    w_down = centred(arg_keys[11], (FF, D), FF ** -0.5, 0.078125, ((0, 4),))
    cotangent = heavy_noise(arg_keys[12], (TOKENS, D), 1.0, 6.0, ((0, 8),), (0, 1, 8, 2.0))
    return dict(tokens=tokens, g_attn=g_attn, w_query=w_query, w_key=w_key, w_value=w_value, q_gain=q_gain, k_gain=k_gain, w_out=w_out, g_mlp=g_mlp, w_gate=w_gate, w_up=w_up, w_down=w_down, cotangent=cotangent)


EPS = 1e-06
THETA = 1000000.0

def rope_tables(length, width):
    half = width // 2
    inverse = THETA ** (-(jnp.arange(half).astype(jnp.float32) * 2.0 / width))
    angles = jnp.arange(length).astype(jnp.float32)[:, None] * inverse[None, :]
    angles = jnp.concatenate([angles, angles], axis=1)
    return (jnp.cos(angles)[None, :, None, :], jnp.sin(angles)[None, :, None, :])

def rotate(values, cosine, sine):
    half = values.shape[-1] // 2
    turned = jnp.concatenate([-values[..., half:], values[..., :half]], axis=-1)
    return values * cosine + turned * sine

def rotate_back(grads, cosine, sine):
    half = grads.shape[-1] // 2
    sined = grads * sine
    return grads * cosine + jnp.concatenate([sined[..., half:], -sined[..., :half]], axis=-1)

def rms_norm(values, gain):
    inv_rms = lax.rsqrt(lax.optimization_barrier(jnp.mean(values * values, axis=-1, keepdims=True)) + EPS)
    unit_rows = values * inv_rms
    return (unit_rows * gain, unit_rows, inv_rms)

def rms_back(grads, gain, unit_rows, inv_rms):
    scaled = grads * gain
    return inv_rms * (scaled - unit_rows * lax.optimization_barrier(jnp.mean(scaled * unit_rows, axis=-1, keepdims=True)))

def causal_scores(query_five, keys, scale):
    length = query_five.shape[1]
    scores = jnp.einsum('sqkgd,spkd->skgqp', query_five.astype(jnp.float32), keys.astype(jnp.float32)) * scale
    allowed = jnp.arange(length)[:, None] >= jnp.arange(length)[None, :]
    return jnp.where(allowed, scores, -1e+30)

def layer(x_block, cot_block, g_attn, w_query, w_key, w_value, q_gain, k_gain, w_out, g_mlp, w_gate, w_up, w_down):
    f32 = jnp.float32
    b16 = jnp.bfloat16
    rows = x_block.shape[0]
    head_dim = q_gain.shape[0]
    heads = w_query.shape[1] // head_dim
    kv_heads = w_key.shape[1] // head_dim
    group = heads // kv_heads
    seqs = rows // SEQ_LEN
    scale = head_dim ** (-0.5)
    cosine, sine = rope_tables(SEQ_LEN, head_dim)
    x_full = x_block.astype(f32)
    normed1, unit1, rms1 = rms_norm(x_full, g_attn)
    normed1 = normed1.astype(b16)
    query = jnp.dot(normed1, w_query, preferred_element_type=f32).reshape(seqs, SEQ_LEN, heads, head_dim)
    keyvec = jnp.dot(normed1, w_key, preferred_element_type=f32).reshape(seqs, SEQ_LEN, kv_heads, head_dim)
    values = jnp.dot(normed1, w_value, preferred_element_type=f32).astype(b16).reshape(seqs, SEQ_LEN, kv_heads, head_dim)
    q_normed, q_unit, q_inv = rms_norm(query, q_gain)
    k_normed, k_unit, k_inv = rms_norm(keyvec, k_gain)
    q_rot = rotate(q_normed, cosine, sine).astype(b16)
    k_rot = rotate(k_normed, cosine, sine).astype(b16)
    q_group = q_rot.reshape(seqs, SEQ_LEN, kv_heads, group, head_dim)
    scores = causal_scores(q_group, k_rot, scale)
    row_top = lax.optimization_barrier(jnp.max(scores, axis=-1, keepdims=True))
    log_total = row_top + jnp.log(lax.optimization_barrier(jnp.sum(jnp.exp(scores - row_top), axis=-1, keepdims=True)))
    probs = jnp.exp(scores - log_total)
    probs_b = probs.astype(b16)
    att_five = jnp.einsum('skgqp,spkd->sqkgd', probs_b.astype(f32), values.astype(f32)).astype(b16)
    attended = att_five.reshape(rows, heads * head_dim)
    resid = x_full + jnp.dot(attended, w_out, preferred_element_type=f32)
    normed2, unit2, rms2 = rms_norm(resid, g_mlp)
    normed2 = normed2.astype(b16)
    gate_pre = jnp.dot(normed2, w_gate, preferred_element_type=f32)
    up_pre = jnp.dot(normed2, w_up, preferred_element_type=f32)
    sigmoid_g = jax.nn.sigmoid(gate_pre)
    act_gate = gate_pre * sigmoid_g
    hidden = (act_gate * up_pre).astype(b16)
    output = (resid + jnp.dot(hidden, w_down, preferred_element_type=f32)).astype(b16)
    grad_down = jnp.dot(hidden.T, cot_block, preferred_element_type=f32)
    d_hidden = jnp.dot(cot_block, w_down.T, preferred_element_type=f32)
    d_up = (d_hidden * act_gate).astype(b16)
    d_gate = (d_hidden * up_pre * (sigmoid_g * (1.0 + gate_pre * (1.0 - sigmoid_g)))).astype(b16)
    grad_gate = jnp.dot(normed2.T, d_gate, preferred_element_type=f32)
    grad_up = jnp.dot(normed2.T, d_up, preferred_element_type=f32)
    d_norm2 = jnp.dot(d_gate, w_gate.T, preferred_element_type=f32) + jnp.dot(d_up, w_up.T, preferred_element_type=f32)
    grad_g_mlp = lax.optimization_barrier(jnp.sum(d_norm2 * unit2, axis=0))
    d_resid = cot_block.astype(f32) + rms_back(d_norm2, g_mlp, unit2, rms2)
    d_resid_b = d_resid.astype(b16)
    grad_out = jnp.dot(attended.T, d_resid_b, preferred_element_type=f32)
    d_att = jnp.dot(d_resid_b, w_out.T, preferred_element_type=f32).astype(b16)
    d_att_five = d_att.reshape(seqs, SEQ_LEN, kv_heads, group, head_dim)
    d_prob = jnp.einsum('sqkgd,spkd->skgqp', d_att_five.astype(f32), values.astype(f32))
    delta = lax.optimization_barrier(jnp.sum(d_att_five.astype(f32) * att_five.astype(f32), axis=-1))
    delta = jnp.transpose(delta, (0, 2, 3, 1))[..., None]
    d_score = (probs * (d_prob - delta) * scale).astype(b16)
    d_qrot = jnp.einsum('skgqp,spkd->sqkgd', d_score.astype(f32), k_rot.astype(f32)).reshape(seqs, SEQ_LEN, heads, head_dim)
    d_krot = jnp.einsum('skgqp,sqkgd->spkd', d_score.astype(f32), q_group.astype(f32))
    d_values = jnp.einsum('skgqp,sqkgd->spkd', probs_b.astype(f32), d_att_five.astype(f32))
    d_qn = rotate_back(d_qrot, cosine, sine)
    d_kn = rotate_back(d_krot, cosine, sine)
    grad_q_gain = lax.optimization_barrier(jnp.sum(d_qn * q_unit, axis=(0, 1, 2)))
    grad_k_gain = lax.optimization_barrier(jnp.sum(d_kn * k_unit, axis=(0, 1, 2)))
    d_query_b = rms_back(d_qn, q_gain, q_unit, q_inv).astype(b16).reshape(rows, heads * head_dim)
    d_keys_b = rms_back(d_kn, k_gain, k_unit, k_inv).astype(b16).reshape(rows, kv_heads * head_dim)
    d_values_b = d_values.astype(b16).reshape(rows, kv_heads * head_dim)
    grad_query = jnp.dot(normed1.T, d_query_b, preferred_element_type=f32)
    grad_key = jnp.dot(normed1.T, d_keys_b, preferred_element_type=f32)
    grad_value = jnp.dot(normed1.T, d_values_b, preferred_element_type=f32)
    d_norm1 = jnp.dot(d_query_b, w_query.T, preferred_element_type=f32) + jnp.dot(d_keys_b, w_key.T, preferred_element_type=f32) + jnp.dot(d_values_b, w_value.T, preferred_element_type=f32)
    grad_g_attn = lax.optimization_barrier(jnp.sum(d_norm1 * unit1, axis=0))
    grad_tokens = d_resid + rms_back(d_norm1, g_attn, unit1, rms1)
    grads = (grad_g_attn, grad_query, grad_key, grad_value, grad_q_gain, grad_k_gain, grad_out, grad_g_mlp, grad_gate, grad_up, grad_down)
    return (output, grad_tokens, grads)

def reference(tokens, g_attn, w_query, w_key, w_value, q_gain, k_gain, w_out, g_mlp, w_gate, w_up, w_down, cotangent):
    block_rows = SEQ_DEV * SEQ_LEN
    width = tokens.shape[1]
    blocks_x = tokens.reshape(N_DP, block_rows, width)
    blocks_c = cotangent.reshape(N_DP, block_rows, width)
    shaped = (g_attn, w_query, w_key, w_value, q_gain, k_gain, w_out, g_mlp, w_gate, w_up, w_down)
    initial = tuple((jnp.zeros(item.shape, jnp.float32) for item in shaped))

    def step(carry, pair):
        output, grad_tokens, grads = layer(pair[0], pair[1], g_attn, w_query, w_key, w_value, q_gain, k_gain, w_out, g_mlp, w_gate, w_up, w_down)
        return (tuple((total + grad for total, grad in zip(carry, grads))), (output, grad_tokens))
    totals, (outputs, grad_rows) = lax.scan(step, initial, (blocks_x, blocks_c))
    return (outputs.reshape(tokens.shape), grad_rows.reshape(tokens.shape), totals[0], totals[1], totals[2], totals[3], totals[4], totals[5], totals[6], totals[7], totals[8], totals[9], totals[10])
```

```python
import jax
import jax.numpy as jnp
from jax import lax
from jax.sharding import PartitionSpec as P

SEQ_LEN = 256


EPS = 1e-06
THETA = 1000000.0

f32 = jnp.float32
b16 = jnp.bfloat16


def rope_tables(length, width):
    half = width // 2
    inverse = THETA ** (-(jnp.arange(half).astype(jnp.float32) * 2.0 / width))
    angles = jnp.arange(length).astype(jnp.float32)[:, None] * inverse[None, :]
    angles = jnp.concatenate([angles, angles], axis=1)
    return (jnp.cos(angles)[None, :, None, :], jnp.sin(angles)[None, :, None, :])


def rotate(values, cosine, sine):
    half = values.shape[-1] // 2
    turned = jnp.concatenate([-values[..., half:], values[..., :half]], axis=-1)
    return values * cosine + turned * sine


def rotate_back(grads, cosine, sine):
    half = grads.shape[-1] // 2
    sined = grads * sine
    return grads * cosine + jnp.concatenate([sined[..., half:], -sined[..., :half]], axis=-1)


def rms_norm(values, gain):
    inv_rms = lax.rsqrt(jnp.mean(values * values, axis=-1, keepdims=True) + EPS)
    unit_rows = values * inv_rms
    return (unit_rows * gain, unit_rows, inv_rms)


def rms_back(grads, gain, unit_rows, inv_rms):
    scaled = grads * gain
    return inv_rms * (scaled - unit_rows * jnp.mean(scaled * unit_rows, axis=-1, keepdims=True))


def causal_scores(query_five, keys, scale):
    length = query_five.shape[1]
    scores = (
        jnp.einsum("sqkgd,spkd->skgqp", query_five, keys, preferred_element_type=jnp.float32)
        * scale
    )
    allowed = jnp.arange(length)[:, None] >= jnp.arange(length)[None, :]
    return jnp.where(allowed, scores, -1e30)


def swap(value, axis, mask):
    size = lax.axis_size(axis)
    return lax.ppermute(value, axis, [(i, i ^ mask) for i in range(size)])


def dot(a, b):
    return jnp.dot(a, b, preferred_element_type=f32)


def dot_nt(a, b):
    return lax.dot_general(a, b, (((1,), (1,)), ((), ())), preferred_element_type=f32)


def dot_tn(a, b):
    return lax.dot_general(a, b, (((0,), (0,)), ((), ())), preferred_element_type=f32)


def tensor_masks():
    size = lax.axis_size("tensor")
    return [1 << i for i in range(1, size.bit_length() - 1)]


def halves_sum(mine, theirs):
    total = mine + swap(theirs, "tensor", 1)
    for mask in tensor_masks():
        total = total + swap(total, "tensor", mask)
    return total


def scatter_sum(parts, masks):
    for mask in masks:
        half = len(parts) // 2
        received = [swap(p, "dp", mask) for p in parts[half:]]
        parts = [a + b for a, b in zip(parts[:half], received)]
    return parts[0]


def relative(masks):
    offsets = [0]
    for mask in reversed(masks):
        offsets = offsets + [o ^ mask for o in offsets]
    return offsets


def body(
    tokens,
    g_attn,
    w_query,
    w_key,
    w_value,
    q_gain,
    k_gain,
    w_out,
    g_mlp,
    w_gate,
    w_up,
    w_down,
    cotangent,
):
    rows, width = tokens.shape
    head_dim = q_gain.shape[0]
    heads = w_query.shape[1] // head_dim
    kv_heads = w_key.shape[1] // head_dim
    group = heads // kv_heads
    seqs = rows // SEQ_LEN
    scale = head_dim ** (-0.5)
    cosine, sine = rope_tables(SEQ_LEN, head_dim)

    n_dp = lax.axis_size("dp")
    me = lax.axis_index("dp")
    core = lax.axis_index("tensor") % 2
    half = rows // 2
    block = width // n_dp
    bits = [1 << i for i in range(n_dp.bit_length() - 1)]
    near, far = bits[0], bits[-1]
    middle = bits[1:-1]

    def mine_of(a):
        return lax.dynamic_slice_in_dim(a, core * half, half, 0)

    def theirs_of(a):
        return lax.dynamic_slice_in_dim(a, (1 - core) * half, half, 0)

    def in_order(mine, theirs):
        out = jnp.zeros((rows,) + mine.shape[1:], mine.dtype)
        out = lax.dynamic_update_slice_in_dim(out, mine, core * half, 0)
        return lax.dynamic_update_slice_in_dim(out, theirs, (1 - core) * half, 0)

    def columns(a, offset):
        return lax.dynamic_slice_in_dim(a, (me ^ offset) * block, block, 1)

    cot_mine, cot_theirs = mine_of(cotangent), theirs_of(cotangent)
    cot_own = jnp.concatenate([cot_mine, cot_theirs])
    c0 = cot_mine.astype(f32) * 2.0
    c1 = swap(c0, "dp", near)
    c2 = swap(c0, "dp", far)
    c3 = swap(c2, "dp", near)
    cot_near = (jnp.concatenate([c1, swap(c1, "tensor", 1)]) * 0.5).astype(b16)
    c23 = jnp.concatenate([c2, c3])
    cot_far = (jnp.concatenate([c23, swap(c23, "tensor", 1)]) * 0.5).astype(b16)

    tok = jnp.concatenate([mine_of(tokens), theirs_of(tokens)])
    x_full = tok.astype(f32)
    normed1, unit1, rms1 = rms_norm(x_full, g_attn)
    normed1 = normed1.astype(b16)
    query = dot(normed1, w_query).reshape(seqs, SEQ_LEN, heads, head_dim)
    keyvec = dot(normed1, w_key).reshape(seqs, SEQ_LEN, kv_heads, head_dim)
    values = dot(normed1, w_value).astype(b16).reshape(seqs, SEQ_LEN, kv_heads, head_dim)
    q_normed, q_unit, q_inv = rms_norm(query, q_gain)
    k_normed, k_unit, k_inv = rms_norm(keyvec, k_gain)
    q_rot = rotate(q_normed, cosine, sine).astype(b16)
    k_rot = rotate(k_normed, cosine, sine).astype(b16)
    q_group = q_rot.reshape(seqs, SEQ_LEN, kv_heads, group, head_dim)
    scores = causal_scores(q_group, k_rot, scale)
    row_top = jnp.max(scores, axis=-1, keepdims=True)
    log_total = row_top + jnp.log(jnp.sum(jnp.exp(scores - row_top), axis=-1, keepdims=True))
    probs = jnp.exp(scores - log_total)
    probs_b = probs.astype(b16)
    att_five = jnp.einsum("skgqp,spkd->sqkgd", probs_b, values, preferred_element_type=f32).astype(
        b16
    )
    attended = att_five.reshape(rows, heads * head_dim)
    mixed = dot(attended, w_out)
    resid_mine = x_full[:half] + halves_sum(mixed[:half], mixed[half:])
    _, n0, _ = rms_norm(resid_mine, g_mlp)
    n1 = swap(n0, "dp", near)
    n2 = swap(n0, "dp", far)
    n3 = swap(n2, "dp", near)
    resid = jnp.concatenate([resid_mine, swap(resid_mine, "tensor", 1)])
    normed2, unit2, rms2 = rms_norm(resid, g_mlp)
    normed2 = normed2.astype(b16)

    def feed(normed, cot):
        gate_pre = dot(normed, w_gate)
        up_pre = dot(normed, w_up)
        d_hidden = dot_nt(cot, w_down)
        sigmoid_g = jax.nn.sigmoid(gate_pre)
        act_gate = gate_pre * sigmoid_g
        hidden = (act_gate * up_pre).astype(b16)
        d_up = (d_hidden * act_gate).astype(b16)
        d_gate = (
            d_hidden * up_pre * (sigmoid_g * (1.0 + gate_pre * (1.0 - sigmoid_g)))
        ).astype(b16)
        return hidden, d_gate, d_up

    hidden, d_gate, d_up = feed(normed2, cot_own)
    dn_part = dot_nt(d_gate, w_gate) + dot_nt(d_up, w_up)
    down_part = dot(hidden, w_down)
    mlp_gain_term = jnp.sum(dn_part * unit2, axis=0)
    dn_mine = halves_sum(dn_part[:half], dn_part[half:])
    down_mine = halves_sum(down_part[:half], down_part[half:])

    normed2_near = (jnp.concatenate([n1, swap(n1, "tensor", 1)]) * g_mlp).astype(b16)
    n23 = jnp.concatenate([n2, n3])
    normed2_far = (jnp.concatenate([n23, swap(n23, "tensor", 1)]) * g_mlp).astype(b16)
    near_parts = feed(normed2_near, cot_near)
    far_parts = feed(normed2_far, cot_far)
    all_hidden, all_gate, all_up = (
        jnp.concatenate(list(three)) for three in zip((hidden, d_gate, d_up), near_parts, far_parts)
    )
    all_cot = jnp.concatenate([cot_own, cot_near, cot_far])
    all_normed = jnp.concatenate([normed2, normed2_near, normed2_far])
    offsets = relative(middle)
    summed_down = scatter_sum([dot_tn(all_hidden, columns(all_cot, o)) for o in offsets], middle)
    summed_gate = scatter_sum([dot_tn(columns(all_normed, o), all_gate) for o in offsets], middle)
    summed_up = scatter_sum([dot_tn(columns(all_normed, o), all_up) for o in offsets], middle)

    d_norm2 = jnp.concatenate([dn_mine, swap(dn_mine, "tensor", 1)])
    d_resid = cot_own.astype(f32) + rms_back(d_norm2, g_mlp, unit2, rms2)
    d_resid_b = d_resid.astype(b16)
    down_sum = jnp.concatenate([down_mine, swap(down_mine, "tensor", 1)])
    out_own = (resid + down_sum).astype(b16)
    output = in_order(out_own[:half], out_own[half:])

    every = [near] + middle + [far]
    blocks = relative(every)
    summed_out = scatter_sum([dot_tn(attended, columns(d_resid_b, o)) for o in blocks], every)
    d_att = dot_nt(d_resid_b, w_out).astype(b16)
    d_att_five = d_att.reshape(seqs, SEQ_LEN, kv_heads, group, head_dim)
    d_prob = jnp.einsum("sqkgd,spkd->skgqp", d_att_five, values, preferred_element_type=f32)
    delta = jnp.sum(d_att_five.astype(f32) * att_five.astype(f32), axis=-1)
    delta = jnp.transpose(delta, (0, 2, 3, 1))[..., None]
    d_score = (probs * (d_prob - delta) * scale).astype(b16)
    d_qrot = jnp.einsum("skgqp,spkd->sqkgd", d_score, k_rot, preferred_element_type=f32).reshape(
        seqs, SEQ_LEN, heads, head_dim
    )
    d_krot = jnp.einsum("skgqp,sqkgd->spkd", d_score, q_group, preferred_element_type=f32)
    d_values = jnp.einsum("skgqp,sqkgd->spkd", probs_b, d_att_five, preferred_element_type=f32)
    d_qn = rotate_back(d_qrot, cosine, sine)
    d_kn = rotate_back(d_krot, cosine, sine)
    q_gain_term = jnp.sum(d_qn * q_unit, axis=(0, 1, 2))
    k_gain_term = jnp.sum(d_kn * k_unit, axis=(0, 1, 2))
    d_query_b = rms_back(d_qn, q_gain, q_unit, q_inv).astype(b16).reshape(rows, heads * head_dim)
    d_keys_b = rms_back(d_kn, k_gain, k_unit, k_inv).astype(b16).reshape(rows, kv_heads * head_dim)
    d_values_b = d_values.astype(b16).reshape(rows, kv_heads * head_dim)
    d1_part = dot_nt(d_query_b, w_query) + dot_nt(d_keys_b, w_key) + dot_nt(d_values_b, w_value)
    attn_gain_term = jnp.sum(d1_part * unit1, axis=0)
    gains = jnp.concatenate([attn_gain_term, q_gain_term, k_gain_term, mlp_gain_term])
    for mask in [1] + tensor_masks():
        gains = gains + swap(gains, "tensor", mask)
    for mask in bits:
        gains = gains + swap(gains, "dp", mask)
    hd = head_dim
    gain_attn, gain_q, gain_k, gain_mlp = (
        gains[:width],
        gains[width : width + hd],
        gains[width + hd : width + 2 * hd],
        gains[width + 2 * hd :],
    )
    d_qkv = jnp.concatenate([d_query_b, d_keys_b, d_values_b], axis=1)
    summed_qkv = scatter_sum([dot_tn(columns(normed1, o), d_qkv) for o in blocks], every)
    nq, nk = heads * head_dim, kv_heads * head_dim
    summed_query, summed_key, summed_value = (
        summed_qkv[:, :nq],
        summed_qkv[:, nq : nq + nk],
        summed_qkv[:, nq + nk :],
    )
    d1_mine = halves_sum(d1_part[:half], d1_part[half:])
    gt_mine = d_resid[:half] + rms_back(d1_mine, g_attn, unit1[:half], rms1[:half])
    grad_tokens = in_order(gt_mine, swap(gt_mine, "tensor", 1))
    return (
        output,
        grad_tokens,
        gain_attn,
        summed_query,
        summed_key,
        summed_value,
        gain_q,
        gain_k,
        summed_out,
        gain_mlp,
        summed_gate,
        summed_up,
        summed_down,
    )


def solution(mesh):
    in_specs = (
        P("dp", None),
        P(),
        P(None, "tensor"),
        P(None, "tensor"),
        P(None, "tensor"),
        P(),
        P(),
        P("tensor", None),
        P(),
        P(None, "tensor"),
        P(None, "tensor"),
        P("tensor", None),
        P("dp", None),
    )
    out_specs = (
        P("dp", None),
        P("dp", None),
        P(),
        P("dp", "tensor"),
        P("dp", "tensor"),
        P("dp", "tensor"),
        P(),
        P(),
        P("tensor", "dp"),
        P(),
        P("dp", "tensor"),
        P("dp", "tensor"),
        P("tensor", "dp"),
    )
    return jax.shard_map(body, mesh=mesh, in_specs=in_specs, out_specs=out_specs, check_vma=False)
```

```python
import functools

import jax
import jax.numpy as jnp
from jax import lax
from jax.experimental import pallas as pl
from jax.experimental.pallas import tpu as pltpu
from jax.sharding import PartitionSpec as P

SEQ_LEN = 256


EPS = 1e-06
THETA = 1000000.0

f32 = jnp.float32
b16 = jnp.bfloat16


def rms_norm(values, gain):
    inv_rms = lax.rsqrt(jnp.mean(values * values, axis=-1, keepdims=True) + EPS)
    unit_rows = values * inv_rms
    return (unit_rows * gain, unit_rows, inv_rms)


def rms_back(grads, gain, unit_rows, inv_rms):
    scaled = grads * gain
    return inv_rms * (scaled - unit_rows * jnp.mean(scaled * unit_rows, axis=-1, keepdims=True))


def swap(value, axis, mask):
    size = lax.axis_size(axis)
    return lax.ppermute(value, axis, [(i, i ^ mask) for i in range(size)])


class Sequence:
    def __init__(self):
        self.token = None

    def __call__(self, *values):
        if self.token is None:
            out = lax.optimization_barrier(values)
        else:
            *out, self.token = lax.optimization_barrier((*values, self.token))
        self.token = out[0].reshape(-1)[:1] if self.token is None else self.token
        return out[0] if len(out) == 1 else tuple(out)


def dot(a, b):
    return jnp.dot(a, b, preferred_element_type=f32)


def dot_nt(a, b):
    return lax.dot_general(a, b, (((1,), (1,)), ((), ())), preferred_element_type=f32)


def dot_tn(a, b):
    return lax.dot_general(a, b, (((0,), (0,)), ((), ())), preferred_element_type=f32)


TILE = 512
PIECES = 4


def vmem(mib=60):
    return pltpu.CompilerParams(vmem_limit_bytes=mib << 20)


def whole(shape):
    return pl.BlockSpec(shape, lambda *_: (0,) * len(shape))


def gated(nb, cb, wg_ref, wu_ref, wd_ref):
    gate_pre = dot(nb[...], wg_ref[...])
    up_pre = dot(nb[...], wu_ref[...])
    d_hidden = dot_nt(cb[...], wd_ref[...])
    sig = jax.nn.sigmoid(gate_pre)
    act = gate_pre * sig
    hidden = (act * up_pre).astype(b16)
    d_up = (d_hidden * act).astype(b16)
    d_gate = (d_hidden * up_pre * (sig * (1.0 + gate_pre * (1.0 - sig)))).astype(b16)
    return hidden, d_gate, d_up


def own_kernel(ra_ref, *refs):
    rb_refs, refs = refs[:PIECES], refs[PIECES:]
    cot_ref, g_ref, wg_ref, wu_ref, wd_ref, normed_ref, hid_ref, dg_ref, du_ref, dna_ref = refs[:10]
    dnb_refs, (gain_ref, rms_ref) = refs[10:-2], refs[-2:]
    step = pl.program_id(0)
    half = ra_ref.shape[0]
    part = half // PIECES

    @pl.when(step == 0)
    def _():
        for i, ref in enumerate((ra_ref, *rb_refs)):
            r = ref[...]
            at = 0 if i == 0 else half + (i - 1) * part
            inv = lax.rsqrt(jnp.mean(r * r, axis=-1, keepdims=True) + EPS)
            rms_ref[at : at + r.shape[0], :] = inv
            normed_ref[at : at + r.shape[0], :] = (r * inv * g_ref[...]).astype(b16)
        dna_ref[...] = jnp.zeros_like(dna_ref)
        for ref in dnb_refs:
            ref[...] = jnp.zeros_like(ref)

    hidden, d_gate, d_up = gated(normed_ref, cot_ref, wg_ref, wu_ref, wd_ref)
    hid_ref[...] = hidden
    dg_ref[...] = d_gate
    du_ref[...] = d_up
    dna_ref[...] += dot_nt(d_gate[:half], wg_ref[...]) + dot_nt(d_up[:half], wu_ref[...])
    far = dot_nt(d_gate[half:], wg_ref[...]) + dot_nt(d_up[half:], wu_ref[...])
    for i, ref in enumerate(dnb_refs):
        ref[...] += far[i * part : (i + 1) * part]

    @pl.when(step == pl.num_programs(0) - 1)
    def _():
        total = jnp.sum(dna_ref[...] * (ra_ref[...] * rms_ref[:half, :]), axis=0, keepdims=True)
        for i, (r_ref, d_ref) in enumerate(zip(rb_refs, dnb_refs)):
            at = half + i * part
            unit = r_ref[...] * rms_ref[at : at + part, :]
            total += jnp.sum(d_ref[...] * unit, axis=0, keepdims=True)
        gain_ref[...] = total


def own_feed(r_a, r_b, cot, g, w_gate, w_up, w_down):
    half, width = r_a.shape
    rows, hidden = 2 * half, w_gate.shape[1]
    col = pl.BlockSpec((rows, TILE), lambda i: (0, i))
    wide = jax.ShapeDtypeStruct((rows, hidden), b16)
    piece = (half // PIECES, width)
    return pl.pallas_call(
        own_kernel,
        grid=(hidden // TILE,),
        in_specs=[whole((half, width))]
        + [whole(piece)] * PIECES
        + [
            whole((rows, width)),
            whole((1, width)),
            pl.BlockSpec((width, TILE), lambda i: (0, i)),
            pl.BlockSpec((width, TILE), lambda i: (0, i)),
            pl.BlockSpec((TILE, width), lambda i: (i, 0)),
        ],
        out_specs=[
            whole((rows, width)),
            col,
            col,
            col,
            whole((half, width)),
        ]
        + [whole(piece)] * PIECES
        + [whole((1, width))],
        out_shape=[
            jax.ShapeDtypeStruct((rows, width), b16),
            wide,
            wide,
            wide,
            jax.ShapeDtypeStruct((half, width), f32),
        ]
        + [jax.ShapeDtypeStruct(piece, f32)] * PIECES
        + [jax.ShapeDtypeStruct((1, width), f32)],
        scratch_shapes=[pltpu.VMEM((rows, 1), f32)],
        compiler_params=vmem(),
        name="own_feed",
    )(r_a, *r_b, cot, g.reshape(1, -1), w_gate, w_up, w_down)


def put_columns(at_ref, cc_ref, nb_ref, cb_ref, where_ref, count, block):
    for j in range(count):
        here = pl.ds(pl.multiple_of(where_ref[j] * block, 128), block)
        at_ref[j * block : (j + 1) * block, :] = nb_ref[:, here].T
        cc_ref[:, j * block : (j + 1) * block] = cb_ref[:, here]


def put_grads(sums, at_ref, cc_ref, hidden, d_gate, d_up, block, before=None):
    down = dot_tn(hidden, cc_ref[...])
    gate = dot(at_ref[...], d_gate)
    up = dot(at_ref[...], d_up)
    count = len(sums) // 2
    for j in range(count):
        part = slice(j * block, (j + 1) * block)
        for k, rows, fresh in (
            (j, slice(None), down[:, part]),
            (count + j, slice(0, block), gate[part]),
            (count + j, slice(block, 2 * block), up[part]),
        ):
            old = 0.0 if before is None else before[k][rows, :]
            sums[k][rows, :] = fresh + old


def rest_kernel(where_ref, nb_ref, cb_ref, hid_ref, dg_ref, du_ref, wd_ref, *rest):
    count = (len(rest) - 4) // 2
    ya_ref, yb_ref, *sums = rest[:-2]
    at_ref, cc_ref = rest[-2:]
    half = ya_ref.shape[0]
    block = cc_ref.shape[1] // count

    @pl.when(pl.program_id(0) == 0)
    def _():
        put_columns(at_ref, cc_ref, nb_ref, cb_ref, where_ref, count, block)
        ya_ref[...] = jnp.zeros_like(ya_ref)
        yb_ref[...] = jnp.zeros_like(yb_ref)

    hidden = hid_ref[...]
    ya_ref[...] += dot(hidden[:half], wd_ref[...])
    yb_ref[...] += dot(hidden[half:], wd_ref[...])
    put_grads(sums, at_ref, cc_ref, hidden, dg_ref[...], du_ref[...], block)


def sum_specs(count, block, hidden):
    specs = [pl.BlockSpec((TILE, block), lambda i, *_: (i, 0))] * count
    specs += [pl.BlockSpec((2 * block, TILE), lambda i, *_: (0, i))] * count
    shapes = [jax.ShapeDtypeStruct((hidden, block), f32)] * count
    shapes += [jax.ShapeDtypeStruct((2 * block, hidden), f32)] * count
    return specs, shapes


def own_rest(where, nb, cb, hidden, d_gate, d_up, w_down, block):
    rows, width = nb.shape
    count = where.shape[0]
    half, ff = rows // 2, hidden.shape[1]
    specs, shapes = sum_specs(count, block, ff)
    col = pl.BlockSpec((rows, TILE), lambda i, *_: (0, i))
    part = jax.ShapeDtypeStruct((half, width), f32)
    out = pl.pallas_call(
        rest_kernel,
        grid_spec=pltpu.PrefetchScalarGridSpec(
            num_scalar_prefetch=1,
            grid=(ff // TILE,),
            in_specs=[
                whole((rows, width)),
                whole((rows, width)),
                col,
                col,
                col,
                pl.BlockSpec((TILE, width), lambda i, *_: (i, 0)),
            ],
            out_specs=[whole((half, width)), whole((half, width))] + specs,
            scratch_shapes=[
                pltpu.VMEM((count * block, rows), b16),
                pltpu.VMEM((rows, count * block), b16),
            ],
        ),
        out_shape=[part, part] + shapes,
        compiler_params=vmem(),
        name="own_rest",
    )(where, nb, cb, hidden, d_gate, d_up, w_down)
    return out[0], out[1], list(out[2:])


def group_kernel(pieces, count, where_ref, *refs):
    n_refs, refs = refs[:pieces], refs[pieces:]
    c_refs, refs = refs[:pieces], refs[pieces:]
    g_ref, wg_ref, wu_ref, wd_ref = refs[:4]
    before = refs[4 : 4 + 2 * count]
    sums = refs[4 + 2 * count : 4 + 4 * count]
    nb_ref, cb_ref, at_ref, cc_ref = refs[4 + 4 * count :]
    block = cc_ref.shape[1] // count

    @pl.when(pl.program_id(0) == 0)
    def _():
        at = 0
        for n_ref, c_ref in zip(n_refs, c_refs):
            size = n_ref.shape[0]
            nb_ref[at : at + size, :] = (n_ref[...] * g_ref[...]).astype(b16)
            cb_ref[at : at + size, :] = (c_ref[...] * 0.5).astype(b16)
            at += size
        put_columns(at_ref, cc_ref, nb_ref, cb_ref, where_ref, count, block)

    hidden, d_gate, d_up = gated(nb_ref, cb_ref, wg_ref, wu_ref, wd_ref)
    put_grads(sums, at_ref, cc_ref, hidden, d_gate, d_up, block, before)


def group_feed(where, ns, cs, g, w_gate, w_up, w_down, before, block):
    width, ff = w_gate.shape
    count = where.shape[0]
    rows = sum(n.shape[0] for n in ns)
    specs, shapes = sum_specs(count, block, ff)
    return list(
        pl.pallas_call(
            functools.partial(group_kernel, len(ns), count),
            grid_spec=pltpu.PrefetchScalarGridSpec(
                num_scalar_prefetch=1,
                grid=(ff // TILE,),
                in_specs=[whole(a.shape) for a in (*ns, *cs)]
                + [
                    whole((1, width)),
                    pl.BlockSpec((width, TILE), lambda i, *_: (0, i)),
                    pl.BlockSpec((width, TILE), lambda i, *_: (0, i)),
                    pl.BlockSpec((TILE, width), lambda i, *_: (i, 0)),
                ]
                + specs,
                out_specs=specs,
                scratch_shapes=[
                    pltpu.VMEM((rows, width), b16),
                    pltpu.VMEM((rows, width), b16),
                    pltpu.VMEM((count * block, rows), b16),
                    pltpu.VMEM((rows, count * block), b16),
                ],
            ),
            out_shape=shapes,
            compiler_params=vmem(),
            name="group_feed",
        )(where, *ns, *cs, g.reshape(1, -1), w_gate, w_up, w_down, *before)
    )


def sum_kernel(count, *refs):
    a_ref, b_refs, outs = refs[0], refs[1 : 1 + count], refs[1 + count :]
    size = a_ref.shape[0] // count
    for i, b_ref in enumerate(b_refs):
        at = slice(i * size, (i + 1) * size)
        total = a_ref[at, :] + b_ref[...]
        outs[0][at, :] = total
        if len(outs) == 1 + count:
            outs[1 + i][...] = total
        elif len(outs) > 1:
            small = outs[1].shape[0]
            for j in range(size // small):
                outs[1 + i * (size // small) + j][...] = total[j * small : (j + 1) * small]


def sum_of(a, bs, split=False):
    shapes = [jax.ShapeDtypeStruct(a.shape, f32)]
    if split:
        shapes += [jax.ShapeDtypeStruct((a.shape[0] // PIECES, a.shape[1]), f32)] * PIECES
    return pl.pallas_call(
        functools.partial(sum_kernel, len(bs)),
        in_specs=[whole(x.shape) for x in (a, *bs)],
        out_specs=[whole(x.shape) for x in shapes],
        out_shape=shapes,
        grid=(1,),
        compiler_params=vmem(),
        name="sum_of",
    )(a, *bs)


def resid_kernel(x_at_ref, tok_ref, a_ref, b_ref, r_ref, n_ref, quarter_ref, *pieces):
    size = pieces[0].shape[0]
    for i, piece in enumerate(pieces):
        at = slice(i * size, (i + 1) * size)
        resid = tok_ref[at, :].astype(f32) + (a_ref[at, :] + b_ref[at, :])
        r_ref[at, :] = resid
        piece[...] = resid
        n_ref[at, :] = resid * lax.rsqrt(jnp.mean(resid * resid, axis=-1, keepdims=True) + EPS)
    small = quarter_ref.shape[0]
    quarter_ref[...] = n_ref[pl.ds(pl.multiple_of(x_at_ref[0] * small, small), small), :]


def resid_of(x_at, tok, a, b):
    rows, width = a.shape
    shapes = [(rows, width), (rows, width), (rows // 2, width)] + [(rows // PIECES, width)] * PIECES
    return pl.pallas_call(
        resid_kernel,
        grid_spec=pltpu.PrefetchScalarGridSpec(
            num_scalar_prefetch=1,
            grid=(1,),
            in_specs=[whole(a.shape)] * 3,
            out_specs=[whole(s) for s in shapes],
        ),
        out_shape=[jax.ShapeDtypeStruct(s, f32) for s in shapes],
        compiler_params=vmem(),
        name="resid_of",
    )(x_at, tok, a, b)


def feed(normed, cot, w_gate, w_up, w_down):
    gate_pre = dot(normed, w_gate)
    up_pre = dot(normed, w_up)
    d_hidden = dot_nt(cot, w_down)
    sigmoid_g = jax.nn.sigmoid(gate_pre)
    act_gate = gate_pre * sigmoid_g
    hidden = (act_gate * up_pre).astype(b16)
    d_up = (d_hidden * act_gate).astype(b16)
    d_gate = (d_hidden * up_pre * (sigmoid_g * (1.0 + gate_pre * (1.0 - sigmoid_g)))).astype(b16)
    return hidden, d_gate, d_up


def plain_grads(where, normed, cot, parts, block):
    hidden, d_gate, d_up = parts
    takes = [functools.partial(lax.dynamic_slice_in_dim, start_index=w * block, slice_size=block, axis=1) for w in where]
    pair = jnp.concatenate([d_gate, d_up], axis=1)
    both = [dot_tn(take(normed), pair) for take in takes]
    ff = hidden.shape[1]
    return [dot_tn(hidden, take(cot)) for take in takes] + [
        jnp.concatenate([b[:, :ff], b[:, ff:]]) for b in both
    ]


def plain_own_feed(r_a, r_b, cot, g, w_gate, w_up, w_down):
    resid = jnp.concatenate([r_a, *r_b])
    normed, unit, _ = rms_norm(resid, g)
    normed = normed.astype(b16)
    parts = feed(normed, cot, w_gate, w_up, w_down)
    total = dot_nt(parts[1], w_gate) + dot_nt(parts[2], w_up)
    half = r_a.shape[0]
    gain = jnp.sum(total * unit, axis=0, keepdims=True)
    return (normed, *parts, total[:half], *jnp.split(total[half:], PIECES), gain)


def plain_own_rest(where, nb, cb, hidden, d_gate, d_up, w_down, block):
    down = dot(hidden, w_down)
    half = nb.shape[0] // 2
    return down[:half], down[half:], plain_grads(where, nb, cb, (hidden, d_gate, d_up), block)


def plain_group_feed(where, ns, cs, g, w_gate, w_up, w_down, before, block):
    normed = (jnp.concatenate(ns) * g).astype(b16)
    cot = (jnp.concatenate(cs) * 0.5).astype(b16)
    parts = feed(normed, cot, w_gate, w_up, w_down)
    return [old + new for old, new in zip(before, plain_grads(where, normed, cot, parts, block))]


def rope_tables(length, width):
    half = width // 2
    inverse = THETA ** (-(jnp.arange(half).astype(f32) * 2.0 / width))
    angles = jnp.arange(length).astype(f32)[:, None] * inverse[None, :]
    angles = jnp.concatenate([angles, angles], axis=1)
    sign = jnp.where(jnp.arange(width) < half, -1.0, 1.0).astype(f32)
    return jnp.cos(angles), jnp.sin(angles) * sign[None, :]


def turn(values, cosine, sine):
    return values * cosine + pltpu.roll(values, values.shape[-1] // 2, 1) * sine


def turn_back(grads, cosine, sine):
    return grads * cosine + pltpu.roll(grads * sine, grads.shape[-1] // 2, 1)


def norm_of(values):
    inv = lax.rsqrt(jnp.mean(values * values, axis=-1, keepdims=True) + EPS)
    return values * inv, inv


def norm_back(scaled, unit, inv):
    return inv * (scaled - unit * jnp.mean(scaled * unit, axis=-1, keepdims=True))


def softmax_of(q_rot, k_rot):
    length, width = q_rot.shape
    scores = dot_nt(q_rot, k_rot) * (width**-0.5)
    at = lax.broadcasted_iota(jnp.int32, (length, length), 0)
    to = lax.broadcasted_iota(jnp.int32, (length, length), 1)
    scores = jnp.where(at >= to, scores, -1e30)
    grown = jnp.exp(scores - jnp.max(scores, axis=-1, keepdims=True))
    return grown * (1.0 / jnp.sum(grown, axis=-1, keepdims=True))


def attend_kernel(half, core_ref, tok_ref, g_ref, wq_ref, wk_ref, wv_ref, qg_ref, kg_ref, wo_ref, cos_ref, sin_ref, *outs):
    n_ref, q_ref, k_ref, v_ref, att_ref, mine_ref = outs[:6]
    width = qg_ref.shape[1]
    cosine, sine = cos_ref[...], sin_ref[...]
    unit, _ = norm_of(tok_ref[...].astype(f32))
    normed = (unit * g_ref[...]).astype(b16)
    n_ref[...] = normed
    query = dot(normed, wq_ref[...])
    keys = dot(normed, wk_ref[...])
    values = dot(normed, wv_ref[...]).astype(b16)
    q_ref[...] = query
    k_ref[...] = keys
    v_ref[...] = values
    kv_heads = keys.shape[1] // width
    share = query.shape[1] // keys.shape[1]
    for kv in range(kv_heads):
        at = slice(kv * width, (kv + 1) * width)
        k_unit, _ = norm_of(keys[:, at])
        k_rot = turn(k_unit * kg_ref[...], cosine, sine).astype(b16)
        for h in range(kv * share, (kv + 1) * share):
            to = slice(h * width, (h + 1) * width)
            q_unit, _ = norm_of(query[:, to])
            q_rot = turn(q_unit * qg_ref[...], cosine, sine).astype(b16)
            probs = softmax_of(q_rot, k_rot).astype(b16)
            att_ref[:, to] = dot(probs, values[:, at]).astype(b16)
    mixed = dot(att_ref[...], wo_ref[...])

    @pl.when(pl.program_id(0) < half)
    def _():
        for i, ref in enumerate(outs[6:]):
            ref[...] = mixed[i * ref.shape[0] : (i + 1) * ref.shape[0]]

    @pl.when(pl.program_id(0) >= half)
    def _():
        mine_ref[...] = mixed


def attend(core, tokens, g, wq, wk, wv, qg, kg, wo, cosine, sine):
    rows, width = tokens.shape
    seqs = rows // SEQ_LEN
    half = seqs // 2

    def source(i, core_ref):
        mine = core_ref[0]
        return (jnp.where(i < half, (1 - mine) * half + i, mine * half + i - half), 0)

    def place(i, _):
        return ((i + half) % seqs, 0)

    def out(columns, dtype):
        return pl.BlockSpec((SEQ_LEN, columns), place), jax.ShapeDtypeStruct((rows, columns), dtype)

    nq, nk = wq.shape[1], wk.shape[1]
    outs = [out(width, b16), out(nq, f32), out(nk, f32), out(nk, b16), out(nq, b16)]
    part = jax.ShapeDtypeStruct((rows // 2, width), f32)
    piece = SEQ_LEN // PIECES
    return pl.pallas_call(
        functools.partial(attend_kernel, half),
        grid_spec=pltpu.PrefetchScalarGridSpec(
            num_scalar_prefetch=1,
            grid=(seqs,),
            in_specs=[pl.BlockSpec((SEQ_LEN, width), source)]
            + [whole(a.shape) for a in (g, wq, wk, wv, qg, kg, wo, cosine, sine)],
            out_specs=[o[0] for o in outs]
            + [
                pl.BlockSpec((SEQ_LEN, width), lambda i, _: (jnp.maximum(i - half, 0), 0)),
            ]
            + [pl.BlockSpec((piece, width), lambda i, _: (jnp.minimum(i, half - 1), 0))] * PIECES,
        ),
        out_shape=[o[1] for o in outs]
        + [part]
        + [jax.ShapeDtypeStruct((piece * half, width), f32)] * PIECES,
        compiler_params=vmem(),
        name="attend",
    )(core, tokens, g, wq, wk, wv, qg, kg, wo, cosine, sine)


def attend_back_kernel(half, core_ref, *refs):
    dnb_refs, rb_refs, refs = refs[:PIECES], refs[PIECES : 2 * PIECES], refs[2 * PIECES :]
    ins, outs = refs[:18], refs[18:]
    dna_ref, ra_ref, cot_ref, tok_ref, q_ref, k_ref, v_ref, att_ref = ins[:8]
    gm_ref, ga_ref, qg_ref, kg_ref, wq_ref, wk_ref, wv_ref, wo_ref, cos_ref, sin_ref = ins[8:]
    dr_ref, drm_ref, dqkv_ref, d1a_ref, ga_out, gq_out, gk_out = outs[:7]
    d1b_refs, (r_ref, dn_ref) = outs[7:-2], outs[-2:]
    step = pl.program_id(0)
    width = qg_ref.shape[1]
    cosine, sine = cos_ref[...], sin_ref[...]

    @pl.when(step == 0)
    def _():
        ga_out[...] = jnp.zeros_like(ga_out)
        gq_out[...] = jnp.zeros_like(gq_out)
        gk_out[...] = jnp.zeros_like(gk_out)

    mine = step < half

    @pl.when(mine)
    def _():
        r_ref[...] = ra_ref[...]
        dn_ref[...] = dna_ref[...]

    @pl.when(step >= half)
    def _():
        for i, (r_piece, dn_piece) in enumerate(zip(rb_refs, dnb_refs)):
            at = slice(i * r_piece.shape[0], (i + 1) * r_piece.shape[0])
            r_ref[at, :] = r_piece[...]
            dn_ref[at, :] = dn_piece[...]

    unit2, inv2 = norm_of(r_ref[...])
    scaled = dn_ref[...] * gm_ref[...]
    d_resid = cot_ref[...].astype(f32) + norm_back(scaled, unit2, inv2)
    d_resid_b = d_resid.astype(b16)
    dr_ref[...] = d_resid_b

    @pl.when(mine)
    def _():
        drm_ref[...] = d_resid

    d_att = dot_nt(d_resid_b, wo_ref[...]).astype(b16)
    nq, nk = q_ref.shape[1], k_ref.shape[1]
    share = nq // nk
    for kv in range(nk // width):
        at = slice(kv * width, (kv + 1) * width)
        k_unit, k_inv = norm_of(k_ref[:, at])
        k_rot = turn(k_unit * kg_ref[...], cosine, sine).astype(b16)
        values = v_ref[:, at]
        d_krot = d_values = 0.0
        for h in range(kv * share, (kv + 1) * share):
            to = slice(h * width, (h + 1) * width)
            q_unit, q_inv = norm_of(q_ref[:, to])
            q_rot = turn(q_unit * qg_ref[...], cosine, sine).astype(b16)
            probs = softmax_of(q_rot, k_rot)
            d_head = d_att[:, to]
            d_prob = dot_nt(d_head, values)
            delta = jnp.sum(d_head.astype(f32) * att_ref[:, to].astype(f32), axis=-1, keepdims=True)
            d_score = (probs * (d_prob - delta) * (width**-0.5)).astype(b16)
            d_krot += dot_tn(d_score, q_rot)
            d_values += dot_tn(probs.astype(b16), d_head)
            d_qn = turn_back(dot(d_score, k_rot), cosine, sine)
            gq_out[...] += jnp.sum(d_qn * q_unit, axis=0, keepdims=True)
            dqkv_ref[:, to] = norm_back(d_qn * qg_ref[...], q_unit, q_inv).astype(b16)
        d_kn = turn_back(d_krot, cosine, sine)
        gk_out[...] += jnp.sum(d_kn * k_unit, axis=0, keepdims=True)
        here = slice(nq + kv * width, nq + (kv + 1) * width)
        dqkv_ref[:, here] = norm_back(d_kn * kg_ref[...], k_unit, k_inv).astype(b16)
        here = slice(nq + nk + kv * width, nq + nk + (kv + 1) * width)
        dqkv_ref[:, here] = d_values.astype(b16)
    d_norm1 = (
        dot_nt(dqkv_ref[:, :nq], wq_ref[...])
        + dot_nt(dqkv_ref[:, nq : nq + nk], wk_ref[...])
        + dot_nt(dqkv_ref[:, nq + nk :], wv_ref[...])
    )
    unit1, _ = norm_of(tok_ref[...].astype(f32))
    ga_out[...] += jnp.sum(d_norm1 * unit1, axis=0, keepdims=True)

    @pl.when(mine)
    def _():
        d1a_ref[...] = d_norm1

    @pl.when(step >= half)
    def _():
        for i, ref in enumerate(d1b_refs):
            ref[...] = d_norm1[i * ref.shape[0] : (i + 1) * ref.shape[0]]


def attend_back(core, dn_a, dn_b, r_a, r_b, cot, tokens, q, k, v, att, gm, ga, qg, kg, wq, wk, wv, wo, cosine, sine):
    rows, width = tokens.shape
    seqs = rows // SEQ_LEN
    half = seqs // 2

    def source(i, core_ref):
        mine = core_ref[0]
        return (jnp.where(i < half, mine * half + i, (1 - mine) * half + i - half), 0)

    def low(i, _):
        return (jnp.minimum(i, half - 1), 0)

    def high(i, _):
        return (jnp.maximum(i - half, 0), 0)

    def same(i, _):
        return (i, 0)

    def block(columns, place):
        return pl.BlockSpec((SEQ_LEN, columns), place)

    nq, nk = wq.shape[1], wk.shape[1]
    part = jax.ShapeDtypeStruct((rows // 2, width), f32)
    consts = (gm, ga, qg, kg, wq, wk, wv, wo, cosine, sine)
    small = [(1, width), qg.shape, kg.shape]
    piece = SEQ_LEN // PIECES
    return pl.pallas_call(
        functools.partial(attend_back_kernel, half),
        grid_spec=pltpu.PrefetchScalarGridSpec(
            num_scalar_prefetch=1,
            grid=(seqs,),
            in_specs=[
                pl.BlockSpec((piece, width), high),
            ]
            * (2 * PIECES)
            + [
                block(width, low),
                block(width, low),
                block(width, same),
                block(width, source),
                block(nq, same),
                block(nk, same),
                block(nk, same),
                block(nq, same),
            ]
            + [whole(a.shape) for a in consts],
            out_specs=[
                block(width, same),
                block(width, low),
                block(nq + 2 * nk, same),
                block(width, low),
            ]
            + [whole(s) for s in small]
            + [pl.BlockSpec((piece, width), high)] * PIECES,
            scratch_shapes=[pltpu.VMEM((SEQ_LEN, width), f32)] * 2,
        ),
        out_shape=[
            jax.ShapeDtypeStruct((rows, width), b16),
            part,
            jax.ShapeDtypeStruct((rows, nq + 2 * nk), b16),
            part,
        ]
        + [jax.ShapeDtypeStruct(s, f32) for s in small]
        + [jax.ShapeDtypeStruct((piece * half, width), f32)] * PIECES,
        compiler_params=vmem(),
        name="attend_back",
    )(core, *dn_b, *r_b, dn_a, r_a, cot, tokens, q, k, v, att, *consts)


def rows_kernel(where_ref, a_ref, b_ref, out_ref):
    out_ref[...] = dot_tn(a_ref[...], b_ref[...])


def input_grads(where, a, b, block):
    rows, columns, count = a.shape[0], b.shape[1], where.shape[0]
    return pl.pallas_call(
        rows_kernel,
        grid_spec=pltpu.PrefetchScalarGridSpec(
            num_scalar_prefetch=1,
            grid=(count,),
            in_specs=[pl.BlockSpec((rows, block), lambda j, at: (0, at[j])), whole((rows, columns))],
            out_specs=pl.BlockSpec((block, columns), lambda j, _: (j, 0)),
        ),
        out_shape=jax.ShapeDtypeStruct((count * block, columns), f32),
        compiler_params=vmem(),
        name="input_grads",
    )(where, a, b)


def output_grads(where, a, b, block):
    rows, columns, count = a.shape[0], a.shape[1], where.shape[0]
    return pl.pallas_call(
        rows_kernel,
        grid_spec=pltpu.PrefetchScalarGridSpec(
            num_scalar_prefetch=1,
            grid=(count,),
            in_specs=[whole((rows, columns)), pl.BlockSpec((rows, block), lambda j, at: (0, at[j]))],
            out_specs=pl.BlockSpec((columns, block), lambda j, _: (j, 0)),
        ),
        out_shape=jax.ShapeDtypeStruct((count * columns, block), f32),
        compiler_params=vmem(),
        name="output_grads",
    )(where, a, b)


def plain_input_grads(where, a, b, block):
    return jnp.concatenate([dot_tn(lax.dynamic_slice_in_dim(a, w * block, block, 1), b) for w in where])


def plain_output_grads(where, a, b, block):
    return jnp.concatenate([dot_tn(a, lax.dynamic_slice_in_dim(b, w * block, block, 1)) for w in where])


def tensor_masks():
    size = lax.axis_size("tensor")
    return [1 << i for i in range(1, size.bit_length() - 1)]


def scatter_sum(parts, masks):
    for mask in masks:
        half = len(parts) // 2
        received = [swap(p, "dp", mask) for p in parts[half:]]
        parts = [a + b for a, b in zip(parts[:half], received)]
    return parts[0]


def relative(masks):
    offsets = [0]
    for mask in reversed(masks):
        offsets = offsets + [o ^ mask for o in offsets]
    return offsets


def body(
    tokens,
    g_attn,
    w_query,
    w_key,
    w_value,
    q_gain,
    k_gain,
    w_out,
    g_mlp,
    w_gate,
    w_up,
    w_down,
    cotangent,
):
    rows, width = tokens.shape
    hd = q_gain.shape[0]
    cosine, sine = rope_tables(SEQ_LEN, hd)
    n_dp = lax.axis_size("dp")
    me = lax.axis_index("dp")
    core = lax.axis_index("tensor") % 2
    core_at = core.astype(jnp.int32).reshape(1)
    x_at = (lax.axis_index("tensor") // 2).astype(jnp.int32).reshape(1)
    half = rows // 2
    block = width // n_dp
    bits = [1 << i for i in range(n_dp.bit_length() - 1)]
    near, far = bits[0], bits[-1]
    middle = bits[1:-1]
    ga, gm, gq, gk = (g.reshape(1, -1) for g in (g_attn, g_mlp, q_gain, k_gain))
    seq = Sequence()

    def mine_of(a):
        return lax.dynamic_slice_in_dim(a, core * half, half, 0)

    def theirs_of(a):
        return lax.dynamic_slice_in_dim(a, (1 - core) * half, half, 0)

    def in_order(mine, theirs):
        out = jnp.zeros((rows,) + mine.shape[1:], mine.dtype)
        out = lax.dynamic_update_slice_in_dim(out, mine, core * half, 0)
        return lax.dynamic_update_slice_in_dim(out, theirs, (1 - core) * half, 0)

    def quarter_of(a):
        size = a.shape[0] // 2
        return lax.dynamic_slice_in_dim(a, (lax.axis_index("tensor") // 2) * size, size, 0)

    def one(value, count):
        return [value] if count == 1 else list(value)

    def pick(kernel, plain):
        return kernel if block % 128 == 0 else plain

    def at(offsets):
        return me ^ jnp.array(offsets, jnp.int32)

    def core_swap(a):
        return swap(a, "tensor", 1)

    def core_swaps(pieces):
        return [swap(a, "tensor", 1) for a in pieces]

    def x_swap(a):
        return swap(a, "tensor", 2)

    cot_mine, cot_theirs = mine_of(cotangent), theirs_of(cotangent)
    cot_own = jnp.concatenate([cot_mine, cot_theirs])
    c0 = cot_mine.astype(f32) * 2.0
    c0, c0_quarter, tokens_then = seq(c0, quarter_of(c0), tokens)
    c1 = swap(c0, "dp", near)
    c2 = swap(c0_quarter, "dp", far)
    tok_mine = mine_of(tokens)
    normed1, query, keys, values, attended, mixed_a, *mixed_b = seq(
        *attend(core_at, tokens_then, ga, w_query, w_key, w_value, gq, gk, w_out, cosine, sine)
    )
    mixed_got = seq(*core_swaps(mixed_b))
    (mixed_chip,) = sum_of(mixed_a, mixed_got)
    mixed_chip = seq(mixed_chip)
    mixed_x = x_swap(mixed_chip)
    c1, c2 = seq(c1, c2)
    c3 = swap(c2, "dp", near)
    c2x = x_swap(c2)
    c1t = core_swap(c1)

    mixed_x = seq(mixed_x)
    r_a, n0, n0_quarter, *r_split = seq(*resid_of(x_at, tok_mine, mixed_chip, mixed_x))
    n1 = swap(n0, "dp", near)
    n2 = swap(n0_quarter, "dp", far)
    r_b = core_swaps(r_split)
    c3, *r_b = seq(c3, *r_b)
    c3x = x_swap(c3)

    normed2, hidden, d_gate, d_up, dn_a, *dn_b, mlp_gain = seq(
        *pick(own_feed, plain_own_feed)(r_a, r_b, cot_own, gm, w_gate, w_up, w_down)
    )
    dn_got = core_swaps(dn_b)
    offsets = relative(middle)
    down_a, down_b, sums = pick(own_rest, plain_own_rest)(
        at(offsets), normed2, cot_own, hidden, d_gate, d_up, w_down, block
    )
    down_a, down_b, *sums = seq(down_a, down_b, *sums)
    n1, n2, c1t, c2x, c3x = seq(n1, n2, c1t, c2x, c3x)
    n3 = swap(n2, "dp", near)
    n2x = x_swap(n2)
    n1t = core_swap(n1)
    moved_c = core_swaps((c2, c2x, c3, c3x))
    down_got = core_swap(down_b)
    dn_got = seq(*dn_got)
    (dn_chip,) = sum_of(dn_a, dn_got)
    n1t, dn_chip = seq(n1t, dn_chip)

    def add_group(ns, cs, sums):
        group = pick(group_feed, plain_group_feed)
        return list(seq(*group(at(offsets), ns, cs, gm, w_gate, w_up, w_down, sums, block)))

    sums = add_group([n1, n1t], [c1, c1t], sums)
    n3, n2x, *moved_c = seq(n3, n2x, *moved_c)
    n3x = x_swap(n3)
    n2t, n2xt, n3t = core_swaps((n2, n2x, n3))
    n2t, n2xt = seq(n2t, n2xt)
    dn_chip = seq(dn_chip)
    dn_x = x_swap(dn_chip)
    sums = add_group([n2, n2x, n2t, n2xt], [c2, c2x, moved_c[0], moved_c[1]], sums)
    n3x, n3t, down_got = seq(n3x, n3t, down_got)
    (down_chip,) = sum_of(down_a, [down_got])
    n3xt, down_chip = seq(core_swap(n3x), down_chip)
    sums = add_group([n3, n3x, n3t, n3xt], [c3, c3x, moved_c[2], moved_c[3]], sums)
    k = len(offsets)
    h = k // 2

    def first_step(parts):
        return [swap(p, "dp", middle[0]) for p in parts[h:]]

    got_down, got_gu = first_step(sums[:k]), first_step(sums[k:])
    keep_down, keep_gu = sums[:h], sums[k : k + h]

    dn_x = seq(dn_x)
    dn_mine, *dn_split = seq(*sum_of(dn_chip, [dn_x], split=True))
    down_x = x_swap(down_chip)
    dn_theirs = seq(*core_swaps(dn_split))
    dr_b, dr_mine, d_qkv, d1_a, gain_a, gain_q, gain_k, *d1_b = seq(
        *attend_back(
            core_at, dn_mine, dn_theirs, r_a, r_b, cot_own, tokens, query, keys, values, attended,
            gm, ga, gq, gk, w_query, w_key, w_value, w_out, cosine, sine,
        )
    )
    gains = jnp.concatenate([gain_a[0], gain_q[0], gain_k[0], mlp_gain[0]])
    gains_got = swap(gains, "dp", near)
    d1_got = core_swaps(d1_b)

    every = [near] + middle + [far]
    rest = every[1:]
    blocks = relative(every)
    q = len(blocks) // 4
    of_in, of_out = pick(input_grads, plain_input_grads), pick(output_grads, plain_output_grads)

    def ins(i, count=1):
        return of_in(at(blocks[i * q : (i + count) * q]), normed1, d_qkv, block)

    def outs(i, count=1):
        return of_out(at(blocks[i * q : (i + count) * q]), attended, dr_b, block)

    in_3 = seq(ins(3))
    in_got3 = swap(in_3, "dp", near)
    out_23 = seq(outs(2, 2))
    out_got = swap(out_23, "dp", near)
    *d1_got, gains_got = seq(*d1_got, gains_got)
    (d1_chip,) = sum_of(d1_a, d1_got)
    d1_chip = seq(d1_chip)
    d1_x = x_swap(d1_chip)
    gains = gains + gains_got
    in_2 = seq(ins(2))
    in_got2 = swap(in_2, "dp", near)
    out_01, in_1, in_0 = seq(outs(0, 2), ins(1), ins(0))
    got_down = one(seq(*got_down), h)

    def finish(keep, got):
        return scatter_sum([a + b for a, b in zip(keep, got)], middle[1:])

    summed_down = finish(keep_down, got_down)
    down_x = seq(down_x)
    down_mine, *down_split = seq(*sum_of(down_chip, [down_x], split=True))
    down_theirs = core_swaps(down_split)
    in_got3, *down_theirs = seq(in_got3, *down_theirs)
    (in_1,) = sum_of(in_1, [in_got3])
    in_mid = swap(in_1, "dp", rest[0])
    down_theirs = jnp.concatenate(down_theirs)
    r_theirs = jnp.concatenate(r_b)
    output = in_order((r_a + down_mine).astype(b16), (r_theirs + down_theirs).astype(b16))
    d1_x = seq(d1_x)
    d1_mine = d1_chip + d1_x
    _, unit1, rms1 = rms_norm(tok_mine.astype(f32), ga)
    gt_mine = seq(dr_mine + rms_back(d1_mine, ga, unit1, rms1))
    gt_theirs = core_swap(gt_mine)
    got_gu = one(seq(*got_gu), h)
    summed_gu = finish(keep_gu, got_gu)
    out_got, gt_theirs = seq(out_got, gt_theirs)
    (out_01,) = sum_of(out_01, [out_got])
    at_half = out_01.shape[0] // 2
    out_mid = swap(out_01[at_half:], "dp", rest[0])
    grad_tokens = in_order(gt_mine, gt_theirs)
    gains = seq(gains + x_swap(gains))
    gains = seq(gains + core_swap(gains))
    for mask in bits[1:]:
        gains = seq(gains + swap(gains, "dp", mask))
    in_got2 = seq(in_got2)

    def split(a):
        return list(a.reshape(q, a.shape[0] // q, a.shape[1]))

    in_mid = seq(in_mid)
    summed_qkv = scatter_sum(split(in_0 + in_got2 + in_mid), rest[1:])
    out_mid = seq(out_mid)
    summed_out = scatter_sum(split(out_01[:at_half] + out_mid), rest[1:])
    summed_qkv, summed_out = seq(summed_qkv, summed_out)
    nq, nk = w_query.shape[1], w_key.shape[1]
    gains = gains + 0.0 * seq.token.astype(f32)
    return (
        output,
        grad_tokens,
        gains[:width],
        summed_qkv[:, :nq],
        summed_qkv[:, nq : nq + nk],
        summed_qkv[:, nq + nk :],
        gains[width : width + hd],
        gains[width + hd : width + 2 * hd],
        summed_out,
        gains[width + 2 * hd :],
        summed_gu[:block],
        summed_gu[block:],
        summed_down,
    )


def solution(mesh):
    in_specs = (
        P("dp", None),
        P(),
        P(None, "tensor"),
        P(None, "tensor"),
        P(None, "tensor"),
        P(),
        P(),
        P("tensor", None),
        P(),
        P(None, "tensor"),
        P(None, "tensor"),
        P("tensor", None),
        P("dp", None),
    )
    out_specs = (
        P("dp", None),
        P("dp", None),
        P(),
        P("dp", "tensor"),
        P("dp", "tensor"),
        P("dp", "tensor"),
        P(),
        P(),
        P("tensor", "dp"),
        P(),
        P("dp", "tensor"),
        P("dp", "tensor"),
        P("tensor", "dp"),
    )
    return jax.shard_map(body, mesh=mesh, in_specs=in_specs, out_specs=out_specs, check_vma=False)
```

```python
import functools

import jax
import jax.numpy as jnp
from jax import lax
from jax.experimental import pallas as pl
from jax.experimental.pallas import tpu as pltpu
from jax.sharding import PartitionSpec as P

SEQ_LEN = 256


EPS = 1e-06
THETA = 1000000.0

f32 = jnp.float32
b16 = jnp.bfloat16


def rms_norm(values, gain):
    inv_rms = lax.rsqrt(jnp.mean(values * values, axis=-1, keepdims=True) + EPS)
    unit_rows = values * inv_rms
    return (unit_rows * gain, unit_rows, inv_rms)


def rms_back(grads, gain, unit_rows, inv_rms):
    scaled = grads * gain
    return inv_rms * (scaled - unit_rows * jnp.mean(scaled * unit_rows, axis=-1, keepdims=True))


def swap(value, axis, mask):
    size = lax.axis_size(axis)
    return lax.ppermute(value, axis, [(i, i ^ mask) for i in range(size)])


class Sequence:
    def __init__(self):
        self.token = None

    def __call__(self, *values):
        if self.token is None:
            out = lax.optimization_barrier(values)
        else:
            *out, self.token = lax.optimization_barrier((*values, self.token))
        self.token = out[0].reshape(-1)[:1] if self.token is None else self.token
        return out[0] if len(out) == 1 else tuple(out)


def dot(a, b):
    return jnp.dot(a, b, preferred_element_type=f32)


def dot_nt(a, b):
    return lax.dot_general(a, b, (((1,), (1,)), ((), ())), preferred_element_type=f32)


def dot_tn(a, b):
    return lax.dot_general(a, b, (((0,), (0,)), ((), ())), preferred_element_type=f32)


TILE = 512
PIECES = 4


def vmem(mib=60):
    return pltpu.CompilerParams(vmem_limit_bytes=mib << 20)


def whole(shape):
    return pl.BlockSpec(shape, lambda *_: (0,) * len(shape))


def gated(nb, cb, wg_ref, wu_ref, wd_ref):
    gate_pre = dot(nb[...], wg_ref[...])
    up_pre = dot(nb[...], wu_ref[...])
    d_hidden = dot_nt(cb[...], wd_ref[...])
    sig = jax.nn.sigmoid(gate_pre)
    act = gate_pre * sig
    hidden = (act * up_pre).astype(b16)
    d_up = (d_hidden * act).astype(b16)
    d_gate = (d_hidden * up_pre * (sig * (1.0 + gate_pre * (1.0 - sig)))).astype(b16)
    return hidden, d_gate, d_up


def own_kernel(ra_ref, *refs):
    rb_refs, refs = refs[:PIECES], refs[PIECES:]
    cot_ref, g_ref, wg_ref, wu_ref, wd_ref, normed_ref, hid_ref, dg_ref, du_ref, dna_ref = refs[:10]
    dnb_refs, (gain_ref, rms_ref) = refs[10:-2], refs[-2:]
    step = pl.program_id(0)
    half = ra_ref.shape[0]
    part = half // PIECES

    @pl.when(step == 0)
    def _():
        for i, ref in enumerate((ra_ref, *rb_refs)):
            r = ref[...]
            at = 0 if i == 0 else half + (i - 1) * part
            inv = lax.rsqrt(jnp.mean(r * r, axis=-1, keepdims=True) + EPS)
            rms_ref[at : at + r.shape[0], :] = inv
            normed_ref[at : at + r.shape[0], :] = (r * inv * g_ref[...]).astype(b16)
        dna_ref[...] = jnp.zeros_like(dna_ref)
        for ref in dnb_refs:
            ref[...] = jnp.zeros_like(ref)

    hidden, d_gate, d_up = gated(normed_ref, cot_ref, wg_ref, wu_ref, wd_ref)
    hid_ref[...] = hidden
    dg_ref[...] = d_gate
    du_ref[...] = d_up
    dna_ref[...] += dot_nt(d_gate[:half], wg_ref[...]) + dot_nt(d_up[:half], wu_ref[...])
    far = dot_nt(d_gate[half:], wg_ref[...]) + dot_nt(d_up[half:], wu_ref[...])
    for i, ref in enumerate(dnb_refs):
        ref[...] += far[i * part : (i + 1) * part]

    @pl.when(step == pl.num_programs(0) - 1)
    def _():
        total = jnp.sum(dna_ref[...] * (ra_ref[...] * rms_ref[:half, :]), axis=0, keepdims=True)
        for i, (r_ref, d_ref) in enumerate(zip(rb_refs, dnb_refs)):
            at = half + i * part
            unit = r_ref[...] * rms_ref[at : at + part, :]
            total += jnp.sum(d_ref[...] * unit, axis=0, keepdims=True)
        gain_ref[...] = total


def own_feed(r_a, r_b, cot, g, w_gate, w_up, w_down):
    half, width = r_a.shape
    rows, hidden = 2 * half, w_gate.shape[1]
    col = pl.BlockSpec((rows, TILE), lambda i: (0, i))
    wide = jax.ShapeDtypeStruct((rows, hidden), b16)
    piece = (half // PIECES, width)
    return pl.pallas_call(
        own_kernel,
        grid=(hidden // TILE,),
        in_specs=[whole((half, width))]
        + [whole(piece)] * PIECES
        + [
            whole((rows, width)),
            whole((1, width)),
            pl.BlockSpec((width, TILE), lambda i: (0, i)),
            pl.BlockSpec((width, TILE), lambda i: (0, i)),
            pl.BlockSpec((TILE, width), lambda i: (i, 0)),
        ],
        out_specs=[
            whole((rows, width)),
            col,
            col,
            col,
            whole((half, width)),
        ]
        + [whole(piece)] * PIECES
        + [whole((1, width))],
        out_shape=[
            jax.ShapeDtypeStruct((rows, width), b16),
            wide,
            wide,
            wide,
            jax.ShapeDtypeStruct((half, width), f32),
        ]
        + [jax.ShapeDtypeStruct(piece, f32)] * PIECES
        + [jax.ShapeDtypeStruct((1, width), f32)],
        scratch_shapes=[pltpu.VMEM((rows, 1), f32)],
        compiler_params=vmem(),
        name="own_feed",
    )(r_a, *r_b, cot, g.reshape(1, -1), w_gate, w_up, w_down)


def put_columns(at_ref, cc_ref, nb_ref, cb_ref, where_ref, count, block):
    for j in range(count):
        here = pl.ds(pl.multiple_of(where_ref[j] * block, 128), block)
        at_ref[j * block : (j + 1) * block, :] = nb_ref[:, here].T
        cc_ref[:, j * block : (j + 1) * block] = cb_ref[:, here]


def put_grads(sums, at_ref, cc_ref, hidden, d_gate, d_up, block, before=None):
    down = dot_tn(hidden, cc_ref[...])
    gate = dot(at_ref[...], d_gate)
    up = dot(at_ref[...], d_up)
    count = len(sums) // 3
    for j in range(count):
        part = slice(j * block, (j + 1) * block)
        for k, fresh in ((j, down[:, part]), (count + j, gate[part]), (2 * count + j, up[part])):
            old = 0.0 if before is None else before[k][...]
            sums[k][...] = fresh + old


def rest_kernel(where_ref, nb_ref, cb_ref, hid_ref, dg_ref, du_ref, wd_ref, *rest):
    count = (len(rest) - 4) // 3
    ya_ref, yb_ref, *sums = rest[:-2]
    at_ref, cc_ref = rest[-2:]
    half = ya_ref.shape[0]
    block = cc_ref.shape[1] // count

    @pl.when(pl.program_id(0) == 0)
    def _():
        put_columns(at_ref, cc_ref, nb_ref, cb_ref, where_ref, count, block)
        ya_ref[...] = jnp.zeros_like(ya_ref)
        yb_ref[...] = jnp.zeros_like(yb_ref)

    hidden = hid_ref[...]
    ya_ref[...] += dot(hidden[:half], wd_ref[...])
    yb_ref[...] += dot(hidden[half:], wd_ref[...])
    put_grads(sums, at_ref, cc_ref, hidden, dg_ref[...], du_ref[...], block)


def sum_specs(count, block, hidden):
    specs = [pl.BlockSpec((TILE, block), lambda i, *_: (i, 0))] * count
    specs += [pl.BlockSpec((block, TILE), lambda i, *_: (0, i))] * (2 * count)
    shapes = [jax.ShapeDtypeStruct((hidden, block), f32)] * count
    shapes += [jax.ShapeDtypeStruct((block, hidden), f32)] * (2 * count)
    return specs, shapes


def own_rest(where, nb, cb, hidden, d_gate, d_up, w_down, block):
    rows, width = nb.shape
    count = where.shape[0]
    half, ff = rows // 2, hidden.shape[1]
    specs, shapes = sum_specs(count, block, ff)
    col = pl.BlockSpec((rows, TILE), lambda i, *_: (0, i))
    part = jax.ShapeDtypeStruct((half, width), f32)
    out = pl.pallas_call(
        rest_kernel,
        grid_spec=pltpu.PrefetchScalarGridSpec(
            num_scalar_prefetch=1,
            grid=(ff // TILE,),
            in_specs=[
                whole((rows, width)),
                whole((rows, width)),
                col,
                col,
                col,
                pl.BlockSpec((TILE, width), lambda i, *_: (i, 0)),
            ],
            out_specs=[whole((half, width)), whole((half, width))] + specs,
            scratch_shapes=[
                pltpu.VMEM((count * block, rows), b16),
                pltpu.VMEM((rows, count * block), b16),
            ],
        ),
        out_shape=[part, part] + shapes,
        compiler_params=vmem(),
        name="own_rest",
    )(where, nb, cb, hidden, d_gate, d_up, w_down)
    return out[0], out[1], list(out[2:])


def group_kernel(n_pieces, c_pieces, count, where_ref, *refs):
    n_refs, refs = refs[:n_pieces], refs[n_pieces:]
    c_refs, refs = refs[:c_pieces], refs[c_pieces:]
    g_ref, wg_ref, wu_ref, wd_ref = refs[:4]
    before = refs[4 : 4 + 3 * count]
    sums = refs[4 + 3 * count : 4 + 6 * count]
    nb_ref, cb_ref, at_ref, cc_ref = refs[4 + 6 * count :]
    block = cc_ref.shape[1] // count

    @pl.when(pl.program_id(0) == 0)
    def _():
        at = 0
        for n_ref in n_refs:
            size = n_ref.shape[0]
            nb_ref[at : at + size, :] = (n_ref[...] * g_ref[...]).astype(b16)
            at += size
        at = 0
        for c_ref in c_refs:
            size = c_ref.shape[0]
            cb_ref[at : at + size, :] = (c_ref[...] * 0.5).astype(b16)
            at += size
        put_columns(at_ref, cc_ref, nb_ref, cb_ref, where_ref, count, block)

    hidden, d_gate, d_up = gated(nb_ref, cb_ref, wg_ref, wu_ref, wd_ref)
    put_grads(sums, at_ref, cc_ref, hidden, d_gate, d_up, block, before)


def group_feed(where, ns, cs, g, w_gate, w_up, w_down, before, block):
    width, ff = w_gate.shape
    count = where.shape[0]
    rows = sum(n.shape[0] for n in ns)
    specs, shapes = sum_specs(count, block, ff)
    return list(
        pl.pallas_call(
            functools.partial(group_kernel, len(ns), len(cs), count),
            grid_spec=pltpu.PrefetchScalarGridSpec(
                num_scalar_prefetch=1,
                grid=(ff // TILE,),
                in_specs=[whole(a.shape) for a in (*ns, *cs)]
                + [
                    whole((1, width)),
                    pl.BlockSpec((width, TILE), lambda i, *_: (0, i)),
                    pl.BlockSpec((width, TILE), lambda i, *_: (0, i)),
                    pl.BlockSpec((TILE, width), lambda i, *_: (i, 0)),
                ]
                + specs,
                out_specs=specs,
                scratch_shapes=[
                    pltpu.VMEM((rows, width), b16),
                    pltpu.VMEM((rows, width), b16),
                    pltpu.VMEM((count * block, rows), b16),
                    pltpu.VMEM((rows, count * block), b16),
                ],
            ),
            out_shape=shapes,
            compiler_params=vmem(),
            name="group_feed",
        )(where, *ns, *cs, g.reshape(1, -1), w_gate, w_up, w_down, *before)
    )


def sum_kernel(count, *refs):
    a_ref, b_refs, outs = refs[0], refs[1 : 1 + count], refs[1 + count :]
    size = a_ref.shape[0] // count
    for i, b_ref in enumerate(b_refs):
        at = slice(i * size, (i + 1) * size)
        total = a_ref[at, :] + b_ref[...]
        outs[0][at, :] = total
    pieces = outs[1:]
    for i, piece in enumerate(pieces):
        piece[...] = outs[0][i * piece.shape[0] : (i + 1) * piece.shape[0], :]


def sum_of(a, bs, split=0):
    shapes = [jax.ShapeDtypeStruct(a.shape, f32)]
    shapes += [jax.ShapeDtypeStruct((a.shape[0] // max(split, 1), a.shape[1]), f32)] * split
    return pl.pallas_call(
        functools.partial(sum_kernel, len(bs)),
        in_specs=[whole(x.shape) for x in (a, *bs)],
        out_specs=[whole(x.shape) for x in shapes],
        out_shape=shapes,
        grid=(1,),
        compiler_params=vmem(),
        name="sum_of",
    )(a, *bs)


def resid_kernel(x_at_ref, tok_ref, a_ref, b_ref, c_ref, r_ref, n_ref, quarter_ref, *pieces):
    size = pieces[0].shape[0]
    for i, piece in enumerate(pieces):
        at = slice(i * size, (i + 1) * size)
        part, first = (b_ref, 0) if i < len(pieces) // 2 else (c_ref, len(pieces) // 2)
        far = part[(i - first) * size : (i - first + 1) * size, :]
        resid = tok_ref[at, :].astype(f32) + (a_ref[at, :] + far)
        r_ref[at, :] = resid
        piece[...] = resid
        n_ref[at, :] = resid * lax.rsqrt(jnp.mean(resid * resid, axis=-1, keepdims=True) + EPS)
    small = quarter_ref.shape[0]
    quarter_ref[...] = n_ref[pl.ds(pl.multiple_of(x_at_ref[0] * small, small), small), :]


def resid_of(x_at, tok, a, b, c):
    rows, width = a.shape
    shapes = [(rows, width), (rows, width), (rows // 2, width)] + [(rows // PIECES, width)] * PIECES
    return pl.pallas_call(
        resid_kernel,
        grid_spec=pltpu.PrefetchScalarGridSpec(
            num_scalar_prefetch=1,
            grid=(1,),
            in_specs=[whole(a.shape)] * 2 + [whole(b.shape)] * 2,
            out_specs=[whole(s) for s in shapes],
        ),
        out_shape=[jax.ShapeDtypeStruct(s, f32) for s in shapes],
        compiler_params=vmem(),
        name="resid_of",
    )(x_at, tok, a, b, c)


def feed(normed, cot, w_gate, w_up, w_down):
    gate_pre = dot(normed, w_gate)
    up_pre = dot(normed, w_up)
    d_hidden = dot_nt(cot, w_down)
    sigmoid_g = jax.nn.sigmoid(gate_pre)
    act_gate = gate_pre * sigmoid_g
    hidden = (act_gate * up_pre).astype(b16)
    d_up = (d_hidden * act_gate).astype(b16)
    d_gate = (d_hidden * up_pre * (sigmoid_g * (1.0 + gate_pre * (1.0 - sigmoid_g)))).astype(b16)
    return hidden, d_gate, d_up


def plain_grads(where, normed, cot, parts, block):
    hidden, d_gate, d_up = parts
    takes = [functools.partial(lax.dynamic_slice_in_dim, start_index=w * block, slice_size=block, axis=1) for w in where]
    pair = jnp.concatenate([d_gate, d_up], axis=1)
    both = [dot_tn(take(normed), pair) for take in takes]
    ff = hidden.shape[1]
    return [dot_tn(hidden, take(cot)) for take in takes] + [b[:, :ff] for b in both] + [b[:, ff:] for b in both]


def plain_own_feed(r_a, r_b, cot, g, w_gate, w_up, w_down):
    resid = jnp.concatenate([r_a, *r_b])
    normed, unit, _ = rms_norm(resid, g)
    normed = normed.astype(b16)
    parts = feed(normed, cot, w_gate, w_up, w_down)
    total = dot_nt(parts[1], w_gate) + dot_nt(parts[2], w_up)
    half = r_a.shape[0]
    gain = jnp.sum(total * unit, axis=0, keepdims=True)
    return (normed, *parts, total[:half], *jnp.split(total[half:], PIECES), gain)


def plain_own_rest(where, nb, cb, hidden, d_gate, d_up, w_down, block):
    down = dot(hidden, w_down)
    half = nb.shape[0] // 2
    return down[:half], down[half:], plain_grads(where, nb, cb, (hidden, d_gate, d_up), block)


def plain_group_feed(where, ns, cs, g, w_gate, w_up, w_down, before, block):
    normed = (jnp.concatenate(ns) * g).astype(b16)
    cot = (jnp.concatenate(cs) * 0.5).astype(b16)
    parts = feed(normed, cot, w_gate, w_up, w_down)
    return [old + new for old, new in zip(before, plain_grads(where, normed, cot, parts, block))]


def rope_tables(length, width):
    half = width // 2
    inverse = THETA ** (-(jnp.arange(half).astype(f32) * 2.0 / width))
    angles = jnp.arange(length).astype(f32)[:, None] * inverse[None, :]
    angles = jnp.concatenate([angles, angles], axis=1)
    sign = jnp.where(jnp.arange(width) < half, -1.0, 1.0).astype(f32)
    return jnp.cos(angles), jnp.sin(angles) * sign[None, :]


def turn(values, cosine, sine):
    return values * cosine + pltpu.roll(values, values.shape[-1] // 2, 1) * sine


def turn_back(grads, cosine, sine):
    return grads * cosine + pltpu.roll(grads * sine, grads.shape[-1] // 2, 1)


def norm_of(values):
    inv = lax.rsqrt(jnp.mean(values * values, axis=-1, keepdims=True) + EPS)
    return values * inv, inv


def norm_back(scaled, unit, inv):
    return inv * (scaled - unit * jnp.mean(scaled * unit, axis=-1, keepdims=True))


def softmax_of(q_rot, k_rot):
    length, width = q_rot.shape
    scores = dot_nt(q_rot, k_rot) * (width**-0.5)
    at = lax.broadcasted_iota(jnp.int32, (length, length), 0)
    to = lax.broadcasted_iota(jnp.int32, (length, length), 1)
    scores = jnp.where(at >= to, scores, -1e30)
    grown = jnp.exp(scores - jnp.max(scores, axis=-1, keepdims=True))
    return grown * (1.0 / jnp.sum(grown, axis=-1, keepdims=True))


def attend_kernel(half, core_ref, tok_ref, g_ref, wq_ref, wk_ref, wv_ref, qg_ref, kg_ref, wo_ref, cos_ref, sin_ref, *outs):
    n_ref, q_ref, k_ref, v_ref, att_ref, wide_ref, mine_ref = outs[:7]
    width = qg_ref.shape[1]
    cosine, sine = cos_ref[...], sin_ref[...]
    unit, _ = norm_of(tok_ref[...].astype(f32))
    normed = (unit * g_ref[...]).astype(b16)
    n_ref[...] = normed
    query = dot(normed, wq_ref[...])
    keys = dot(normed, wk_ref[...])
    values = dot(normed, wv_ref[...]).astype(b16)
    q_ref[...] = query
    k_ref[...] = keys
    v_ref[...] = values
    kv_heads = keys.shape[1] // width
    share = query.shape[1] // keys.shape[1]
    for kv in range(kv_heads):
        at = slice(kv * width, (kv + 1) * width)
        k_unit, _ = norm_of(keys[:, at])
        k_rot = turn(k_unit * kg_ref[...], cosine, sine).astype(b16)
        for h in range(kv * share, (kv + 1) * share):
            to = slice(h * width, (h + 1) * width)
            q_unit, _ = norm_of(query[:, to])
            q_rot = turn(q_unit * qg_ref[...], cosine, sine).astype(b16)
            probs = softmax_of(q_rot, k_rot).astype(b16)
            att_ref[:, to] = dot(probs, values[:, at]).astype(b16)
    wide_ref[...] = att_ref[...].astype(f32) * 2.0
    mixed = dot(att_ref[...], wo_ref[...])

    @pl.when(pl.program_id(0) < half)
    def _():
        for i, ref in enumerate(outs[7:]):
            ref[...] = mixed[i * ref.shape[0] : (i + 1) * ref.shape[0]]

    @pl.when(pl.program_id(0) >= half)
    def _():
        mine_ref[...] = mixed


def attend(core, tokens, g, wq, wk, wv, qg, kg, wo, cosine, sine):
    rows, width = tokens.shape
    seqs = rows // SEQ_LEN
    half = seqs // 2

    def source(i, core_ref):
        mine = core_ref[0]
        return (jnp.where(i < half, (1 - mine) * half + i, mine * half + i - half), 0)

    def place(i, _):
        return ((i + half) % seqs, 0)

    def out(columns, dtype):
        return pl.BlockSpec((SEQ_LEN, columns), place), jax.ShapeDtypeStruct((rows, columns), dtype)

    nq, nk = wq.shape[1], wk.shape[1]
    outs = [out(width, b16), out(nq, f32), out(nk, f32), out(nk, b16), out(nq, b16), out(nq, f32)]
    part = jax.ShapeDtypeStruct((rows // 2, width), f32)
    piece = SEQ_LEN // PIECES
    return pl.pallas_call(
        functools.partial(attend_kernel, half),
        grid_spec=pltpu.PrefetchScalarGridSpec(
            num_scalar_prefetch=1,
            grid=(seqs,),
            in_specs=[pl.BlockSpec((SEQ_LEN, width), source)]
            + [whole(a.shape) for a in (g, wq, wk, wv, qg, kg, wo, cosine, sine)],
            out_specs=[o[0] for o in outs]
            + [
                pl.BlockSpec((SEQ_LEN, width), lambda i, _: (jnp.maximum(i - half, 0), 0)),
            ]
            + [pl.BlockSpec((piece, width), lambda i, _: (jnp.minimum(i, half - 1), 0))] * PIECES,
        ),
        out_shape=[o[1] for o in outs]
        + [part]
        + [jax.ShapeDtypeStruct((piece * half, width), f32)] * PIECES,
        compiler_params=vmem(),
        name="attend",
    )(core, tokens, g, wq, wk, wv, qg, kg, wo, cosine, sine)


def attend_back_kernel(half, core_ref, *refs):
    dnb_refs, rb_refs, refs = refs[:PIECES], refs[PIECES : 2 * PIECES], refs[2 * PIECES :]
    ins, outs = refs[:18], refs[18:]
    dna_ref, ra_ref, cot_ref, tok_ref, q_ref, k_ref, v_ref, att_ref = ins[:8]
    gm_ref, ga_ref, qg_ref, kg_ref, wq_ref, wk_ref, wv_ref, wo_ref, cos_ref, sin_ref = ins[8:]
    dr_ref, drm_ref, dqkv_ref, wide_ref, d1a_ref, ga_out, gq_out, gk_out = outs[:8]
    d1b_refs, (r_ref, dn_ref) = outs[8:-2], outs[-2:]
    step = pl.program_id(0)
    width = qg_ref.shape[1]
    cosine, sine = cos_ref[...], sin_ref[...]

    @pl.when(step == 0)
    def _():
        ga_out[...] = jnp.zeros_like(ga_out)
        gq_out[...] = jnp.zeros_like(gq_out)
        gk_out[...] = jnp.zeros_like(gk_out)

    mine = step < half

    @pl.when(mine)
    def _():
        r_ref[...] = ra_ref[...]
        dn_ref[...] = dna_ref[...]

    @pl.when(step >= half)
    def _():
        for i, (r_piece, dn_piece) in enumerate(zip(rb_refs, dnb_refs)):
            at = slice(i * r_piece.shape[0], (i + 1) * r_piece.shape[0])
            r_ref[at, :] = r_piece[...]
            dn_ref[at, :] = dn_piece[...]

    unit2, inv2 = norm_of(r_ref[...])
    scaled = dn_ref[...] * gm_ref[...]
    d_resid = cot_ref[...].astype(f32) + norm_back(scaled, unit2, inv2)
    d_resid_b = d_resid.astype(b16)
    dr_ref[...] = d_resid_b

    @pl.when(mine)
    def _():
        drm_ref[...] = d_resid

    d_att = dot_nt(d_resid_b, wo_ref[...]).astype(b16)
    nq, nk = q_ref.shape[1], k_ref.shape[1]
    share = nq // nk
    for kv in range(nk // width):
        at = slice(kv * width, (kv + 1) * width)
        k_unit, k_inv = norm_of(k_ref[:, at])
        k_rot = turn(k_unit * kg_ref[...], cosine, sine).astype(b16)
        values = v_ref[:, at]
        d_krot = d_values = 0.0
        for h in range(kv * share, (kv + 1) * share):
            to = slice(h * width, (h + 1) * width)
            q_unit, q_inv = norm_of(q_ref[:, to])
            q_rot = turn(q_unit * qg_ref[...], cosine, sine).astype(b16)
            probs = softmax_of(q_rot, k_rot)
            d_head = d_att[:, to]
            d_prob = dot_nt(d_head, values)
            delta = jnp.sum(d_head.astype(f32) * att_ref[:, to].astype(f32), axis=-1, keepdims=True)
            d_score = (probs * (d_prob - delta) * (width**-0.5)).astype(b16)
            d_krot += dot_tn(d_score, q_rot)
            d_values += dot_tn(probs.astype(b16), d_head)
            d_qn = turn_back(dot(d_score, k_rot), cosine, sine)
            gq_out[...] += jnp.sum(d_qn * q_unit, axis=0, keepdims=True)
            dqkv_ref[:, to] = norm_back(d_qn * qg_ref[...], q_unit, q_inv).astype(b16)
        d_kn = turn_back(d_krot, cosine, sine)
        gk_out[...] += jnp.sum(d_kn * k_unit, axis=0, keepdims=True)
        here = slice(nq + kv * width, nq + (kv + 1) * width)
        dqkv_ref[:, here] = norm_back(d_kn * kg_ref[...], k_unit, k_inv).astype(b16)
        here = slice(nq + nk + kv * width, nq + nk + (kv + 1) * width)
        dqkv_ref[:, here] = d_values.astype(b16)
    wide_ref[...] = dqkv_ref[...].astype(f32) * 2.0
    d_norm1 = (
        dot_nt(dqkv_ref[:, :nq], wq_ref[...])
        + dot_nt(dqkv_ref[:, nq : nq + nk], wk_ref[...])
        + dot_nt(dqkv_ref[:, nq + nk :], wv_ref[...])
    )
    unit1, _ = norm_of(tok_ref[...].astype(f32))
    ga_out[...] += jnp.sum(d_norm1 * unit1, axis=0, keepdims=True)

    @pl.when(mine)
    def _():
        d1a_ref[...] = d_norm1

    @pl.when(step >= half)
    def _():
        for i, ref in enumerate(d1b_refs):
            ref[...] = d_norm1[i * ref.shape[0] : (i + 1) * ref.shape[0]]


def attend_back(core, dn_a, dn_b, r_a, r_b, cot, tokens, q, k, v, att, gm, ga, qg, kg, wq, wk, wv, wo, cosine, sine):
    rows, width = tokens.shape
    seqs = rows // SEQ_LEN
    half = seqs // 2

    def source(i, core_ref):
        mine = core_ref[0]
        return (jnp.where(i < half, mine * half + i, (1 - mine) * half + i - half), 0)

    def low(i, _):
        return (jnp.minimum(i, half - 1), 0)

    def high(i, _):
        return (jnp.maximum(i - half, 0), 0)

    def same(i, _):
        return (i, 0)

    def block(columns, place):
        return pl.BlockSpec((SEQ_LEN, columns), place)

    nq, nk = wq.shape[1], wk.shape[1]
    part = jax.ShapeDtypeStruct((rows // 2, width), f32)
    consts = (gm, ga, qg, kg, wq, wk, wv, wo, cosine, sine)
    small = [(1, width), qg.shape, kg.shape]
    piece = SEQ_LEN // PIECES
    return pl.pallas_call(
        functools.partial(attend_back_kernel, half),
        grid_spec=pltpu.PrefetchScalarGridSpec(
            num_scalar_prefetch=1,
            grid=(seqs,),
            in_specs=[
                pl.BlockSpec((piece, width), high),
            ]
            * (2 * PIECES)
            + [
                block(width, low),
                block(width, low),
                block(width, same),
                block(width, source),
                block(nq, same),
                block(nk, same),
                block(nk, same),
                block(nq, same),
            ]
            + [whole(a.shape) for a in consts],
            out_specs=[
                block(width, same),
                block(width, low),
                block(nq + 2 * nk, same),
                block(nq + 2 * nk, same),
                block(width, low),
            ]
            + [whole(s) for s in small]
            + [pl.BlockSpec((piece, width), high)] * PIECES,
            scratch_shapes=[pltpu.VMEM((SEQ_LEN, width), f32)] * 2,
        ),
        out_shape=[
            jax.ShapeDtypeStruct((rows, width), b16),
            part,
            jax.ShapeDtypeStruct((rows, nq + 2 * nk), b16),
            jax.ShapeDtypeStruct((rows, nq + 2 * nk), f32),
            part,
        ]
        + [jax.ShapeDtypeStruct(s, f32) for s in small]
        + [jax.ShapeDtypeStruct((piece * half, width), f32)] * PIECES,
        compiler_params=vmem(),
        name="attend_back",
    )(core, *dn_b, *r_b, dn_a, r_a, cot, tokens, q, k, v, att, *consts)


def back_kernel(dr_ref, a_ref, b_ref, tok_ref, g_ref, out_ref, *pieces):
    size = pieces[0].shape[0]
    for i, piece in enumerate(pieces):
        at = slice(i * size, (i + 1) * size)
        unit, inv = norm_of(tok_ref[at, :].astype(f32))
        grads = dr_ref[at, :] + norm_back((a_ref[at, :] + b_ref[at, :]) * g_ref[...], unit, inv)
        out_ref[at, :] = grads
        piece[...] = grads


def back_of(dr, a, b, tok, g):
    rows, width = a.shape
    shapes = [(rows, width)] + [(rows // PIECES, width)] * PIECES
    return pl.pallas_call(
        back_kernel,
        grid=(1,),
        in_specs=[whole(x.shape) for x in (dr, a, b, tok, g)],
        out_specs=[whole(x) for x in shapes],
        out_shape=[jax.ShapeDtypeStruct(x, f32) for x in shapes],
        compiler_params=vmem(),
        name="back_of",
    )(dr, a, b, tok, g)


def few_kernel(normed, where_ref, a_ref, g_ref, out_ref, row_ref):
    block = out_ref.shape[1] // where_ref.shape[0]
    here = a_ref[...].astype(f32)
    if normed:
        here = (norm_of(here)[0] * g_ref[...]).astype(b16).astype(f32)
    row_ref[...] = here
    for j in range(where_ref.shape[0]):
        at = pl.ds(pl.multiple_of(where_ref[j] * block, 128), block)
        out_ref[:, j * block : (j + 1) * block] = row_ref[:, at]


def few_of(where, a, g, block, normed):
    half, width = a.shape[0] if normed else a.shape[0] // 2, a.shape[1]
    out = (half, where.shape[0] * block)
    return pl.pallas_call(
        functools.partial(few_kernel, normed),
        grid_spec=pltpu.PrefetchScalarGridSpec(
            num_scalar_prefetch=1,
            grid=(1,),
            in_specs=[whole((half, width)), whole(g.shape)],
            out_specs=whole(out),
            scratch_shapes=[pltpu.VMEM((half, width), f32)],
        ),
        out_shape=jax.ShapeDtypeStruct(out, f32),
        compiler_params=vmem(),
        name="few_of",
    )(where, a, g)


def plain_few_of(where, a, g, block, normed):
    half = a.shape[0] if normed else a.shape[0] // 2
    here = a[:half].astype(f32)
    if normed:
        here = rms_norm(here, g)[0].astype(b16).astype(f32)
    return jnp.concatenate([lax.dynamic_slice_in_dim(here, w * block, block, 1) for w in where], axis=1) * 2.0


def pair_kernel(inward, where_ref, a_ref, b_ref, few_a_ref, few_b_ref, wide_ref, out_ref, far_a_ref, far_b_ref):
    half = few_a_ref.shape[0]

    @pl.when(pl.program_id(0) == 0)
    def _():
        far_b_ref[...] = (wide_ref[...] * 0.5).astype(b16)

    far_a_ref[:half, :] = few_a_ref[...].astype(b16)
    far_a_ref[half:, :] = few_b_ref[...].astype(b16)
    if inward:
        out_ref[...] = dot_tn(a_ref[...], b_ref[...]) + dot_tn(far_a_ref[...], far_b_ref[...])
    else:
        out_ref[...] = dot_tn(b_ref[...], a_ref[...]) + dot_tn(far_b_ref[...], far_a_ref[...])


def pair_grads(where, first, a, b, few, wide, block, inward):
    rows, columns, count = a.shape[0], b.shape[1], where.shape[0]
    out = (block, columns) if inward else (columns, block)
    return pl.pallas_call(
        functools.partial(pair_kernel, inward),
        grid_spec=pltpu.PrefetchScalarGridSpec(
            num_scalar_prefetch=1,
            grid=(count,),
            in_specs=[pl.BlockSpec((rows, block), lambda j, at: (0, at[j])), whole((rows, columns))]
            + [pl.BlockSpec((rows // 2, block), lambda j, _: (0, first + j))] * 2
            + [whole((rows, columns))],
            out_specs=pl.BlockSpec(out, lambda j, _: (j, 0)),
            scratch_shapes=[pltpu.VMEM((rows, block), b16), pltpu.VMEM((rows, columns), b16)],
        ),
        out_shape=jax.ShapeDtypeStruct((count * out[0], out[1]), f32),
        compiler_params=vmem(),
        name="pair_grads",
    )(where, a, b, *few, wide)


def plain_pair_grads(where, first, a, b, few, wide, block, inward):
    far_a = (jnp.concatenate(few) * 0.5).astype(b16)
    far_b = (wide * 0.5).astype(b16)
    out = []
    for j, w in enumerate(where):
        near_a = lax.dynamic_slice_in_dim(a, w * block, block, 1)
        other = far_a[:, (first + j) * block : (first + j + 1) * block]
        if inward:
            out.append(dot_tn(near_a, b) + dot_tn(other, far_b))
        else:
            out.append(dot_tn(b, near_a) + dot_tn(far_b, other))
    return jnp.concatenate(out)


def tensor_masks():
    size = lax.axis_size("tensor")
    return [1 << i for i in range(1, size.bit_length() - 1)]


def scatter_sum(parts, masks):
    for mask in masks:
        half = len(parts) // 2
        received = [swap(p, "dp", mask) for p in parts[half:]]
        parts = [a + b for a, b in zip(parts[:half], received)]
    return parts[0]


def relative(masks):
    offsets = [0]
    for mask in reversed(masks):
        offsets = offsets + [o ^ mask for o in offsets]
    return offsets


def body(
    tokens,
    g_attn,
    w_query,
    w_key,
    w_value,
    q_gain,
    k_gain,
    w_out,
    g_mlp,
    w_gate,
    w_up,
    w_down,
    cotangent,
):
    rows, width = tokens.shape
    hd = q_gain.shape[0]
    cosine, sine = rope_tables(SEQ_LEN, hd)
    n_dp = lax.axis_size("dp")
    me = lax.axis_index("dp")
    core = lax.axis_index("tensor") % 2
    core_at = core.astype(jnp.int32).reshape(1)
    x_at = (lax.axis_index("tensor") // 2).astype(jnp.int32).reshape(1)
    half = rows // 2
    block = width // n_dp
    bits = [1 << i for i in range(n_dp.bit_length() - 1)]
    near, far = bits[0], bits[-1]
    middle = bits[1:-1]
    ga, gm, gq, gk = (g.reshape(1, -1) for g in (g_attn, g_mlp, q_gain, k_gain))
    seq = Sequence()

    def mine_of(a):
        return lax.dynamic_slice_in_dim(a, core * half, half, 0)

    def theirs_of(a):
        return lax.dynamic_slice_in_dim(a, (1 - core) * half, half, 0)

    def in_order(mine, theirs):
        out = jnp.zeros((rows,) + mine.shape[1:], mine.dtype)
        out = lax.dynamic_update_slice_in_dim(out, mine, core * half, 0)
        return lax.dynamic_update_slice_in_dim(out, theirs, (1 - core) * half, 0)

    def quarter_of(a):
        size = a.shape[0] // 2
        return lax.dynamic_slice_in_dim(a, (lax.axis_index("tensor") // 2) * size, size, 0)

    def one(value, count):
        return [value] if count == 1 else list(value)

    def pick(kernel, plain):
        return kernel if block % 128 == 0 else plain

    def at(offsets):
        return me ^ jnp.array(offsets, jnp.int32)

    def core_swap(a):
        return swap(a, "tensor", 1)

    def core_swaps(pieces):
        return [swap(a, "tensor", 1) for a in pieces]

    def x_swap(a):
        return swap(a, "tensor", 2)

    few = pick(few_of, plain_few_of)
    pair = pick(pair_grads, plain_pair_grads)
    rest = middle + [far]
    blocks = relative(rest)
    q = len(blocks) // 2
    theirs_at = at([near ^ o for o in blocks])

    cot_mine, cot_theirs = mine_of(cotangent), theirs_of(cotangent)
    cot_own = jnp.concatenate([cot_mine, cot_theirs])
    c0 = cot_mine.astype(f32) * 2.0
    c0, c0_quarter, tokens_then = seq(c0, quarter_of(c0), tokens)
    c1 = swap(c0, "dp", near)
    c2 = swap(c0_quarter, "dp", far)
    tok_mine = mine_of(tokens)
    normed1, query, keys, values, attended, att_wide, mixed_a, *mixed_b = seq(
        *attend(core_at, tokens_then, ga, w_query, w_key, w_value, gq, gk, w_out, cosine, sine)
    )
    mixed_got = seq(*core_swaps(mixed_b))
    mixed_chip, *mixed_split = seq(*sum_of(mixed_a, mixed_got, split=2))
    mixed_x = [x_swap(p) for p in mixed_split]
    near_n = swap(seq(few(theirs_at, tok_mine, ga, block, True)), "dp", near)
    c1, c2, near_n, *mixed_x = seq(c1, c2, near_n, *mixed_x)

    r_a, n0, n0_quarter, *r_split = seq(*resid_of(x_at, tok_mine, mixed_chip, *mixed_x))
    n1 = swap(n0, "dp", near)
    n2 = swap(n0_quarter, "dp", far)
    c2x = x_swap(c2)
    r_b = seq(*core_swaps(r_split))

    normed2, hidden, d_gate, d_up, dn_a, *dn_b, mlp_gain = seq(
        *pick(own_feed, plain_own_feed)(r_a, r_b, cot_own, gm, w_gate, w_up, w_down)
    )
    offsets = relative(middle)
    down_a, down_b, sums = pick(own_rest, plain_own_rest)(
        at(offsets), normed2, cot_own, hidden, d_gate, d_up, w_down, block
    )
    down_a, down_b, *both = seq(down_a, down_b, *sums, *dn_b)
    sums, dn_b = both[:-PIECES], both[-PIECES:]
    n2, c2x = seq(n2, c2x)
    n2x = x_swap(n2)
    n3 = swap(n2, "dp", near)
    n1, *dn_got = seq(n1, *core_swaps(dn_b))
    (dn_chip,) = sum_of(dn_a, dn_got)
    c2 = jnp.concatenate([c2, c2x])
    dn_chip, c2 = seq(dn_chip, c2)
    n1t, c1t = core_swaps((n1, c1))
    n1t, c1t, n2x, n3, dn_chip, c2 = seq(n1t, c1t, n2x, n3, dn_chip, c2)
    dn_x = x_swap(dn_chip)
    c3 = swap(c2, "dp", near)

    def add_group(ns, cs, sums):
        group = pick(group_feed, plain_group_feed)
        return list(seq(*group(at(offsets), ns, cs, gm, w_gate, w_up, w_down, sums, block)))

    n2t, c2t = core_swaps((n2, c2))
    sums = add_group([n1, n1t], [c1, c1t], sums)
    n2t, c2t = seq(n2t, c2t)
    n2xt = seq(core_swap(n2x))
    sums = add_group([n2, n2x, n2t, n2xt], [c2, c2t], sums)
    dn_x, c3, n3 = seq(dn_x, c3, n3)

    n3x = x_swap(n3)
    dn_mine, *dn_split = seq(*sum_of(dn_chip, [dn_x], split=PIECES))
    dn_theirs = seq(*core_swaps(dn_split))
    near_att = swap(att_wide, "dp", near)
    c3t, n3t, down_got = core_swaps((c3, n3, down_b))
    dr_b, dr_mine, d_qkv, d_wide, d1_a, gain_a, gain_q, gain_k, *d1_b = seq(
        *attend_back(
            core_at, dn_mine, dn_theirs, r_a, r_b, cot_own, tokens, query, keys, values, attended,
            gm, ga, gq, gk, w_query, w_key, w_value, w_out, cosine, sine,
        )
    )
    near_r = few(theirs_at, dr_b, gm, block, False)
    near_r, n3x, c3t, n3t, near_att, down_got = seq(near_r, n3x, c3t, n3t, near_att, down_got)
    near_d = swap(d_wide, "dp", near)
    near_r = swap(near_r, "dp", near)
    gains = jnp.concatenate([gain_a[0], gain_q[0], gain_k[0], mlp_gain[0]])
    gains_got = x_swap(gains)
    n3xt = seq(core_swap(n3x))
    sums = add_group([n3, n3x, n3t, n3xt], [c3, c3t], sums)
    k = len(offsets)
    h = k // 2
    lists = [sums[i * k : (i + 1) * k] for i in range(3)]
    keep = [p[:h] for p in lists]
    send = [p[h:] for p in lists]

    def first_step(parts):
        return [swap(p, "dp", middle[0]) for p in parts]

    def finish(keep, got):
        return scatter_sum([a + b for a, b in zip(keep, got)], middle[1:])

    got = first_step(send[0]) + first_step(send[1])
    gains = gains + seq(gains_got)
    near_nt, gains_got, *d1_got = seq(*core_swaps((near_n, gains, *d1_b)))
    gains = gains + gains_got
    gains_got = swap(gains, "dp", near)
    (d1_chip,), (down_chip,) = sum_of(d1_a, d1_got), sum_of(down_a, [down_got])
    d1_chip, down_chip = seq(d1_chip, down_chip)
    d1_x = x_swap(d1_chip)
    near_d, near_r, gains_got, down_chip, *got = seq(near_d, near_r, gains_got, down_chip, *got)
    gains = gains + gains_got
    near_ns = [near_n, near_nt]
    down_x = x_swap(down_chip)

    def ins(i):
        return pair(at(blocks[i * q : (i + 1) * q]), i * q, normed1, d_qkv, near_ns, near_d, block, True)

    def outs(i):
        return pair(at(blocks[i * q : (i + 1) * q]), i * q, dr_b, attended, near_rs, near_att, block, False)

    near_rt = core_swap(near_r)
    in_1 = seq(ins(1))
    in_mid = swap(in_1, "dp", rest[0])
    near_rs = [near_r, seq(near_rt)]
    out_1 = seq(outs(1))
    out_mid = swap(out_1, "dp", rest[0])
    gains_got = swap(gains, "dp", rest[0])
    in_0, out_0 = seq(ins(0), outs(0))
    summed_down = finish(keep[0], got[:h])
    summed_gate = finish(keep[1], got[h:])
    if len(rest) == 2:
        summed_down, summed_gate = seq(summed_down, summed_gate)

    def split(a):
        return list(a.reshape(q, a.shape[0] // q, a.shape[1]))

    d1_x = seq(d1_x)
    gt_mine, *gt_split = seq(*back_of(dr_mine, d1_chip, d1_x, tok_mine, ga))
    gt_theirs = jnp.concatenate(seq(*core_swaps(gt_split)))
    grad_tokens = seq(in_order(gt_mine, gt_theirs))
    in_mid, out_mid, gains_got, down_x, *send_up = seq(in_mid, out_mid, gains_got, down_x, *send[2])
    got_up = first_step(send_up)
    gains = gains + gains_got
    gains_got = swap(gains, "dp", far)
    both = seq(*split(in_0 + in_mid), *split(out_0 + out_mid))
    summed_qkv, summed_out = scatter_sum(both[:q], rest[1:]), scatter_sum(both[q:], rest[1:])
    down_mine, *down_split = seq(*sum_of(down_chip, [down_x], split=PIECES))
    down_theirs = seq(*core_swaps(down_split))
    down_theirs, r_theirs = jnp.concatenate(down_theirs), jnp.concatenate(r_b)
    output = seq(in_order((r_a + down_mine).astype(b16), (r_theirs + down_theirs).astype(b16)))
    gains = gains + gains_got
    for mask in rest[1:-1]:
        gains = gains + swap(gains, "dp", mask)
    if len(rest) == 2:
        summed_qkv, summed_out, *got_up = seq(summed_qkv, summed_out, *got_up)
    summed_up = finish(keep[2], got_up)
    nq, nk = w_query.shape[1], w_key.shape[1]
    gains = gains + 0.0 * seq.token.astype(f32)
    return (
        output,
        grad_tokens,
        gains[:width],
        summed_qkv[:, :nq],
        summed_qkv[:, nq : nq + nk],
        summed_qkv[:, nq + nk :],
        gains[width : width + hd],
        gains[width + hd : width + 2 * hd],
        summed_out,
        gains[width + 2 * hd :],
        summed_gate,
        summed_up,
        summed_down,
    )


def solution(mesh):
    in_specs = (
        P("dp", None),
        P(),
        P(None, "tensor"),
        P(None, "tensor"),
        P(None, "tensor"),
        P(),
        P(),
        P("tensor", None),
        P(),
        P(None, "tensor"),
        P(None, "tensor"),
        P("tensor", None),
        P("dp", None),
    )
    out_specs = (
        P("dp", None),
        P("dp", None),
        P(),
        P("dp", "tensor"),
        P("dp", "tensor"),
        P("dp", "tensor"),
        P(),
        P(),
        P("tensor", "dp"),
        P(),
        P("dp", "tensor"),
        P("dp", "tensor"),
        P("tensor", "dp"),
    )
    return jax.shard_map(body, mesh=mesh, in_specs=in_specs, out_specs=out_specs, check_vma=False)
```

```python
import functools

import jax
import jax.numpy as jnp
from jax import lax
from jax.experimental import pallas as pl
from jax.experimental.pallas import tpu as pltpu
from jax.sharding import PartitionSpec as P

SEQ_LEN = 256


EPS = 1e-06
THETA = 1000000.0

f32 = jnp.float32
b16 = jnp.bfloat16


def rms_norm(values, gain):
    inv_rms = lax.rsqrt(jnp.mean(values * values, axis=-1, keepdims=True) + EPS)
    unit_rows = values * inv_rms
    return (unit_rows * gain, unit_rows, inv_rms)


def rms_back(grads, gain, unit_rows, inv_rms):
    scaled = grads * gain
    return inv_rms * (scaled - unit_rows * jnp.mean(scaled * unit_rows, axis=-1, keepdims=True))


def swap(value, axis, mask):
    size = lax.axis_size(axis)
    return lax.ppermute(value, axis, [(i, i ^ mask) for i in range(size)])


class Sequence:
    def __init__(self):
        self.token = None

    def __call__(self, *values):
        if self.token is None:
            out = lax.optimization_barrier(values)
        else:
            *out, self.token = lax.optimization_barrier((*values, self.token))
        self.token = out[0].reshape(-1)[:1] if self.token is None else self.token
        return out[0] if len(out) == 1 else tuple(out)


def dot(a, b):
    return jnp.dot(a, b, preferred_element_type=f32)


def dot_nt(a, b):
    return lax.dot_general(a, b, (((1,), (1,)), ((), ())), preferred_element_type=f32)


def dot_tn(a, b):
    return lax.dot_general(a, b, (((0,), (0,)), ((), ())), preferred_element_type=f32)


TILE = 512
PIECES = 4


def vmem(mib=60):
    return pltpu.CompilerParams(vmem_limit_bytes=mib << 20)


def whole(shape):
    return pl.BlockSpec(shape, lambda *_: (0,) * len(shape))


def gated(nb, cb, wg_ref, wu_ref, wd_ref):
    gate_pre = dot(nb[...], wg_ref[...])
    up_pre = dot(nb[...], wu_ref[...])
    d_hidden = dot_nt(cb[...], wd_ref[...])
    sig = jax.nn.sigmoid(gate_pre)
    act = gate_pre * sig
    hidden = (act * up_pre).astype(b16)
    d_up = (d_hidden * act).astype(b16)
    d_gate = (d_hidden * up_pre * (sig * (1.0 + gate_pre * (1.0 - sig)))).astype(b16)
    return hidden, d_gate, d_up


def own_kernel(ra_ref, *refs):
    rb_refs, refs = refs[:PIECES], refs[PIECES:]
    cot_ref, g_ref, wg_ref, wu_ref, wd_ref, normed_ref, hid_ref, dg_ref, du_ref, dna_ref = refs[:10]
    dnb_refs, (gain_ref, rms_ref) = refs[10:-2], refs[-2:]
    step = pl.program_id(0)
    half = ra_ref.shape[0]
    part = half // PIECES

    @pl.when(step == 0)
    def _():
        for i, ref in enumerate((ra_ref, *rb_refs)):
            r = ref[...]
            at = 0 if i == 0 else half + (i - 1) * part
            inv = lax.rsqrt(jnp.mean(r * r, axis=-1, keepdims=True) + EPS)
            rms_ref[at : at + r.shape[0], :] = inv
            normed_ref[at : at + r.shape[0], :] = (r * inv * g_ref[...]).astype(b16)
        dna_ref[...] = jnp.zeros_like(dna_ref)
        for ref in dnb_refs:
            ref[...] = jnp.zeros_like(ref)

    hidden, d_gate, d_up = gated(normed_ref, cot_ref, wg_ref, wu_ref, wd_ref)
    hid_ref[...] = hidden
    dg_ref[...] = d_gate
    du_ref[...] = d_up
    dna_ref[...] += dot_nt(d_gate[:half], wg_ref[...]) + dot_nt(d_up[:half], wu_ref[...])
    far = dot_nt(d_gate[half:], wg_ref[...]) + dot_nt(d_up[half:], wu_ref[...])
    for i, ref in enumerate(dnb_refs):
        ref[...] += far[i * part : (i + 1) * part]

    @pl.when(step == pl.num_programs(0) - 1)
    def _():
        total = jnp.sum(dna_ref[...] * (ra_ref[...] * rms_ref[:half, :]), axis=0, keepdims=True)
        for i, (r_ref, d_ref) in enumerate(zip(rb_refs, dnb_refs)):
            at = half + i * part
            unit = r_ref[...] * rms_ref[at : at + part, :]
            total += jnp.sum(d_ref[...] * unit, axis=0, keepdims=True)
        gain_ref[...] = total


def own_feed(r_a, r_b, cot, g, w_gate, w_up, w_down):
    half, width = r_a.shape
    rows, hidden = 2 * half, w_gate.shape[1]
    col = pl.BlockSpec((rows, TILE), lambda i: (0, i))
    wide = jax.ShapeDtypeStruct((rows, hidden), b16)
    piece = (half // PIECES, width)
    return pl.pallas_call(
        own_kernel,
        grid=(hidden // TILE,),
        in_specs=[whole((half, width))]
        + [whole(piece)] * PIECES
        + [
            whole((rows, width)),
            whole((1, width)),
            pl.BlockSpec((width, TILE), lambda i: (0, i)),
            pl.BlockSpec((width, TILE), lambda i: (0, i)),
            pl.BlockSpec((TILE, width), lambda i: (i, 0)),
        ],
        out_specs=[
            whole((rows, width)),
            col,
            col,
            col,
            whole((half, width)),
        ]
        + [whole(piece)] * PIECES
        + [whole((1, width))],
        out_shape=[
            jax.ShapeDtypeStruct((rows, width), b16),
            wide,
            wide,
            wide,
            jax.ShapeDtypeStruct((half, width), f32),
        ]
        + [jax.ShapeDtypeStruct(piece, f32)] * PIECES
        + [jax.ShapeDtypeStruct((1, width), f32)],
        scratch_shapes=[pltpu.VMEM((rows, 1), f32)],
        compiler_params=vmem(),
        name="own_feed",
    )(r_a, *r_b, cot, g.reshape(1, -1), w_gate, w_up, w_down)


def put_columns(at_ref, cc_ref, nb_ref, cb_ref, where_ref, count, block):
    for j in range(count):
        here = pl.ds(pl.multiple_of(where_ref[j] * block, 128), block)
        at_ref[j * block : (j + 1) * block, :] = nb_ref[:, here].T
        cc_ref[:, j * block : (j + 1) * block] = cb_ref[:, here]


def put_grads(sums, at_ref, cc_ref, hidden, d_gate, d_up, block, before=None):
    down = dot_tn(hidden, cc_ref[...])
    gate = dot(at_ref[...], d_gate)
    up = dot(at_ref[...], d_up)
    count = len(sums) // 3
    for j in range(count):
        part = slice(j * block, (j + 1) * block)
        for k, fresh in ((j, down[:, part]), (count + j, gate[part]), (2 * count + j, up[part])):
            old = 0.0 if before is None else before[k][...]
            sums[k][...] = fresh + old


def rest_kernel(where_ref, nb_ref, cb_ref, hid_ref, dg_ref, du_ref, wd_ref, *rest):
    count = (len(rest) - 4) // 3
    ya_ref, yb_ref, *sums = rest[:-2]
    at_ref, cc_ref = rest[-2:]
    half = ya_ref.shape[0]
    block = cc_ref.shape[1] // count

    @pl.when(pl.program_id(0) == 0)
    def _():
        put_columns(at_ref, cc_ref, nb_ref, cb_ref, where_ref, count, block)
        ya_ref[...] = jnp.zeros_like(ya_ref)
        yb_ref[...] = jnp.zeros_like(yb_ref)

    hidden = hid_ref[...]
    ya_ref[...] += dot(hidden[:half], wd_ref[...])
    yb_ref[...] += dot(hidden[half:], wd_ref[...])
    put_grads(sums, at_ref, cc_ref, hidden, dg_ref[...], du_ref[...], block)


def sum_specs(count, block, hidden):
    specs = [pl.BlockSpec((TILE, block), lambda i, *_: (i, 0))] * count
    specs += [pl.BlockSpec((block, TILE), lambda i, *_: (0, i))] * (2 * count)
    shapes = [jax.ShapeDtypeStruct((hidden, block), f32)] * count
    shapes += [jax.ShapeDtypeStruct((block, hidden), f32)] * (2 * count)
    return specs, shapes


def own_rest(where, nb, cb, hidden, d_gate, d_up, w_down, block):
    rows, width = nb.shape
    count = where.shape[0]
    half, ff = rows // 2, hidden.shape[1]
    specs, shapes = sum_specs(count, block, ff)
    col = pl.BlockSpec((rows, TILE), lambda i, *_: (0, i))
    part = jax.ShapeDtypeStruct((half, width), f32)
    out = pl.pallas_call(
        rest_kernel,
        grid_spec=pltpu.PrefetchScalarGridSpec(
            num_scalar_prefetch=1,
            grid=(ff // TILE,),
            in_specs=[
                whole((rows, width)),
                whole((rows, width)),
                col,
                col,
                col,
                pl.BlockSpec((TILE, width), lambda i, *_: (i, 0)),
            ],
            out_specs=[whole((half, width)), whole((half, width))] + specs,
            scratch_shapes=[
                pltpu.VMEM((count * block, rows), b16),
                pltpu.VMEM((rows, count * block), b16),
            ],
        ),
        out_shape=[part, part] + shapes,
        compiler_params=vmem(),
        name="own_rest",
    )(where, nb, cb, hidden, d_gate, d_up, w_down)
    return out[0], out[1], list(out[2:])


def group_kernel(n_pieces, c_pieces, count, where_ref, *refs):
    n_refs, refs = refs[:n_pieces], refs[n_pieces:]
    c_refs, refs = refs[:c_pieces], refs[c_pieces:]
    g_ref, wg_ref, wu_ref, wd_ref = refs[:4]
    before = refs[4 : 4 + 3 * count]
    sums = refs[4 + 3 * count : 4 + 6 * count]
    nb_ref, cb_ref, at_ref, cc_ref = refs[4 + 6 * count :]
    block = cc_ref.shape[1] // count

    @pl.when(pl.program_id(0) == 0)
    def _():
        at = 0
        for n_ref in n_refs:
            size = n_ref.shape[0]
            nb_ref[at : at + size, :] = (n_ref[...] * g_ref[...]).astype(b16)
            at += size
        at = 0
        for c_ref in c_refs:
            size = c_ref.shape[0]
            cb_ref[at : at + size, :] = (c_ref[...] * 0.5).astype(b16)
            at += size
        put_columns(at_ref, cc_ref, nb_ref, cb_ref, where_ref, count, block)

    hidden, d_gate, d_up = gated(nb_ref, cb_ref, wg_ref, wu_ref, wd_ref)
    put_grads(sums, at_ref, cc_ref, hidden, d_gate, d_up, block, before)


def group_feed(where, ns, cs, g, w_gate, w_up, w_down, before, block):
    width, ff = w_gate.shape
    count = where.shape[0]
    rows = sum(n.shape[0] for n in ns)
    specs, shapes = sum_specs(count, block, ff)
    return list(
        pl.pallas_call(
            functools.partial(group_kernel, len(ns), len(cs), count),
            grid_spec=pltpu.PrefetchScalarGridSpec(
                num_scalar_prefetch=1,
                grid=(ff // TILE,),
                in_specs=[whole(a.shape) for a in (*ns, *cs)]
                + [
                    whole((1, width)),
                    pl.BlockSpec((width, TILE), lambda i, *_: (0, i)),
                    pl.BlockSpec((width, TILE), lambda i, *_: (0, i)),
                    pl.BlockSpec((TILE, width), lambda i, *_: (i, 0)),
                ]
                + specs,
                out_specs=specs,
                scratch_shapes=[
                    pltpu.VMEM((rows, width), b16),
                    pltpu.VMEM((rows, width), b16),
                    pltpu.VMEM((count * block, rows), b16),
                    pltpu.VMEM((rows, count * block), b16),
                ],
            ),
            out_shape=shapes,
            compiler_params=vmem(),
            name="group_feed",
        )(where, *ns, *cs, g.reshape(1, -1), w_gate, w_up, w_down, *before)
    )


def sum_kernel(count, *refs):
    a_ref, b_refs, outs = refs[0], refs[1 : 1 + count], refs[1 + count :]
    size = a_ref.shape[0] // count
    for i, b_ref in enumerate(b_refs):
        at = slice(i * size, (i + 1) * size)
        total = a_ref[at, :] + b_ref[...]
        outs[0][at, :] = total
    pieces = outs[1:]
    for i, piece in enumerate(pieces):
        piece[...] = outs[0][i * piece.shape[0] : (i + 1) * piece.shape[0], :]


def sum_of(a, bs, split=0):
    shapes = [jax.ShapeDtypeStruct(a.shape, f32)]
    shapes += [jax.ShapeDtypeStruct((a.shape[0] // max(split, 1), a.shape[1]), f32)] * split
    return pl.pallas_call(
        functools.partial(sum_kernel, len(bs)),
        in_specs=[whole(x.shape) for x in (a, *bs)],
        out_specs=[whole(x.shape) for x in shapes],
        out_shape=shapes,
        grid=(1,),
        compiler_params=vmem(),
        name="sum_of",
    )(a, *bs)


def resid_kernel(x_at_ref, tok_ref, a_ref, b_ref, c_ref, r_ref, n_ref, quarter_ref, *pieces):
    size = pieces[0].shape[0]
    for i, piece in enumerate(pieces):
        at = slice(i * size, (i + 1) * size)
        part, first = (b_ref, 0) if i < len(pieces) // 2 else (c_ref, len(pieces) // 2)
        far = part[(i - first) * size : (i - first + 1) * size, :]
        resid = tok_ref[at, :].astype(f32) + (a_ref[at, :] + far)
        r_ref[at, :] = resid
        piece[...] = resid
        n_ref[at, :] = resid * lax.rsqrt(jnp.mean(resid * resid, axis=-1, keepdims=True) + EPS)
    small = quarter_ref.shape[0]
    quarter_ref[...] = n_ref[pl.ds(pl.multiple_of(x_at_ref[0] * small, small), small), :]


def resid_of(x_at, tok, a, b, c):
    rows, width = a.shape
    shapes = [(rows, width), (rows, width), (rows // 2, width)] + [(rows // PIECES, width)] * PIECES
    return pl.pallas_call(
        resid_kernel,
        grid_spec=pltpu.PrefetchScalarGridSpec(
            num_scalar_prefetch=1,
            grid=(1,),
            in_specs=[whole(a.shape)] * 2 + [whole(b.shape)] * 2,
            out_specs=[whole(s) for s in shapes],
        ),
        out_shape=[jax.ShapeDtypeStruct(s, f32) for s in shapes],
        compiler_params=vmem(),
        name="resid_of",
    )(x_at, tok, a, b, c)


def feed(normed, cot, w_gate, w_up, w_down):
    gate_pre = dot(normed, w_gate)
    up_pre = dot(normed, w_up)
    d_hidden = dot_nt(cot, w_down)
    sigmoid_g = jax.nn.sigmoid(gate_pre)
    act_gate = gate_pre * sigmoid_g
    hidden = (act_gate * up_pre).astype(b16)
    d_up = (d_hidden * act_gate).astype(b16)
    d_gate = (d_hidden * up_pre * (sigmoid_g * (1.0 + gate_pre * (1.0 - sigmoid_g)))).astype(b16)
    return hidden, d_gate, d_up


def plain_grads(where, normed, cot, parts, block):
    hidden, d_gate, d_up = parts
    takes = [functools.partial(lax.dynamic_slice_in_dim, start_index=w * block, slice_size=block, axis=1) for w in where]
    pair = jnp.concatenate([d_gate, d_up], axis=1)
    both = [dot_tn(take(normed), pair) for take in takes]
    ff = hidden.shape[1]
    return [dot_tn(hidden, take(cot)) for take in takes] + [b[:, :ff] for b in both] + [b[:, ff:] for b in both]


def plain_own_feed(r_a, r_b, cot, g, w_gate, w_up, w_down):
    resid = jnp.concatenate([r_a, *r_b])
    normed, unit, _ = rms_norm(resid, g)
    normed = normed.astype(b16)
    parts = feed(normed, cot, w_gate, w_up, w_down)
    total = dot_nt(parts[1], w_gate) + dot_nt(parts[2], w_up)
    half = r_a.shape[0]
    gain = jnp.sum(total * unit, axis=0, keepdims=True)
    return (normed, *parts, total[:half], *jnp.split(total[half:], PIECES), gain)


def plain_own_rest(where, nb, cb, hidden, d_gate, d_up, w_down, block):
    down = dot(hidden, w_down)
    half = nb.shape[0] // 2
    return down[:half], down[half:], plain_grads(where, nb, cb, (hidden, d_gate, d_up), block)


def plain_group_feed(where, ns, cs, g, w_gate, w_up, w_down, before, block):
    normed = (jnp.concatenate(ns) * g).astype(b16)
    cot = (jnp.concatenate(cs) * 0.5).astype(b16)
    parts = feed(normed, cot, w_gate, w_up, w_down)
    return [old + new for old, new in zip(before, plain_grads(where, normed, cot, parts, block))]


def rope_tables(length, width):
    half = width // 2
    inverse = THETA ** (-(jnp.arange(half).astype(f32) * 2.0 / width))
    angles = jnp.arange(length).astype(f32)[:, None] * inverse[None, :]
    angles = jnp.concatenate([angles, angles], axis=1)
    sign = jnp.where(jnp.arange(width) < half, -1.0, 1.0).astype(f32)
    return jnp.cos(angles), jnp.sin(angles) * sign[None, :]


def turn(values, cosine, sine):
    return values * cosine + pltpu.roll(values, values.shape[-1] // 2, 1) * sine


def turn_back(grads, cosine, sine):
    return grads * cosine + pltpu.roll(grads * sine, grads.shape[-1] // 2, 1)


def norm_of(values):
    inv = lax.rsqrt(jnp.mean(values * values, axis=-1, keepdims=True) + EPS)
    return values * inv, inv


def norm_back(scaled, unit, inv):
    return inv * (scaled - unit * jnp.mean(scaled * unit, axis=-1, keepdims=True))


def softmax_of(q_rot, k_rot):
    length, width = q_rot.shape
    scores = dot_nt(q_rot, k_rot) * (width**-0.5)
    at = lax.broadcasted_iota(jnp.int32, (length, length), 0)
    to = lax.broadcasted_iota(jnp.int32, (length, length), 1)
    scores = jnp.where(at >= to, scores, -1e30)
    grown = jnp.exp(scores - jnp.max(scores, axis=-1, keepdims=True))
    return grown * (1.0 / jnp.sum(grown, axis=-1, keepdims=True))


def attend_kernel(half, core_ref, tok_ref, g_ref, wq_ref, wk_ref, wv_ref, qg_ref, kg_ref, wo_ref, cos_ref, sin_ref, *outs):
    n_ref, q_ref, k_ref, v_ref, att_ref, wide_ref, mine_ref = outs[:7]
    width = qg_ref.shape[1]
    cosine, sine = cos_ref[...], sin_ref[...]
    unit, _ = norm_of(tok_ref[...].astype(f32))
    normed = (unit * g_ref[...]).astype(b16)
    n_ref[...] = normed
    query = dot(normed, wq_ref[...])
    keys = dot(normed, wk_ref[...])
    values = dot(normed, wv_ref[...]).astype(b16)
    q_ref[...] = query
    k_ref[...] = keys
    v_ref[...] = values
    kv_heads = keys.shape[1] // width
    share = query.shape[1] // keys.shape[1]
    for kv in range(kv_heads):
        at = slice(kv * width, (kv + 1) * width)
        k_unit, _ = norm_of(keys[:, at])
        k_rot = turn(k_unit * kg_ref[...], cosine, sine).astype(b16)
        for h in range(kv * share, (kv + 1) * share):
            to = slice(h * width, (h + 1) * width)
            q_unit, _ = norm_of(query[:, to])
            q_rot = turn(q_unit * qg_ref[...], cosine, sine).astype(b16)
            probs = softmax_of(q_rot, k_rot).astype(b16)
            att_ref[:, to] = dot(probs, values[:, at]).astype(b16)
    wide_ref[...] = att_ref[...].astype(f32) * 2.0
    mixed = dot(att_ref[...], wo_ref[...])

    @pl.when(pl.program_id(0) < half)
    def _():
        for i, ref in enumerate(outs[7:]):
            ref[...] = mixed[i * ref.shape[0] : (i + 1) * ref.shape[0]]

    @pl.when(pl.program_id(0) >= half)
    def _():
        mine_ref[...] = mixed


def attend(core, tokens, g, wq, wk, wv, qg, kg, wo, cosine, sine):
    rows, width = tokens.shape
    seqs = rows // SEQ_LEN
    half = seqs // 2

    def source(i, core_ref):
        mine = core_ref[0]
        return (jnp.where(i < half, (1 - mine) * half + i, mine * half + i - half), 0)

    def place(i, _):
        return ((i + half) % seqs, 0)

    def out(columns, dtype):
        return pl.BlockSpec((SEQ_LEN, columns), place), jax.ShapeDtypeStruct((rows, columns), dtype)

    nq, nk = wq.shape[1], wk.shape[1]
    outs = [out(width, b16), out(nq, f32), out(nk, f32), out(nk, b16), out(nq, b16), out(nq, f32)]
    part = jax.ShapeDtypeStruct((rows // 2, width), f32)
    piece = SEQ_LEN // PIECES
    return pl.pallas_call(
        functools.partial(attend_kernel, half),
        grid_spec=pltpu.PrefetchScalarGridSpec(
            num_scalar_prefetch=1,
            grid=(seqs,),
            in_specs=[pl.BlockSpec((SEQ_LEN, width), source)]
            + [whole(a.shape) for a in (g, wq, wk, wv, qg, kg, wo, cosine, sine)],
            out_specs=[o[0] for o in outs]
            + [
                pl.BlockSpec((SEQ_LEN, width), lambda i, _: (jnp.maximum(i - half, 0), 0)),
            ]
            + [pl.BlockSpec((piece, width), lambda i, _: (jnp.minimum(i, half - 1), 0))] * PIECES,
        ),
        out_shape=[o[1] for o in outs]
        + [part]
        + [jax.ShapeDtypeStruct((piece * half, width), f32)] * PIECES,
        compiler_params=vmem(),
        name="attend",
    )(core, tokens, g, wq, wk, wv, qg, kg, wo, cosine, sine)


def attend_back_kernel(half, core_ref, *refs):
    dnb_refs, rb_refs, refs = refs[:PIECES], refs[PIECES : 2 * PIECES], refs[2 * PIECES :]
    ins, outs = refs[:18], refs[18:]
    dna_ref, ra_ref, cot_ref, tok_ref, q_ref, k_ref, v_ref, att_ref = ins[:8]
    gm_ref, ga_ref, qg_ref, kg_ref, wq_ref, wk_ref, wv_ref, wo_ref, cos_ref, sin_ref = ins[8:]
    dr_ref, drm_ref, dqkv_ref, wide_ref, d1a_ref, ga_out, gq_out, gk_out = outs[:8]
    d1b_refs, (r_ref, dn_ref) = outs[8:-2], outs[-2:]
    step = pl.program_id(0)
    width = qg_ref.shape[1]
    cosine, sine = cos_ref[...], sin_ref[...]

    @pl.when(step == 0)
    def _():
        ga_out[...] = jnp.zeros_like(ga_out)
        gq_out[...] = jnp.zeros_like(gq_out)
        gk_out[...] = jnp.zeros_like(gk_out)

    mine = step < half

    @pl.when(mine)
    def _():
        r_ref[...] = ra_ref[...]
        dn_ref[...] = dna_ref[...]

    @pl.when(step >= half)
    def _():
        for i, (r_piece, dn_piece) in enumerate(zip(rb_refs, dnb_refs)):
            at = slice(i * r_piece.shape[0], (i + 1) * r_piece.shape[0])
            r_ref[at, :] = r_piece[...]
            dn_ref[at, :] = dn_piece[...]

    unit2, inv2 = norm_of(r_ref[...])
    scaled = dn_ref[...] * gm_ref[...]
    d_resid = cot_ref[...].astype(f32) + norm_back(scaled, unit2, inv2)
    d_resid_b = d_resid.astype(b16)
    dr_ref[...] = d_resid_b

    @pl.when(mine)
    def _():
        drm_ref[...] = d_resid

    d_att = dot_nt(d_resid_b, wo_ref[...]).astype(b16)
    nq, nk = q_ref.shape[1], k_ref.shape[1]
    share = nq // nk
    for kv in range(nk // width):
        at = slice(kv * width, (kv + 1) * width)
        k_unit, k_inv = norm_of(k_ref[:, at])
        k_rot = turn(k_unit * kg_ref[...], cosine, sine).astype(b16)
        values = v_ref[:, at]
        d_krot = d_values = 0.0
        for h in range(kv * share, (kv + 1) * share):
            to = slice(h * width, (h + 1) * width)
            q_unit, q_inv = norm_of(q_ref[:, to])
            q_rot = turn(q_unit * qg_ref[...], cosine, sine).astype(b16)
            probs = softmax_of(q_rot, k_rot)
            d_head = d_att[:, to]
            d_prob = dot_nt(d_head, values)
            delta = jnp.sum(d_head.astype(f32) * att_ref[:, to].astype(f32), axis=-1, keepdims=True)
            d_score = (probs * (d_prob - delta) * (width**-0.5)).astype(b16)
            d_krot += dot_tn(d_score, q_rot)
            d_values += dot_tn(probs.astype(b16), d_head)
            d_qn = turn_back(dot(d_score, k_rot), cosine, sine)
            gq_out[...] += jnp.sum(d_qn * q_unit, axis=0, keepdims=True)
            dqkv_ref[:, to] = norm_back(d_qn * qg_ref[...], q_unit, q_inv).astype(b16)
        d_kn = turn_back(d_krot, cosine, sine)
        gk_out[...] += jnp.sum(d_kn * k_unit, axis=0, keepdims=True)
        here = slice(nq + kv * width, nq + (kv + 1) * width)
        dqkv_ref[:, here] = norm_back(d_kn * kg_ref[...], k_unit, k_inv).astype(b16)
        here = slice(nq + nk + kv * width, nq + nk + (kv + 1) * width)
        dqkv_ref[:, here] = d_values.astype(b16)
    wide_ref[...] = dqkv_ref[...].astype(f32) * 2.0
    d_norm1 = (
        dot_nt(dqkv_ref[:, :nq], wq_ref[...])
        + dot_nt(dqkv_ref[:, nq : nq + nk], wk_ref[...])
        + dot_nt(dqkv_ref[:, nq + nk :], wv_ref[...])
    )
    unit1, _ = norm_of(tok_ref[...].astype(f32))
    ga_out[...] += jnp.sum(d_norm1 * unit1, axis=0, keepdims=True)

    @pl.when(mine)
    def _():
        d1a_ref[...] = d_norm1

    @pl.when(step >= half)
    def _():
        for i, ref in enumerate(d1b_refs):
            ref[...] = d_norm1[i * ref.shape[0] : (i + 1) * ref.shape[0]]


def attend_back(core, dn_a, dn_b, r_a, r_b, cot, tokens, q, k, v, att, gm, ga, qg, kg, wq, wk, wv, wo, cosine, sine):
    rows, width = tokens.shape
    seqs = rows // SEQ_LEN
    half = seqs // 2

    def source(i, core_ref):
        mine = core_ref[0]
        return (jnp.where(i < half, mine * half + i, (1 - mine) * half + i - half), 0)

    def low(i, _):
        return (jnp.minimum(i, half - 1), 0)

    def high(i, _):
        return (jnp.maximum(i - half, 0), 0)

    def same(i, _):
        return (i, 0)

    def block(columns, place):
        return pl.BlockSpec((SEQ_LEN, columns), place)

    nq, nk = wq.shape[1], wk.shape[1]
    part = jax.ShapeDtypeStruct((rows // 2, width), f32)
    consts = (gm, ga, qg, kg, wq, wk, wv, wo, cosine, sine)
    small = [(1, width), qg.shape, kg.shape]
    piece = SEQ_LEN // PIECES
    return pl.pallas_call(
        functools.partial(attend_back_kernel, half),
        grid_spec=pltpu.PrefetchScalarGridSpec(
            num_scalar_prefetch=1,
            grid=(seqs,),
            in_specs=[
                pl.BlockSpec((piece, width), high),
            ]
            * (2 * PIECES)
            + [
                block(width, low),
                block(width, low),
                block(width, same),
                block(width, source),
                block(nq, same),
                block(nk, same),
                block(nk, same),
                block(nq, same),
            ]
            + [whole(a.shape) for a in consts],
            out_specs=[
                block(width, same),
                block(width, low),
                block(nq + 2 * nk, same),
                block(nq + 2 * nk, same),
                block(width, low),
            ]
            + [whole(s) for s in small]
            + [pl.BlockSpec((piece, width), high)] * PIECES,
            scratch_shapes=[pltpu.VMEM((SEQ_LEN, width), f32)] * 2,
        ),
        out_shape=[
            jax.ShapeDtypeStruct((rows, width), b16),
            part,
            jax.ShapeDtypeStruct((rows, nq + 2 * nk), b16),
            jax.ShapeDtypeStruct((rows, nq + 2 * nk), f32),
            part,
        ]
        + [jax.ShapeDtypeStruct(s, f32) for s in small]
        + [jax.ShapeDtypeStruct((piece * half, width), f32)] * PIECES,
        compiler_params=vmem(),
        name="attend_back",
    )(core, *dn_b, *r_b, dn_a, r_a, cot, tokens, q, k, v, att, *consts)


def back_kernel(dr_ref, a_ref, b_ref, tok_ref, g_ref, out_ref, *pieces):
    size = pieces[0].shape[0]
    for i, piece in enumerate(pieces):
        at = slice(i * size, (i + 1) * size)
        unit, inv = norm_of(tok_ref[at, :].astype(f32))
        grads = dr_ref[at, :] + norm_back((a_ref[at, :] + b_ref[at, :]) * g_ref[...], unit, inv)
        out_ref[at, :] = grads
        piece[...] = grads


def back_of(dr, a, b, tok, g):
    rows, width = a.shape
    shapes = [(rows, width)] + [(rows // PIECES, width)] * PIECES
    return pl.pallas_call(
        back_kernel,
        grid=(1,),
        in_specs=[whole(x.shape) for x in (dr, a, b, tok, g)],
        out_specs=[whole(x) for x in shapes],
        out_shape=[jax.ShapeDtypeStruct(x, f32) for x in shapes],
        compiler_params=vmem(),
        name="back_of",
    )(dr, a, b, tok, g)


def few_kernel(normed, where_ref, a_ref, g_ref, out_ref, row_ref):
    block = out_ref.shape[1] // where_ref.shape[0]
    here = a_ref[...].astype(f32)
    if normed:
        here = (norm_of(here)[0] * g_ref[...]).astype(b16).astype(f32)
    row_ref[...] = here
    for j in range(where_ref.shape[0]):
        at = pl.ds(pl.multiple_of(where_ref[j] * block, 128), block)
        out_ref[:, j * block : (j + 1) * block] = row_ref[:, at]


def few_of(where, a, g, block, normed):
    half, width = a.shape[0] if normed else a.shape[0] // 2, a.shape[1]
    out = (half, where.shape[0] * block)
    return pl.pallas_call(
        functools.partial(few_kernel, normed),
        grid_spec=pltpu.PrefetchScalarGridSpec(
            num_scalar_prefetch=1,
            grid=(1,),
            in_specs=[whole((half, width)), whole(g.shape)],
            out_specs=whole(out),
            scratch_shapes=[pltpu.VMEM((half, width), f32)],
        ),
        out_shape=jax.ShapeDtypeStruct(out, f32),
        compiler_params=vmem(),
        name="few_of",
    )(where, a, g)


def plain_few_of(where, a, g, block, normed):
    half = a.shape[0] if normed else a.shape[0] // 2
    here = a[:half].astype(f32)
    if normed:
        here = rms_norm(here, g)[0].astype(b16).astype(f32)
    return jnp.concatenate([lax.dynamic_slice_in_dim(here, w * block, block, 1) for w in where], axis=1) * 2.0


def pair_kernel(inward, where_ref, a_ref, b_ref, few_a_ref, few_b_ref, wide_ref, out_ref, far_a_ref, far_b_ref):
    half = few_a_ref.shape[0]

    @pl.when(pl.program_id(0) == 0)
    def _():
        far_b_ref[...] = (wide_ref[...] * 0.5).astype(b16)

    far_a_ref[:half, :] = few_a_ref[...].astype(b16)
    far_a_ref[half:, :] = few_b_ref[...].astype(b16)
    if inward:
        out_ref[...] = dot_tn(a_ref[...], b_ref[...]) + dot_tn(far_a_ref[...], far_b_ref[...])
    else:
        out_ref[...] = dot_tn(b_ref[...], a_ref[...]) + dot_tn(far_b_ref[...], far_a_ref[...])


def pair_grads(where, first, a, b, few, wide, block, inward):
    rows, columns, count = a.shape[0], b.shape[1], where.shape[0]
    out = (block, columns) if inward else (columns, block)
    return pl.pallas_call(
        functools.partial(pair_kernel, inward),
        grid_spec=pltpu.PrefetchScalarGridSpec(
            num_scalar_prefetch=1,
            grid=(count,),
            in_specs=[pl.BlockSpec((rows, block), lambda j, at: (0, at[j])), whole((rows, columns))]
            + [pl.BlockSpec((rows // 2, block), lambda j, _: (0, first + j))] * 2
            + [whole((rows, columns))],
            out_specs=pl.BlockSpec(out, lambda j, _: (j, 0)),
            scratch_shapes=[pltpu.VMEM((rows, block), b16), pltpu.VMEM((rows, columns), b16)],
        ),
        out_shape=jax.ShapeDtypeStruct((count * out[0], out[1]), f32),
        compiler_params=vmem(),
        name="pair_grads",
    )(where, a, b, *few, wide)


def plain_pair_grads(where, first, a, b, few, wide, block, inward):
    far_a = (jnp.concatenate(few) * 0.5).astype(b16)
    far_b = (wide * 0.5).astype(b16)
    out = []
    for j, w in enumerate(where):
        near_a = lax.dynamic_slice_in_dim(a, w * block, block, 1)
        other = far_a[:, (first + j) * block : (first + j + 1) * block]
        if inward:
            out.append(dot_tn(near_a, b) + dot_tn(other, far_b))
        else:
            out.append(dot_tn(b, near_a) + dot_tn(far_b, other))
    return jnp.concatenate(out)


def tensor_masks():
    size = lax.axis_size("tensor")
    return [1 << i for i in range(1, size.bit_length() - 1)]


def scatter_sum(parts, masks):
    for mask in masks:
        half = len(parts) // 2
        received = [swap(p, "dp", mask) for p in parts[half:]]
        parts = [a + b for a, b in zip(parts[:half], received)]
    return parts[0]


def relative(masks):
    offsets = [0]
    for mask in reversed(masks):
        offsets = offsets + [o ^ mask for o in offsets]
    return offsets


def body(
    tokens,
    g_attn,
    w_query,
    w_key,
    w_value,
    q_gain,
    k_gain,
    w_out,
    g_mlp,
    w_gate,
    w_up,
    w_down,
    cotangent,
):
    rows, width = tokens.shape
    hd = q_gain.shape[0]
    cosine, sine = rope_tables(SEQ_LEN, hd)
    n_dp = lax.axis_size("dp")
    me = lax.axis_index("dp")
    core = lax.axis_index("tensor") % 2
    core_at = core.astype(jnp.int32).reshape(1)
    x_at = (lax.axis_index("tensor") // 2).astype(jnp.int32).reshape(1)
    half = rows // 2
    block = width // n_dp
    bits = [1 << i for i in range(n_dp.bit_length() - 1)]
    near, far = bits[0], bits[-1]
    middle = bits[1:-1]
    ga, gm, gq, gk = (g.reshape(1, -1) for g in (g_attn, g_mlp, q_gain, k_gain))
    seq = Sequence()

    def mine_of(a):
        return lax.dynamic_slice_in_dim(a, core * half, half, 0)

    def theirs_of(a):
        return lax.dynamic_slice_in_dim(a, (1 - core) * half, half, 0)

    def in_order(mine, theirs):
        out = jnp.zeros((rows,) + mine.shape[1:], mine.dtype)
        out = lax.dynamic_update_slice_in_dim(out, mine, core * half, 0)
        return lax.dynamic_update_slice_in_dim(out, theirs, (1 - core) * half, 0)

    def quarter_of(a):
        size = a.shape[0] // 2
        return lax.dynamic_slice_in_dim(a, (lax.axis_index("tensor") // 2) * size, size, 0)

    def one(value, count):
        return [value] if count == 1 else list(value)

    def pick(kernel, plain):
        return kernel if block % 128 == 0 else plain

    def at(offsets):
        return me ^ jnp.array(offsets, jnp.int32)

    def core_swap(a):
        return swap(a, "tensor", 1)

    def core_swaps(pieces):
        return [swap(a, "tensor", 1) for a in pieces]

    def x_swap(a):
        return swap(a, "tensor", 2)

    few = pick(few_of, plain_few_of)
    pair = pick(pair_grads, plain_pair_grads)
    rest = middle + [far]
    blocks = relative(rest)
    q = len(blocks) // 2
    rest_out = [near] + middle[1:] + [far]
    blocks_out = relative(rest_out)
    theirs_at, theirs_out = at([near ^ o for o in blocks]), at([middle[0] ^ o for o in blocks_out])

    cot_mine, cot_theirs = mine_of(cotangent), theirs_of(cotangent)
    cot_own = jnp.concatenate([cot_mine, cot_theirs])
    c0 = cot_mine.astype(f32) * 2.0
    c0, c0_quarter, tokens_then = seq(c0, quarter_of(c0), tokens)
    c1 = swap(c0, "dp", near)
    c2 = swap(c0_quarter, "dp", far)
    tok_mine = mine_of(tokens)
    normed1, query, keys, values, attended, att_wide, mixed_a, *mixed_b = seq(
        *attend(core_at, tokens_then, ga, w_query, w_key, w_value, gq, gk, w_out, cosine, sine)
    )
    mixed_got = seq(*core_swaps(mixed_b))
    mixed_chip, *mixed_split = seq(*sum_of(mixed_a, mixed_got, split=2))
    mixed_x = [x_swap(p) for p in mixed_split]
    near_n = swap(seq(few(theirs_at, tok_mine, ga, block, True)), "dp", near)
    c1, c2, near_n, *mixed_x = seq(c1, c2, near_n, *mixed_x)

    r_a, n0, n0_quarter, *r_split = seq(*resid_of(x_at, tok_mine, mixed_chip, *mixed_x))
    n1 = swap(n0, "dp", near)
    n2 = swap(n0_quarter, "dp", far)
    c2x = x_swap(c2)
    r_b = seq(*core_swaps(r_split))

    normed2, hidden, d_gate, d_up, dn_a, *dn_b, mlp_gain = seq(
        *pick(own_feed, plain_own_feed)(r_a, r_b, cot_own, gm, w_gate, w_up, w_down)
    )
    offsets = relative(middle)
    down_a, down_b, sums = pick(own_rest, plain_own_rest)(
        at(offsets), normed2, cot_own, hidden, d_gate, d_up, w_down, block
    )
    down_a, down_b, *both = seq(down_a, down_b, *sums, *dn_b)
    sums, dn_b = both[:-PIECES], both[-PIECES:]
    n2, c2x = seq(n2, c2x)
    n2x = x_swap(n2)
    n3 = swap(n2, "dp", near)
    n1, *dn_got = seq(n1, *core_swaps(dn_b))
    (dn_chip,) = sum_of(dn_a, dn_got)
    c2 = jnp.concatenate([c2, c2x])
    dn_chip, c2 = seq(dn_chip, c2)
    n1t, c1t = core_swaps((n1, c1))
    n1t, c1t, n2x, n3, dn_chip, c2 = seq(n1t, c1t, n2x, n3, dn_chip, c2)
    dn_x = x_swap(dn_chip)
    c3 = swap(c2, "dp", near)

    def add_group(ns, cs, sums):
        group = pick(group_feed, plain_group_feed)
        return list(seq(*group(at(offsets), ns, cs, gm, w_gate, w_up, w_down, sums, block)))

    n2t, c2t = core_swaps((n2, c2))
    sums = add_group([n1, n1t], [c1, c1t], sums)
    n2t, c2t = seq(n2t, c2t)
    n2xt = seq(core_swap(n2x))
    sums = add_group([n2, n2x, n2t, n2xt], [c2, c2t], sums)
    dn_x, c3, n3 = seq(dn_x, c3, n3)

    n3x = x_swap(n3)
    dn_mine, *dn_split = seq(*sum_of(dn_chip, [dn_x], split=PIECES))
    dn_theirs = seq(*core_swaps(dn_split))
    near_att = swap(att_wide, "dp", middle[0])
    c3t, n3t, down_got = core_swaps((c3, n3, down_b))
    dr_b, dr_mine, d_qkv, d_wide, d1_a, gain_a, gain_q, gain_k, *d1_b = seq(
        *attend_back(
            core_at, dn_mine, dn_theirs, r_a, r_b, cot_own, tokens, query, keys, values, attended,
            gm, ga, gq, gk, w_query, w_key, w_value, w_out, cosine, sine,
        )
    )
    near_r = few(theirs_out, dr_b, gm, block, False)
    near_r, n3x, c3t, n3t, near_att, down_got = seq(near_r, n3x, c3t, n3t, near_att, down_got)
    near_d = swap(d_wide, "dp", near)
    near_r = swap(near_r, "dp", middle[0])
    gains = jnp.concatenate([gain_a[0], gain_q[0], gain_k[0], mlp_gain[0]])
    gains_got = x_swap(gains)
    n3xt = seq(core_swap(n3x))
    sums = add_group([n3, n3x, n3t, n3xt], [c3, c3t], sums)
    k = len(offsets)
    h = k // 2
    lists = [sums[i * k : (i + 1) * k] for i in range(3)]
    keep = [p[:h] for p in lists]
    send = [p[h:] for p in lists]

    def first_step(parts):
        return [swap(p, "dp", middle[0]) for p in parts]

    def finish(keep, got):
        return scatter_sum([a + b for a, b in zip(keep, got)], middle[1:])

    got = first_step(send[0]) + first_step(send[1])
    near_r, gains_got, *d1_b = seq(near_r, gains_got, *d1_b)
    gains = gains + gains_got
    near_nt, gains_got, *d1_got = seq(*core_swaps((near_n, gains, *d1_b)))
    gains = gains + gains_got
    gains_got = swap(gains, "dp", near)
    (d1_chip,), (down_chip,) = sum_of(d1_a, d1_got), sum_of(down_a, [down_got])
    d1_chip, down_chip = seq(d1_chip, down_chip)
    d1_x = x_swap(d1_chip)
    def ins(i):
        return pair(at(blocks[i * q : (i + 1) * q]), i * q, normed1, d_qkv, near_ns, near_d, block, True)

    def outs(i):
        return pair(at(blocks_out[i * q : (i + 1) * q]), i * q, dr_b, attended, near_rs, near_att, block, False)

    near_rs = [near_r, seq(core_swap(near_r))]
    out_1 = seq(outs(1))
    out_mid = swap(out_1, "dp", rest_out[0])
    near_d, gains_got, near_nt = seq(near_d, gains_got, near_nt)
    gains = gains + gains_got
    near_ns = [near_n, near_nt]
    in_1, out_mid, down_chip, *got = seq(seq(ins(1)), out_mid, down_chip, *got)
    down_x = x_swap(down_chip)
    in_mid = swap(in_1, "dp", rest[0])
    gains_got = swap(gains, "dp", rest[0])
    in_0, out_0 = seq(ins(0), outs(0))
    summed_down = finish(keep[0], got[:h])
    summed_gate = finish(keep[1], got[h:])
    if len(rest) == 2:
        summed_down, summed_gate = seq(summed_down, summed_gate)

    def split(a):
        return list(a.reshape(q, a.shape[0] // q, a.shape[1]))

    d1_x = seq(d1_x)
    gt_mine, *gt_split = seq(*back_of(dr_mine, d1_chip, d1_x, tok_mine, ga))
    gt_theirs = jnp.concatenate(seq(*core_swaps(gt_split)))
    grad_tokens = seq(in_order(gt_mine, gt_theirs))
    in_mid, gains_got, down_x, *send_up = seq(in_mid, gains_got, down_x, *send[2])
    got_up = first_step(send_up)
    gains = gains + gains_got
    gains_got = swap(gains, "dp", far)
    both = seq(*split(in_0 + in_mid), *split(out_0 + out_mid))
    if len(rest) == 2:
        cut = both[3].shape[0] // 2
        last = swap(jnp.concatenate([both[1], both[3][:cut], both[3][cut:]], axis=1), "dp", far)
    else:
        summed_qkv, summed_out = scatter_sum(both[:q], rest[1:]), scatter_sum(both[q:], rest_out[1:])
    down_mine, *down_split = seq(*sum_of(down_chip, [down_x], split=PIECES))
    down_theirs = seq(*core_swaps(down_split))
    down_theirs, r_theirs = jnp.concatenate(down_theirs), jnp.concatenate(r_b)
    output = seq(in_order((r_a + down_mine).astype(b16), (r_theirs + down_theirs).astype(b16)))
    gains = gains + gains_got
    for mask in rest[1:-1]:
        gains = gains + swap(gains, "dp", mask)
    if len(rest) == 2:
        last, *got_up = seq(last, *got_up)
        columns = both[0].shape[1]
        summed_qkv = both[0] + last[:, :columns]
        end = jnp.concatenate([last[:, columns : columns + block], last[:, columns + block :]])
        summed_out = both[2] + end
    summed_up = finish(keep[2], got_up)
    nq, nk = w_query.shape[1], w_key.shape[1]
    gains = gains + 0.0 * seq.token.astype(f32)
    return (
        output,
        grad_tokens,
        gains[:width],
        summed_qkv[:, :nq],
        summed_qkv[:, nq : nq + nk],
        summed_qkv[:, nq + nk :],
        gains[width : width + hd],
        gains[width + hd : width + 2 * hd],
        summed_out,
        gains[width + 2 * hd :],
        summed_gate,
        summed_up,
        summed_down,
    )


def solution(mesh):
    in_specs = (
        P("dp", None),
        P(),
        P(None, "tensor"),
        P(None, "tensor"),
        P(None, "tensor"),
        P(),
        P(),
        P("tensor", None),
        P(),
        P(None, "tensor"),
        P(None, "tensor"),
        P("tensor", None),
        P("dp", None),
    )
    out_specs = (
        P("dp", None),
        P("dp", None),
        P(),
        P("dp", "tensor"),
        P("dp", "tensor"),
        P("dp", "tensor"),
        P(),
        P(),
        P("tensor", "dp"),
        P(),
        P("dp", "tensor"),
        P("dp", "tensor"),
        P("tensor", "dp"),
    )
    return jax.shard_map(body, mesh=mesh, in_specs=in_specs, out_specs=out_specs, check_vma=False)
```

```python
import functools

import jax
import jax.numpy as jnp
from jax import lax
from jax.experimental import pallas as pl
from jax.experimental.pallas import tpu as pltpu
from jax.sharding import PartitionSpec as P

SEQ_LEN = 256


EPS = 1e-06
THETA = 1000000.0

f32 = jnp.float32
b16 = jnp.bfloat16


def rms_norm(values, gain):
    inv_rms = lax.rsqrt(jnp.mean(values * values, axis=-1, keepdims=True) + EPS)
    unit_rows = values * inv_rms
    return (unit_rows * gain, unit_rows, inv_rms)


def rms_back(grads, gain, unit_rows, inv_rms):
    scaled = grads * gain
    return inv_rms * (scaled - unit_rows * jnp.mean(scaled * unit_rows, axis=-1, keepdims=True))


def swap(value, axis, mask):
    size = lax.axis_size(axis)
    return lax.ppermute(value, axis, [(i, i ^ mask) for i in range(size)])


class Sequence:
    def __init__(self):
        self.token = None

    def __call__(self, *values):
        if self.token is None:
            out = lax.optimization_barrier(values)
        else:
            *out, self.token = lax.optimization_barrier((*values, self.token))
        self.token = out[0].reshape(-1)[:1] if self.token is None else self.token
        return out[0] if len(out) == 1 else tuple(out)


def dot(a, b):
    return jnp.dot(a, b, preferred_element_type=f32)


def dot_nt(a, b):
    return lax.dot_general(a, b, (((1,), (1,)), ((), ())), preferred_element_type=f32)


def dot_tn(a, b):
    return lax.dot_general(a, b, (((0,), (0,)), ((), ())), preferred_element_type=f32)


TILE = 512
PIECES = 4


def vmem(mib=60):
    return pltpu.CompilerParams(vmem_limit_bytes=mib << 20)


def whole(shape):
    return pl.BlockSpec(shape, lambda *_: (0,) * len(shape))


def gated(nb, cb, wg_ref, wu_ref, wd_ref):
    gate_pre = dot(nb[...], wg_ref[...])
    up_pre = dot(nb[...], wu_ref[...])
    d_hidden = dot_nt(cb[...], wd_ref[...])
    sig = jax.nn.sigmoid(gate_pre)
    act = gate_pre * sig
    hidden = (act * up_pre).astype(b16)
    d_up = (d_hidden * act).astype(b16)
    d_gate = (d_hidden * up_pre * (sig * (1.0 + gate_pre * (1.0 - sig)))).astype(b16)
    return hidden, d_gate, d_up


def own_kernel(ra_ref, *refs):
    rb_refs, refs = refs[:PIECES], refs[PIECES:]
    cot_ref, g_ref, wg_ref, wu_ref, wd_ref, normed_ref, hid_ref, dg_ref, du_ref, dna_ref = refs[:10]
    dnb_refs, (gain_ref, rms_ref) = refs[10:-2], refs[-2:]
    step = pl.program_id(0)
    half = ra_ref.shape[0]
    part = half // PIECES

    @pl.when(step == 0)
    def _():
        for i, ref in enumerate((ra_ref, *rb_refs)):
            r = ref[...]
            at = 0 if i == 0 else half + (i - 1) * part
            inv = lax.rsqrt(jnp.mean(r * r, axis=-1, keepdims=True) + EPS)
            rms_ref[at : at + r.shape[0], :] = inv
            normed_ref[at : at + r.shape[0], :] = (r * inv * g_ref[...]).astype(b16)
        dna_ref[...] = jnp.zeros_like(dna_ref)
        for ref in dnb_refs:
            ref[...] = jnp.zeros_like(ref)

    hidden, d_gate, d_up = gated(normed_ref, cot_ref, wg_ref, wu_ref, wd_ref)
    hid_ref[...] = hidden
    dg_ref[...] = d_gate
    du_ref[...] = d_up
    dna_ref[...] += dot_nt(d_gate[:half], wg_ref[...]) + dot_nt(d_up[:half], wu_ref[...])
    far = dot_nt(d_gate[half:], wg_ref[...]) + dot_nt(d_up[half:], wu_ref[...])
    for i, ref in enumerate(dnb_refs):
        ref[...] += far[i * part : (i + 1) * part]

    @pl.when(step == pl.num_programs(0) - 1)
    def _():
        total = jnp.sum(dna_ref[...] * (ra_ref[...] * rms_ref[:half, :]), axis=0, keepdims=True)
        for i, (r_ref, d_ref) in enumerate(zip(rb_refs, dnb_refs)):
            at = half + i * part
            unit = r_ref[...] * rms_ref[at : at + part, :]
            total += jnp.sum(d_ref[...] * unit, axis=0, keepdims=True)
        gain_ref[...] = total


def own_feed(r_a, r_b, cot, g, w_gate, w_up, w_down):
    half, width = r_a.shape
    rows, hidden = 2 * half, w_gate.shape[1]
    col = pl.BlockSpec((rows, TILE), lambda i: (0, i))
    wide = jax.ShapeDtypeStruct((rows, hidden), b16)
    piece = (half // PIECES, width)
    return pl.pallas_call(
        own_kernel,
        grid=(hidden // TILE,),
        in_specs=[whole((half, width))]
        + [whole(piece)] * PIECES
        + [
            whole((rows, width)),
            whole((1, width)),
            pl.BlockSpec((width, TILE), lambda i: (0, i)),
            pl.BlockSpec((width, TILE), lambda i: (0, i)),
            pl.BlockSpec((TILE, width), lambda i: (i, 0)),
        ],
        out_specs=[
            whole((rows, width)),
            col,
            col,
            col,
            whole((half, width)),
        ]
        + [whole(piece)] * PIECES
        + [whole((1, width))],
        out_shape=[
            jax.ShapeDtypeStruct((rows, width), b16),
            wide,
            wide,
            wide,
            jax.ShapeDtypeStruct((half, width), f32),
        ]
        + [jax.ShapeDtypeStruct(piece, f32)] * PIECES
        + [jax.ShapeDtypeStruct((1, width), f32)],
        scratch_shapes=[pltpu.VMEM((rows, 1), f32)],
        compiler_params=vmem(),
        name="own_feed",
    )(r_a, *r_b, cot, g.reshape(1, -1), w_gate, w_up, w_down)


def put_columns(at_ref, cc_ref, nb_ref, cb_ref, where_ref, count, block):
    for j in range(count):
        here = pl.ds(pl.multiple_of(where_ref[j] * block, 128), block)
        at_ref[j * block : (j + 1) * block, :] = nb_ref[:, here].T
        cc_ref[:, j * block : (j + 1) * block] = cb_ref[:, here]


def put_grads(sums, at_ref, cc_ref, hidden, d_gate, d_up, block, before=None):
    down = dot_tn(hidden, cc_ref[...])
    gate = dot(at_ref[...], d_gate)
    up = dot(at_ref[...], d_up)
    count = len(sums) // 3
    for j in range(count):
        part = slice(j * block, (j + 1) * block)
        for k, fresh in ((j, down[:, part]), (count + j, gate[part]), (2 * count + j, up[part])):
            old = 0.0 if before is None else before[k][...]
            sums[k][...] = fresh + old


def rest_kernel(where_ref, nb_ref, cb_ref, hid_ref, dg_ref, du_ref, wd_ref, *rest):
    count = (len(rest) - 4) // 3
    ya_ref, yb_ref, *sums = rest[:-2]
    at_ref, cc_ref = rest[-2:]
    half = ya_ref.shape[0]
    block = cc_ref.shape[1] // count

    @pl.when(pl.program_id(0) == 0)
    def _():
        put_columns(at_ref, cc_ref, nb_ref, cb_ref, where_ref, count, block)
        ya_ref[...] = jnp.zeros_like(ya_ref)
        yb_ref[...] = jnp.zeros_like(yb_ref)

    hidden = hid_ref[...]
    ya_ref[...] += dot(hidden[:half], wd_ref[...])
    yb_ref[...] += dot(hidden[half:], wd_ref[...])
    put_grads(sums, at_ref, cc_ref, hidden, dg_ref[...], du_ref[...], block)


def sum_specs(count, block, hidden):
    specs = [pl.BlockSpec((TILE, block), lambda i, *_: (i, 0))] * count
    specs += [pl.BlockSpec((block, TILE), lambda i, *_: (0, i))] * (2 * count)
    shapes = [jax.ShapeDtypeStruct((hidden, block), f32)] * count
    shapes += [jax.ShapeDtypeStruct((block, hidden), f32)] * (2 * count)
    return specs, shapes


def own_rest(where, nb, cb, hidden, d_gate, d_up, w_down, block):
    rows, width = nb.shape
    count = where.shape[0]
    half, ff = rows // 2, hidden.shape[1]
    specs, shapes = sum_specs(count, block, ff)
    col = pl.BlockSpec((rows, TILE), lambda i, *_: (0, i))
    part = jax.ShapeDtypeStruct((half, width), f32)
    out = pl.pallas_call(
        rest_kernel,
        grid_spec=pltpu.PrefetchScalarGridSpec(
            num_scalar_prefetch=1,
            grid=(ff // TILE,),
            in_specs=[
                whole((rows, width)),
                whole((rows, width)),
                col,
                col,
                col,
                pl.BlockSpec((TILE, width), lambda i, *_: (i, 0)),
            ],
            out_specs=[whole((half, width)), whole((half, width))] + specs,
            scratch_shapes=[
                pltpu.VMEM((count * block, rows), b16),
                pltpu.VMEM((rows, count * block), b16),
            ],
        ),
        out_shape=[part, part] + shapes,
        compiler_params=vmem(),
        name="own_rest",
    )(where, nb, cb, hidden, d_gate, d_up, w_down)
    return out[0], out[1], list(out[2:])


def group_kernel(n_pieces, c_pieces, count, where_ref, *refs):
    n_refs, refs = refs[:n_pieces], refs[n_pieces:]
    c_refs, refs = refs[:c_pieces], refs[c_pieces:]
    g_ref, wg_ref, wu_ref, wd_ref = refs[:4]
    before = refs[4 : 4 + 3 * count]
    sums = refs[4 + 3 * count : 4 + 6 * count]
    nb_ref, cb_ref, at_ref, cc_ref = refs[4 + 6 * count :]
    block = cc_ref.shape[1] // count

    @pl.when(pl.program_id(0) == 0)
    def _():
        at = 0
        for n_ref in n_refs:
            size = n_ref.shape[0]
            nb_ref[at : at + size, :] = (n_ref[...] * g_ref[...]).astype(b16)
            at += size
        at = 0
        for c_ref in c_refs:
            size = c_ref.shape[0]
            cb_ref[at : at + size, :] = (c_ref[...] * 0.5).astype(b16)
            at += size
        put_columns(at_ref, cc_ref, nb_ref, cb_ref, where_ref, count, block)

    hidden, d_gate, d_up = gated(nb_ref, cb_ref, wg_ref, wu_ref, wd_ref)
    put_grads(sums, at_ref, cc_ref, hidden, d_gate, d_up, block, before)


def group_feed(where, ns, cs, g, w_gate, w_up, w_down, before, block):
    width, ff = w_gate.shape
    count = where.shape[0]
    rows = sum(n.shape[0] for n in ns)
    specs, shapes = sum_specs(count, block, ff)
    return list(
        pl.pallas_call(
            functools.partial(group_kernel, len(ns), len(cs), count),
            grid_spec=pltpu.PrefetchScalarGridSpec(
                num_scalar_prefetch=1,
                grid=(ff // TILE,),
                in_specs=[whole(a.shape) for a in (*ns, *cs)]
                + [
                    whole((1, width)),
                    pl.BlockSpec((width, TILE), lambda i, *_: (0, i)),
                    pl.BlockSpec((width, TILE), lambda i, *_: (0, i)),
                    pl.BlockSpec((TILE, width), lambda i, *_: (i, 0)),
                ]
                + specs,
                out_specs=specs,
                scratch_shapes=[
                    pltpu.VMEM((rows, width), b16),
                    pltpu.VMEM((rows, width), b16),
                    pltpu.VMEM((count * block, rows), b16),
                    pltpu.VMEM((rows, count * block), b16),
                ],
            ),
            out_shape=shapes,
            compiler_params=vmem(),
            name="group_feed",
        )(where, *ns, *cs, g.reshape(1, -1), w_gate, w_up, w_down, *before)
    )


def sum_kernel(count, *refs):
    a_ref, b_refs, outs = refs[0], refs[1 : 1 + count], refs[1 + count :]
    size = a_ref.shape[0] // count
    for i, b_ref in enumerate(b_refs):
        at = slice(i * size, (i + 1) * size)
        total = a_ref[at, :] + b_ref[...]
        outs[0][at, :] = total
    pieces = outs[1:]
    for i, piece in enumerate(pieces):
        piece[...] = outs[0][i * piece.shape[0] : (i + 1) * piece.shape[0], :]


def sum_of(a, bs, split=0):
    shapes = [jax.ShapeDtypeStruct(a.shape, f32)]
    shapes += [jax.ShapeDtypeStruct((a.shape[0] // max(split, 1), a.shape[1]), f32)] * split
    return pl.pallas_call(
        functools.partial(sum_kernel, len(bs)),
        in_specs=[whole(x.shape) for x in (a, *bs)],
        out_specs=[whole(x.shape) for x in shapes],
        out_shape=shapes,
        grid=(1,),
        compiler_params=vmem(),
        name="sum_of",
    )(a, *bs)


def resid_kernel(x_at_ref, tok_ref, a_ref, b_ref, c_ref, r_ref, n_ref, quarter_ref, *pieces):
    size = pieces[0].shape[0]
    for i, piece in enumerate(pieces):
        at = slice(i * size, (i + 1) * size)
        part, first = (b_ref, 0) if i < len(pieces) // 2 else (c_ref, len(pieces) // 2)
        far = part[(i - first) * size : (i - first + 1) * size, :]
        resid = tok_ref[at, :].astype(f32) + (a_ref[at, :] + far)
        r_ref[at, :] = resid
        piece[...] = resid
        n_ref[at, :] = resid * lax.rsqrt(jnp.mean(resid * resid, axis=-1, keepdims=True) + EPS)
    small = quarter_ref.shape[0]
    quarter_ref[...] = n_ref[pl.ds(pl.multiple_of(x_at_ref[0] * small, small), small), :]


def resid_of(x_at, tok, a, b, c):
    rows, width = a.shape
    shapes = [(rows, width), (rows, width), (rows // 2, width)] + [(rows // PIECES, width)] * PIECES
    return pl.pallas_call(
        resid_kernel,
        grid_spec=pltpu.PrefetchScalarGridSpec(
            num_scalar_prefetch=1,
            grid=(1,),
            in_specs=[whole(a.shape)] * 2 + [whole(b.shape)] * 2,
            out_specs=[whole(s) for s in shapes],
        ),
        out_shape=[jax.ShapeDtypeStruct(s, f32) for s in shapes],
        compiler_params=vmem(),
        name="resid_of",
    )(x_at, tok, a, b, c)


def feed(normed, cot, w_gate, w_up, w_down):
    gate_pre = dot(normed, w_gate)
    up_pre = dot(normed, w_up)
    d_hidden = dot_nt(cot, w_down)
    sigmoid_g = jax.nn.sigmoid(gate_pre)
    act_gate = gate_pre * sigmoid_g
    hidden = (act_gate * up_pre).astype(b16)
    d_up = (d_hidden * act_gate).astype(b16)
    d_gate = (d_hidden * up_pre * (sigmoid_g * (1.0 + gate_pre * (1.0 - sigmoid_g)))).astype(b16)
    return hidden, d_gate, d_up


def plain_grads(where, normed, cot, parts, block):
    hidden, d_gate, d_up = parts
    takes = [functools.partial(lax.dynamic_slice_in_dim, start_index=w * block, slice_size=block, axis=1) for w in where]
    pair = jnp.concatenate([d_gate, d_up], axis=1)
    both = [dot_tn(take(normed), pair) for take in takes]
    ff = hidden.shape[1]
    return [dot_tn(hidden, take(cot)) for take in takes] + [b[:, :ff] for b in both] + [b[:, ff:] for b in both]


def plain_own_feed(r_a, r_b, cot, g, w_gate, w_up, w_down):
    resid = jnp.concatenate([r_a, *r_b])
    normed, unit, _ = rms_norm(resid, g)
    normed = normed.astype(b16)
    parts = feed(normed, cot, w_gate, w_up, w_down)
    total = dot_nt(parts[1], w_gate) + dot_nt(parts[2], w_up)
    half = r_a.shape[0]
    gain = jnp.sum(total * unit, axis=0, keepdims=True)
    return (normed, *parts, total[:half], *jnp.split(total[half:], PIECES), gain)


def plain_own_rest(where, nb, cb, hidden, d_gate, d_up, w_down, block):
    down = dot(hidden, w_down)
    half = nb.shape[0] // 2
    return down[:half], down[half:], plain_grads(where, nb, cb, (hidden, d_gate, d_up), block)


def plain_group_feed(where, ns, cs, g, w_gate, w_up, w_down, before, block):
    normed = (jnp.concatenate(ns) * g).astype(b16)
    cot = (jnp.concatenate(cs) * 0.5).astype(b16)
    parts = feed(normed, cot, w_gate, w_up, w_down)
    return [old + new for old, new in zip(before, plain_grads(where, normed, cot, parts, block))]


def rope_tables(length, width):
    half = width // 2
    inverse = THETA ** (-(jnp.arange(half).astype(f32) * 2.0 / width))
    angles = jnp.arange(length).astype(f32)[:, None] * inverse[None, :]
    angles = jnp.concatenate([angles, angles], axis=1)
    sign = jnp.where(jnp.arange(width) < half, -1.0, 1.0).astype(f32)
    return jnp.cos(angles), jnp.sin(angles) * sign[None, :]


def turn(values, cosine, sine):
    return values * cosine + pltpu.roll(values, values.shape[-1] // 2, 1) * sine


def turn_back(grads, cosine, sine):
    return grads * cosine + pltpu.roll(grads * sine, grads.shape[-1] // 2, 1)


def norm_of(values):
    inv = lax.rsqrt(jnp.mean(values * values, axis=-1, keepdims=True) + EPS)
    return values * inv, inv


def norm_back(scaled, unit, inv):
    return inv * (scaled - unit * jnp.mean(scaled * unit, axis=-1, keepdims=True))


def softmax_of(q_rot, k_rot):
    length, width = q_rot.shape
    scores = dot_nt(q_rot, k_rot) * (width**-0.5)
    at = lax.broadcasted_iota(jnp.int32, (length, length), 0)
    to = lax.broadcasted_iota(jnp.int32, (length, length), 1)
    scores = jnp.where(at >= to, scores, -1e30)
    grown = jnp.exp(scores - jnp.max(scores, axis=-1, keepdims=True))
    return grown * (1.0 / jnp.sum(grown, axis=-1, keepdims=True))


def attend_kernel(half, core_ref, tok_ref, g_ref, wq_ref, wk_ref, wv_ref, qg_ref, kg_ref, wo_ref, cos_ref, sin_ref, *outs):
    n_ref, q_ref, k_ref, v_ref, att_ref, wide_ref, mine_ref = outs[:7]
    width = qg_ref.shape[1]
    cosine, sine = cos_ref[...], sin_ref[...]
    unit, _ = norm_of(tok_ref[...].astype(f32))
    normed = (unit * g_ref[...]).astype(b16)
    n_ref[...] = normed
    query = dot(normed, wq_ref[...])
    keys = dot(normed, wk_ref[...])
    values = dot(normed, wv_ref[...]).astype(b16)
    q_ref[...] = query
    k_ref[...] = keys
    v_ref[...] = values
    kv_heads = keys.shape[1] // width
    share = query.shape[1] // keys.shape[1]
    for kv in range(kv_heads):
        at = slice(kv * width, (kv + 1) * width)
        k_unit, _ = norm_of(keys[:, at])
        k_rot = turn(k_unit * kg_ref[...], cosine, sine).astype(b16)
        for h in range(kv * share, (kv + 1) * share):
            to = slice(h * width, (h + 1) * width)
            q_unit, _ = norm_of(query[:, to])
            q_rot = turn(q_unit * qg_ref[...], cosine, sine).astype(b16)
            probs = softmax_of(q_rot, k_rot).astype(b16)
            att_ref[:, to] = dot(probs, values[:, at]).astype(b16)
    wide_ref[...] = att_ref[...].astype(f32) * 2.0
    mixed = dot(att_ref[...], wo_ref[...])

    @pl.when(pl.program_id(0) < half)
    def _():
        for i, ref in enumerate(outs[7:]):
            ref[...] = mixed[i * ref.shape[0] : (i + 1) * ref.shape[0]]

    @pl.when(pl.program_id(0) >= half)
    def _():
        mine_ref[...] = mixed


def attend(core, tokens, g, wq, wk, wv, qg, kg, wo, cosine, sine):
    rows, width = tokens.shape
    seqs = rows // SEQ_LEN
    half = seqs // 2

    def source(i, core_ref):
        mine = core_ref[0]
        return (jnp.where(i < half, (1 - mine) * half + i, mine * half + i - half), 0)

    def place(i, _):
        return ((i + half) % seqs, 0)

    def out(columns, dtype):
        return pl.BlockSpec((SEQ_LEN, columns), place), jax.ShapeDtypeStruct((rows, columns), dtype)

    nq, nk = wq.shape[1], wk.shape[1]
    outs = [out(width, b16), out(nq, f32), out(nk, f32), out(nk, b16), out(nq, b16), out(nq, f32)]
    part = jax.ShapeDtypeStruct((rows // 2, width), f32)
    piece = SEQ_LEN // PIECES
    return pl.pallas_call(
        functools.partial(attend_kernel, half),
        grid_spec=pltpu.PrefetchScalarGridSpec(
            num_scalar_prefetch=1,
            grid=(seqs,),
            in_specs=[pl.BlockSpec((SEQ_LEN, width), source)]
            + [whole(a.shape) for a in (g, wq, wk, wv, qg, kg, wo, cosine, sine)],
            out_specs=[o[0] for o in outs]
            + [
                pl.BlockSpec((SEQ_LEN, width), lambda i, _: (jnp.maximum(i - half, 0), 0)),
            ]
            + [pl.BlockSpec((piece, width), lambda i, _: (jnp.minimum(i, half - 1), 0))] * PIECES,
        ),
        out_shape=[o[1] for o in outs]
        + [part]
        + [jax.ShapeDtypeStruct((piece * half, width), f32)] * PIECES,
        compiler_params=vmem(),
        name="attend",
    )(core, tokens, g, wq, wk, wv, qg, kg, wo, cosine, sine)


def attend_back_kernel(half, core_ref, *refs):
    dnb_refs, rb_refs, refs = refs[:PIECES], refs[PIECES : 2 * PIECES], refs[2 * PIECES :]
    ins, outs = refs[:18], refs[18:]
    dna_ref, ra_ref, cot_ref, tok_ref, q_ref, k_ref, v_ref, att_ref = ins[:8]
    gm_ref, ga_ref, qg_ref, kg_ref, wq_ref, wk_ref, wv_ref, wo_ref, cos_ref, sin_ref = ins[8:]
    dr_ref, drm_ref, dqkv_ref, wide_ref, d1a_ref, ga_out, gq_out, gk_out = outs[:8]
    d1b_refs, (r_ref, dn_ref) = outs[8:-2], outs[-2:]
    step = pl.program_id(0)
    width = qg_ref.shape[1]
    cosine, sine = cos_ref[...], sin_ref[...]

    @pl.when(step == 0)
    def _():
        ga_out[...] = jnp.zeros_like(ga_out)
        gq_out[...] = jnp.zeros_like(gq_out)
        gk_out[...] = jnp.zeros_like(gk_out)

    mine = step < half

    @pl.when(mine)
    def _():
        r_ref[...] = ra_ref[...]
        dn_ref[...] = dna_ref[...]

    @pl.when(step >= half)
    def _():
        for i, (r_piece, dn_piece) in enumerate(zip(rb_refs, dnb_refs)):
            at = slice(i * r_piece.shape[0], (i + 1) * r_piece.shape[0])
            r_ref[at, :] = r_piece[...]
            dn_ref[at, :] = dn_piece[...]

    unit2, inv2 = norm_of(r_ref[...])
    scaled = dn_ref[...] * gm_ref[...]
    d_resid = cot_ref[...].astype(f32) + norm_back(scaled, unit2, inv2)
    d_resid_b = d_resid.astype(b16)
    dr_ref[...] = d_resid_b

    @pl.when(mine)
    def _():
        drm_ref[...] = d_resid

    d_att = dot_nt(d_resid_b, wo_ref[...]).astype(b16)
    nq, nk = q_ref.shape[1], k_ref.shape[1]
    share = nq // nk
    for kv in range(nk // width):
        at = slice(kv * width, (kv + 1) * width)
        k_unit, k_inv = norm_of(k_ref[:, at])
        k_rot = turn(k_unit * kg_ref[...], cosine, sine).astype(b16)
        values = v_ref[:, at]
        d_krot = d_values = 0.0
        for h in range(kv * share, (kv + 1) * share):
            to = slice(h * width, (h + 1) * width)
            q_unit, q_inv = norm_of(q_ref[:, to])
            q_rot = turn(q_unit * qg_ref[...], cosine, sine).astype(b16)
            probs = softmax_of(q_rot, k_rot)
            d_head = d_att[:, to]
            d_prob = dot_nt(d_head, values)
            delta = jnp.sum(d_head.astype(f32) * att_ref[:, to].astype(f32), axis=-1, keepdims=True)
            d_score = (probs * (d_prob - delta) * (width**-0.5)).astype(b16)
            d_krot += dot_tn(d_score, q_rot)
            d_values += dot_tn(probs.astype(b16), d_head)
            d_qn = turn_back(dot(d_score, k_rot), cosine, sine)
            gq_out[...] += jnp.sum(d_qn * q_unit, axis=0, keepdims=True)
            dqkv_ref[:, to] = norm_back(d_qn * qg_ref[...], q_unit, q_inv).astype(b16)
        d_kn = turn_back(d_krot, cosine, sine)
        gk_out[...] += jnp.sum(d_kn * k_unit, axis=0, keepdims=True)
        here = slice(nq + kv * width, nq + (kv + 1) * width)
        dqkv_ref[:, here] = norm_back(d_kn * kg_ref[...], k_unit, k_inv).astype(b16)
        here = slice(nq + nk + kv * width, nq + nk + (kv + 1) * width)
        dqkv_ref[:, here] = d_values.astype(b16)
    wide_ref[...] = dqkv_ref[...].astype(f32) * 2.0
    d_norm1 = (
        dot_nt(dqkv_ref[:, :nq], wq_ref[...])
        + dot_nt(dqkv_ref[:, nq : nq + nk], wk_ref[...])
        + dot_nt(dqkv_ref[:, nq + nk :], wv_ref[...])
    )
    unit1, _ = norm_of(tok_ref[...].astype(f32))
    ga_out[...] += jnp.sum(d_norm1 * unit1, axis=0, keepdims=True)

    @pl.when(mine)
    def _():
        d1a_ref[...] = d_norm1

    @pl.when(step >= half)
    def _():
        for i, ref in enumerate(d1b_refs):
            ref[...] = d_norm1[i * ref.shape[0] : (i + 1) * ref.shape[0]]


def attend_back(core, dn_a, dn_b, r_a, r_b, cot, tokens, q, k, v, att, gm, ga, qg, kg, wq, wk, wv, wo, cosine, sine):
    rows, width = tokens.shape
    seqs = rows // SEQ_LEN
    half = seqs // 2

    def source(i, core_ref):
        mine = core_ref[0]
        return (jnp.where(i < half, mine * half + i, (1 - mine) * half + i - half), 0)

    def low(i, _):
        return (jnp.minimum(i, half - 1), 0)

    def high(i, _):
        return (jnp.maximum(i - half, 0), 0)

    def same(i, _):
        return (i, 0)

    def block(columns, place):
        return pl.BlockSpec((SEQ_LEN, columns), place)

    nq, nk = wq.shape[1], wk.shape[1]
    part = jax.ShapeDtypeStruct((rows // 2, width), f32)
    consts = (gm, ga, qg, kg, wq, wk, wv, wo, cosine, sine)
    small = [(1, width), qg.shape, kg.shape]
    piece = SEQ_LEN // PIECES
    return pl.pallas_call(
        functools.partial(attend_back_kernel, half),
        grid_spec=pltpu.PrefetchScalarGridSpec(
            num_scalar_prefetch=1,
            grid=(seqs,),
            in_specs=[
                pl.BlockSpec((piece, width), high),
            ]
            * (2 * PIECES)
            + [
                block(width, low),
                block(width, low),
                block(width, same),
                block(width, source),
                block(nq, same),
                block(nk, same),
                block(nk, same),
                block(nq, same),
            ]
            + [whole(a.shape) for a in consts],
            out_specs=[
                block(width, same),
                block(width, low),
                block(nq + 2 * nk, same),
                block(nq + 2 * nk, same),
                block(width, low),
            ]
            + [whole(s) for s in small]
            + [pl.BlockSpec((piece, width), high)] * PIECES,
            scratch_shapes=[pltpu.VMEM((SEQ_LEN, width), f32)] * 2,
        ),
        out_shape=[
            jax.ShapeDtypeStruct((rows, width), b16),
            part,
            jax.ShapeDtypeStruct((rows, nq + 2 * nk), b16),
            jax.ShapeDtypeStruct((rows, nq + 2 * nk), f32),
            part,
        ]
        + [jax.ShapeDtypeStruct(s, f32) for s in small]
        + [jax.ShapeDtypeStruct((piece * half, width), f32)] * PIECES,
        compiler_params=vmem(),
        name="attend_back",
    )(core, *dn_b, *r_b, dn_a, r_a, cot, tokens, q, k, v, att, *consts)


def back_kernel(dr_ref, a_ref, b_ref, tok_ref, g_ref, out_ref, *pieces):
    size = pieces[0].shape[0]
    for i, piece in enumerate(pieces):
        at = slice(i * size, (i + 1) * size)
        unit, inv = norm_of(tok_ref[at, :].astype(f32))
        grads = dr_ref[at, :] + norm_back((a_ref[at, :] + b_ref[at, :]) * g_ref[...], unit, inv)
        out_ref[at, :] = grads
        piece[...] = grads


def back_of(dr, a, b, tok, g):
    rows, width = a.shape
    shapes = [(rows, width)] + [(rows // PIECES, width)] * PIECES
    return pl.pallas_call(
        back_kernel,
        grid=(1,),
        in_specs=[whole(x.shape) for x in (dr, a, b, tok, g)],
        out_specs=[whole(x) for x in shapes],
        out_shape=[jax.ShapeDtypeStruct(x, f32) for x in shapes],
        compiler_params=vmem(),
        name="back_of",
    )(dr, a, b, tok, g)


def few_kernel(normed, where_ref, a_ref, g_ref, out_ref, row_ref):
    block = out_ref.shape[1] // where_ref.shape[0]
    here = a_ref[...].astype(f32)
    if normed:
        here = (norm_of(here)[0] * g_ref[...]).astype(b16).astype(f32)
    row_ref[...] = here
    for j in range(where_ref.shape[0]):
        at = pl.ds(pl.multiple_of(where_ref[j] * block, 128), block)
        out_ref[:, j * block : (j + 1) * block] = row_ref[:, at]


def few_of(where, a, g, block, normed):
    half, width = a.shape[0] if normed else a.shape[0] // 2, a.shape[1]
    out = (half, where.shape[0] * block)
    return pl.pallas_call(
        functools.partial(few_kernel, normed),
        grid_spec=pltpu.PrefetchScalarGridSpec(
            num_scalar_prefetch=1,
            grid=(1,),
            in_specs=[whole((half, width)), whole(g.shape)],
            out_specs=whole(out),
            scratch_shapes=[pltpu.VMEM((half, width), f32)],
        ),
        out_shape=jax.ShapeDtypeStruct(out, f32),
        compiler_params=vmem(),
        name="few_of",
    )(where, a, g)


def plain_few_of(where, a, g, block, normed):
    half = a.shape[0] if normed else a.shape[0] // 2
    here = a[:half].astype(f32)
    if normed:
        here = rms_norm(here, g)[0].astype(b16).astype(f32)
    return jnp.concatenate([lax.dynamic_slice_in_dim(here, w * block, block, 1) for w in where], axis=1) * 2.0


def pair_kernel(inward, where_ref, a_ref, b_ref, few_a_ref, few_b_ref, wide_ref, out_ref, far_a_ref, far_b_ref):
    half = few_a_ref.shape[0]

    @pl.when(pl.program_id(0) == 0)
    def _():
        far_b_ref[...] = (wide_ref[...] * 0.5).astype(b16)

    far_a_ref[:half, :] = few_a_ref[...].astype(b16)
    far_a_ref[half:, :] = few_b_ref[...].astype(b16)
    if inward:
        out_ref[...] = dot_tn(a_ref[...], b_ref[...]) + dot_tn(far_a_ref[...], far_b_ref[...])
    else:
        out_ref[...] = dot_tn(b_ref[...], a_ref[...]) + dot_tn(far_b_ref[...], far_a_ref[...])


def pair_grads(where, first, a, b, few, wide, block, inward):
    rows, columns, count = a.shape[0], b.shape[1], where.shape[0]
    out = (block, columns) if inward else (columns, block)
    return pl.pallas_call(
        functools.partial(pair_kernel, inward),
        grid_spec=pltpu.PrefetchScalarGridSpec(
            num_scalar_prefetch=1,
            grid=(count,),
            in_specs=[pl.BlockSpec((rows, block), lambda j, at: (0, at[j])), whole((rows, columns))]
            + [pl.BlockSpec((rows // 2, block), lambda j, _: (0, first + j))] * 2
            + [whole((rows, columns))],
            out_specs=pl.BlockSpec(out, lambda j, _: (j, 0)),
            scratch_shapes=[pltpu.VMEM((rows, block), b16), pltpu.VMEM((rows, columns), b16)],
        ),
        out_shape=jax.ShapeDtypeStruct((count * out[0], out[1]), f32),
        compiler_params=vmem(),
        name="pair_grads",
    )(where, a, b, *few, wide)


def plain_pair_grads(where, first, a, b, few, wide, block, inward):
    far_a = (jnp.concatenate(few) * 0.5).astype(b16)
    far_b = (wide * 0.5).astype(b16)
    out = []
    for j, w in enumerate(where):
        near_a = lax.dynamic_slice_in_dim(a, w * block, block, 1)
        other = far_a[:, (first + j) * block : (first + j + 1) * block]
        if inward:
            out.append(dot_tn(near_a, b) + dot_tn(other, far_b))
        else:
            out.append(dot_tn(b, near_a) + dot_tn(far_b, other))
    return jnp.concatenate(out)


def tensor_masks():
    size = lax.axis_size("tensor")
    return [1 << i for i in range(1, size.bit_length() - 1)]


def scatter_sum(parts, masks):
    for mask in masks:
        half = len(parts) // 2
        received = [swap(p, "dp", mask) for p in parts[half:]]
        parts = [a + b for a, b in zip(parts[:half], received)]
    return parts[0]


def relative(masks):
    offsets = [0]
    for mask in reversed(masks):
        offsets = offsets + [o ^ mask for o in offsets]
    return offsets


def body(
    tokens,
    g_attn,
    w_query,
    w_key,
    w_value,
    q_gain,
    k_gain,
    w_out,
    g_mlp,
    w_gate,
    w_up,
    w_down,
    cotangent,
):
    rows, width = tokens.shape
    hd = q_gain.shape[0]
    cosine, sine = rope_tables(SEQ_LEN, hd)
    n_dp = lax.axis_size("dp")
    me = lax.axis_index("dp")
    core = lax.axis_index("tensor") % 2
    core_at = core.astype(jnp.int32).reshape(1)
    x_at = (lax.axis_index("tensor") // 2).astype(jnp.int32).reshape(1)
    half = rows // 2
    block = width // n_dp
    bits = [1 << i for i in range(n_dp.bit_length() - 1)]
    near, far = bits[0], bits[-1]
    middle = bits[1:-1]
    ga, gm, gq, gk = (g.reshape(1, -1) for g in (g_attn, g_mlp, q_gain, k_gain))
    seq = Sequence()

    def mine_of(a):
        return lax.dynamic_slice_in_dim(a, core * half, half, 0)

    def theirs_of(a):
        return lax.dynamic_slice_in_dim(a, (1 - core) * half, half, 0)

    def in_order(mine, theirs):
        out = jnp.zeros((rows,) + mine.shape[1:], mine.dtype)
        out = lax.dynamic_update_slice_in_dim(out, mine, core * half, 0)
        return lax.dynamic_update_slice_in_dim(out, theirs, (1 - core) * half, 0)

    def quarter_of(a):
        size = a.shape[0] // 2
        return lax.dynamic_slice_in_dim(a, (lax.axis_index("tensor") // 2) * size, size, 0)

    def one(value, count):
        return [value] if count == 1 else list(value)

    def pick(kernel, plain):
        return kernel if block % 128 == 0 else plain

    def at(offsets):
        return me ^ jnp.array(offsets, jnp.int32)

    def core_swap(a):
        return swap(a, "tensor", 1)

    def core_swaps(pieces):
        return [swap(a, "tensor", 1) for a in pieces]

    def x_swap(a):
        return swap(a, "tensor", 2)

    few = pick(few_of, plain_few_of)
    pair = pick(pair_grads, plain_pair_grads)
    rest = middle + [far]
    blocks = relative(rest)
    q = len(blocks) // 2
    rest_out = [near] + middle[1:] + [far]
    blocks_out = relative(rest_out)
    theirs_at, theirs_out = at([near ^ o for o in blocks]), at([middle[0] ^ o for o in blocks_out])

    cot_mine, cot_theirs = mine_of(cotangent), theirs_of(cotangent)
    cot_own = jnp.concatenate([cot_mine, cot_theirs])
    c0 = cot_mine.astype(f32) * 2.0
    c0, c0_quarter, tokens_then = seq(c0, quarter_of(c0), tokens)
    c1 = swap(c0, "dp", near)
    c2 = swap(c0_quarter, "dp", far)
    tok_mine = mine_of(tokens)
    normed1, query, keys, values, attended, att_wide, mixed_a, *mixed_b = seq(
        *attend(core_at, tokens_then, ga, w_query, w_key, w_value, gq, gk, w_out, cosine, sine)
    )
    mixed_got = seq(*core_swaps(mixed_b))
    mixed_chip, *mixed_split = seq(*sum_of(mixed_a, mixed_got, split=2))
    mixed_x = [x_swap(p) for p in mixed_split]
    c1, c2, *mixed_x = seq(c1, c2, *mixed_x)

    r_a, n0, n0_quarter, *r_split = seq(*resid_of(x_at, tok_mine, mixed_chip, *mixed_x))
    n1 = swap(n0, "dp", near)
    n2 = swap(n0_quarter, "dp", far)
    c2x = x_swap(c2)
    r_b = seq(*core_swaps(r_split))

    normed2, hidden, d_gate, d_up, dn_a, *dn_b, mlp_gain = seq(
        *pick(own_feed, plain_own_feed)(r_a, r_b, cot_own, gm, w_gate, w_up, w_down)
    )
    offsets = relative(middle)
    down_a, down_b, sums = pick(own_rest, plain_own_rest)(
        at(offsets), normed2, cot_own, hidden, d_gate, d_up, w_down, block
    )
    down_a, down_b, *both = seq(down_a, down_b, *sums, *dn_b)
    sums, dn_b = both[:-PIECES], both[-PIECES:]
    n2, c2x = seq(n2, c2x)
    n2x = x_swap(n2)
    n3 = swap(n2, "dp", near)
    n1, *dn_got = seq(n1, *core_swaps(dn_b))
    (dn_chip,) = sum_of(dn_a, dn_got)
    c2 = jnp.concatenate([c2, c2x])
    dn_chip, c2 = seq(dn_chip, c2)
    near_n = few(theirs_at, seq(tok_mine), ga, block, True)
    n1t, c1t, down_got = core_swaps((n1, c1, down_b))
    n1t, c1t, down_got, n2x, n3, dn_chip, c2, near_n = seq(n1t, c1t, down_got, n2x, n3, dn_chip, c2, near_n)
    dn_x = x_swap(dn_chip)
    c3 = swap(c2, "dp", near)

    def add_group(ns, cs, sums):
        group = pick(group_feed, plain_group_feed)
        return list(seq(*group(at(offsets), ns, cs, gm, w_gate, w_up, w_down, sums, block)))

    n2t, c2t = core_swaps((n2, c2))
    sums = add_group([n1, n1t], [c1, c1t], sums)
    n2t, c2t = seq(n2t, c2t)
    n2xt = seq(core_swap(n2x))
    sums = add_group([n2, n2x, n2t, n2xt], [c2, c2t], sums)
    dn_x, c3, n3 = seq(dn_x, c3, n3)

    n3x = x_swap(n3)
    dn_mine, *dn_split = seq(*sum_of(dn_chip, [dn_x], split=PIECES))
    *dn_theirs, c3, n3, near_n, att_wide = seq(*core_swaps(dn_split), c3, n3, near_n, att_wide)
    near_n = swap(near_n, "dp", near)
    near_att = swap(att_wide, "dp", middle[0])
    c3t, n3t = core_swaps((c3, n3))
    dr_b, dr_mine, d_qkv, d_wide, d1_a, gain_a, gain_q, gain_k, *d1_b = seq(
        *attend_back(
            core_at, dn_mine, dn_theirs, r_a, r_b, cot_own, tokens, query, keys, values, attended,
            gm, ga, gq, gk, w_query, w_key, w_value, w_out, cosine, sine,
        )
    )
    near_r = few(theirs_out, dr_b, gm, block, False)
    near_r, n3x, c3t, n3t, near_att, near_n = seq(near_r, n3x, c3t, n3t, near_att, near_n)
    near_d = swap(d_wide, "dp", near)
    near_r = swap(near_r, "dp", middle[0])
    gains = jnp.concatenate([gain_a[0], gain_q[0], gain_k[0], mlp_gain[0]])
    gains_got = x_swap(gains)
    n3xt = seq(core_swap(n3x))
    sums = add_group([n3, n3x, n3t, n3xt], [c3, c3t], sums)
    k = len(offsets)
    h = k // 2
    lists = [sums[i * k : (i + 1) * k] for i in range(3)]
    keep = [p[:h] for p in lists]
    send = [p[h:] for p in lists]

    def first_step(parts):
        return [swap(p, "dp", middle[0]) for p in parts]

    def finish(keep, got):
        return scatter_sum([a + b for a, b in zip(keep, got)], middle[1:])

    got = first_step(send[0]) + first_step(send[1])
    near_r, gains_got, *d1_b = seq(near_r, gains_got, *d1_b)
    gains = gains + gains_got
    near_nt, gains_got, *d1_got = seq(*core_swaps((near_n, gains, *d1_b)))
    gains = gains + gains_got
    gains_got = swap(gains, "dp", near)
    (d1_chip,), (down_chip,) = sum_of(d1_a, d1_got), sum_of(down_a, [down_got])
    d1_chip, down_chip = seq(d1_chip, down_chip)
    d1_x = x_swap(d1_chip)
    def ins(i):
        return pair(at(blocks[i * q : (i + 1) * q]), i * q, normed1, d_qkv, near_ns, near_d, block, True)

    def outs(i):
        return pair(at(blocks_out[i * q : (i + 1) * q]), i * q, dr_b, attended, near_rs, near_att, block, False)

    near_rs = [near_r, seq(core_swap(near_r))]
    out_1 = seq(outs(1))
    out_mid = swap(out_1, "dp", rest_out[0])
    near_d, gains_got, near_nt = seq(near_d, gains_got, near_nt)
    gains = gains + gains_got
    near_ns = [near_n, near_nt]
    in_1, out_mid, down_chip, *got = seq(seq(ins(1)), out_mid, down_chip, *got)
    down_x = x_swap(down_chip)
    in_mid = swap(in_1, "dp", rest[0])
    gains_got = swap(gains, "dp", rest[0])
    in_0, out_0 = seq(ins(0), outs(0))
    summed_down = finish(keep[0], got[:h])
    summed_gate = finish(keep[1], got[h:])
    if len(rest) == 2:
        summed_down, summed_gate = seq(summed_down, summed_gate)

    def split(a):
        return list(a.reshape(q, a.shape[0] // q, a.shape[1]))

    d1_x = seq(d1_x)
    gt_mine, *gt_split = seq(*back_of(dr_mine, d1_chip, d1_x, tok_mine, ga))
    gt_theirs = jnp.concatenate(seq(*core_swaps(gt_split)))
    grad_tokens = seq(in_order(gt_mine, gt_theirs))
    in_mid, gains_got, down_x, *send_up = seq(in_mid, gains_got, down_x, *send[2])
    got_up = first_step(send_up)
    gains = gains + gains_got
    gains_got = swap(gains, "dp", far)
    both = seq(*split(in_0 + in_mid), *split(out_0 + out_mid))
    if len(rest) == 2:
        cut = both[3].shape[0] // 2
        last = swap(jnp.concatenate([both[1], both[3][:cut], both[3][cut:]], axis=1), "dp", far)
    else:
        summed_qkv, summed_out = scatter_sum(both[:q], rest[1:]), scatter_sum(both[q:], rest_out[1:])
    down_mine, *down_split = seq(*sum_of(down_chip, [down_x], split=PIECES))
    down_theirs = seq(*core_swaps(down_split))
    down_theirs, r_theirs = jnp.concatenate(down_theirs), jnp.concatenate(r_b)
    output = seq(in_order((r_a + down_mine).astype(b16), (r_theirs + down_theirs).astype(b16)))
    gains = gains + gains_got
    for mask in rest[1:-1]:
        gains = gains + swap(gains, "dp", mask)
    if len(rest) == 2:
        last, *got_up = seq(last, *got_up)
        columns = both[0].shape[1]
        summed_qkv = both[0] + last[:, :columns]
        end = jnp.concatenate([last[:, columns : columns + block], last[:, columns + block :]])
        summed_out = both[2] + end
    summed_up = finish(keep[2], got_up)
    nq, nk = w_query.shape[1], w_key.shape[1]
    gains = gains + 0.0 * seq.token.astype(f32)
    return (
        output,
        grad_tokens,
        gains[:width],
        summed_qkv[:, :nq],
        summed_qkv[:, nq : nq + nk],
        summed_qkv[:, nq + nk :],
        gains[width : width + hd],
        gains[width + hd : width + 2 * hd],
        summed_out,
        gains[width + 2 * hd :],
        summed_gate,
        summed_up,
        summed_down,
    )


def solution(mesh):
    in_specs = (
        P("dp", None),
        P(),
        P(None, "tensor"),
        P(None, "tensor"),
        P(None, "tensor"),
        P(),
        P(),
        P("tensor", None),
        P(),
        P(None, "tensor"),
        P(None, "tensor"),
        P("tensor", None),
        P("dp", None),
    )
    out_specs = (
        P("dp", None),
        P("dp", None),
        P(),
        P("dp", "tensor"),
        P("dp", "tensor"),
        P("dp", "tensor"),
        P(),
        P(),
        P("tensor", "dp"),
        P(),
        P("dp", "tensor"),
        P("dp", "tensor"),
        P("tensor", "dp"),
    )
    return jax.shard_map(body, mesh=mesh, in_specs=in_specs, out_specs=out_specs, check_vma=False)
```

```python
import functools

import jax
import jax.numpy as jnp
from jax import lax
from jax.experimental import pallas as pl
from jax.experimental.pallas import tpu as pltpu
from jax.sharding import PartitionSpec as P

SEQ_LEN = 256


EPS = 1e-06
THETA = 1000000.0

f32 = jnp.float32
b16 = jnp.bfloat16


def rms_norm(values, gain):
    inv_rms = lax.rsqrt(jnp.mean(values * values, axis=-1, keepdims=True) + EPS)
    unit_rows = values * inv_rms
    return (unit_rows * gain, unit_rows, inv_rms)


def rms_back(grads, gain, unit_rows, inv_rms):
    scaled = grads * gain
    return inv_rms * (scaled - unit_rows * jnp.mean(scaled * unit_rows, axis=-1, keepdims=True))


def swap(value, axis, mask):
    size = lax.axis_size(axis)
    return lax.ppermute(value, axis, [(i, i ^ mask) for i in range(size)])


class Sequence:
    def __init__(self):
        self.token = None

    def __call__(self, *values):
        if self.token is None:
            out = lax.optimization_barrier(values)
        else:
            *out, self.token = lax.optimization_barrier((*values, self.token))
        self.token = out[0].reshape(-1)[:1] if self.token is None else self.token
        return out[0] if len(out) == 1 else tuple(out)


def dot(a, b):
    return jnp.dot(a, b, preferred_element_type=f32)


def dot_nt(a, b):
    return lax.dot_general(a, b, (((1,), (1,)), ((), ())), preferred_element_type=f32)


def dot_tn(a, b):
    return lax.dot_general(a, b, (((0,), (0,)), ((), ())), preferred_element_type=f32)


TILE = 512
PIECES = 4


def vmem(mib=60):
    return pltpu.CompilerParams(vmem_limit_bytes=mib << 20)


def whole(shape):
    return pl.BlockSpec(shape, lambda *_: (0,) * len(shape))


def gated(nb, cb, wg_ref, wu_ref, wd_ref):
    gate_pre = dot(nb[...], wg_ref[...])
    up_pre = dot(nb[...], wu_ref[...])
    d_hidden = dot_nt(cb[...], wd_ref[...])
    sig = jax.nn.sigmoid(gate_pre)
    act = gate_pre * sig
    hidden = (act * up_pre).astype(b16)
    d_up = (d_hidden * act).astype(b16)
    d_gate = (d_hidden * up_pre * (sig * (1.0 + gate_pre * (1.0 - sig)))).astype(b16)
    return hidden, d_gate, d_up


def own_kernel(ra_ref, *refs):
    rb_refs, refs = refs[:PIECES], refs[PIECES:]
    cot_ref, g_ref, wg_ref, wu_ref, wd_ref, normed_ref, hid_ref, dg_ref, du_ref, dna_ref = refs[:10]
    dnb_refs, (gain_ref, rms_ref) = refs[10:-2], refs[-2:]
    step = pl.program_id(0)
    half = ra_ref.shape[0]
    part = half // PIECES

    @pl.when(step == 0)
    def _():
        for i, ref in enumerate((ra_ref, *rb_refs)):
            r = ref[...]
            at = 0 if i == 0 else half + (i - 1) * part
            inv = lax.rsqrt(jnp.mean(r * r, axis=-1, keepdims=True) + EPS)
            rms_ref[at : at + r.shape[0], :] = inv
            normed_ref[at : at + r.shape[0], :] = (r * inv * g_ref[...]).astype(b16)
        dna_ref[...] = jnp.zeros_like(dna_ref)
        for ref in dnb_refs:
            ref[...] = jnp.zeros_like(ref)

    hidden, d_gate, d_up = gated(normed_ref, cot_ref, wg_ref, wu_ref, wd_ref)
    hid_ref[...] = hidden
    dg_ref[...] = d_gate
    du_ref[...] = d_up
    dna_ref[...] += dot_nt(d_gate[:half], wg_ref[...]) + dot_nt(d_up[:half], wu_ref[...])
    far = dot_nt(d_gate[half:], wg_ref[...]) + dot_nt(d_up[half:], wu_ref[...])
    for i, ref in enumerate(dnb_refs):
        ref[...] += far[i * part : (i + 1) * part]

    @pl.when(step == pl.num_programs(0) - 1)
    def _():
        total = jnp.sum(dna_ref[...] * (ra_ref[...] * rms_ref[:half, :]), axis=0, keepdims=True)
        for i, (r_ref, d_ref) in enumerate(zip(rb_refs, dnb_refs)):
            at = half + i * part
            unit = r_ref[...] * rms_ref[at : at + part, :]
            total += jnp.sum(d_ref[...] * unit, axis=0, keepdims=True)
        gain_ref[...] = total


def own_feed(r_a, r_b, cot, g, w_gate, w_up, w_down):
    half, width = r_a.shape
    rows, hidden = 2 * half, w_gate.shape[1]
    col = pl.BlockSpec((rows, TILE), lambda i: (0, i))
    wide = jax.ShapeDtypeStruct((rows, hidden), b16)
    piece = (half // PIECES, width)
    return pl.pallas_call(
        own_kernel,
        grid=(hidden // TILE,),
        in_specs=[whole((half, width))]
        + [whole(piece)] * PIECES
        + [
            whole((rows, width)),
            whole((1, width)),
            pl.BlockSpec((width, TILE), lambda i: (0, i)),
            pl.BlockSpec((width, TILE), lambda i: (0, i)),
            pl.BlockSpec((TILE, width), lambda i: (i, 0)),
        ],
        out_specs=[
            whole((rows, width)),
            col,
            col,
            col,
            whole((half, width)),
        ]
        + [whole(piece)] * PIECES
        + [whole((1, width))],
        out_shape=[
            jax.ShapeDtypeStruct((rows, width), b16),
            wide,
            wide,
            wide,
            jax.ShapeDtypeStruct((half, width), f32),
        ]
        + [jax.ShapeDtypeStruct(piece, f32)] * PIECES
        + [jax.ShapeDtypeStruct((1, width), f32)],
        scratch_shapes=[pltpu.VMEM((rows, 1), f32)],
        compiler_params=vmem(),
        name="own_feed",
    )(r_a, *r_b, cot, g.reshape(1, -1), w_gate, w_up, w_down)


def put_columns(at_ref, cc_ref, nb_ref, cb_ref, where_ref, count, block):
    for j in range(count):
        here = pl.ds(pl.multiple_of(where_ref[j] * block, 128), block)
        at_ref[j * block : (j + 1) * block, :] = nb_ref[:, here].T
        cc_ref[:, j * block : (j + 1) * block] = cb_ref[:, here]


def put_grads(sums, at_ref, cc_ref, hidden, d_gate, d_up, block, before=None):
    down = dot_tn(hidden, cc_ref[...])
    gate = dot(at_ref[...], d_gate)
    up = dot(at_ref[...], d_up)
    count = len(sums) // 2
    for j in range(count):
        part = slice(j * block, (j + 1) * block)
        for k, rows, fresh in (
            (j, slice(None), down[:, part]),
            (count + j, slice(0, block), gate[part]),
            (count + j, slice(block, 2 * block), up[part]),
        ):
            old = 0.0 if before is None else before[k][rows, :]
            sums[k][rows, :] = fresh + old


def rest_kernel(where_ref, nb_ref, cb_ref, hid_ref, dg_ref, du_ref, wd_ref, *rest):
    count = (len(rest) - 4) // 2
    ya_ref, yb_ref, *sums = rest[:-2]
    at_ref, cc_ref = rest[-2:]
    half = ya_ref.shape[0]
    block = cc_ref.shape[1] // count

    @pl.when(pl.program_id(0) == 0)
    def _():
        put_columns(at_ref, cc_ref, nb_ref, cb_ref, where_ref, count, block)
        ya_ref[...] = jnp.zeros_like(ya_ref)
        yb_ref[...] = jnp.zeros_like(yb_ref)

    hidden = hid_ref[...]
    ya_ref[...] += dot(hidden[:half], wd_ref[...])
    yb_ref[...] += dot(hidden[half:], wd_ref[...])
    put_grads(sums, at_ref, cc_ref, hidden, dg_ref[...], du_ref[...], block)


def sum_specs(count, block, hidden):
    specs = [pl.BlockSpec((TILE, block), lambda i, *_: (i, 0))] * count
    specs += [pl.BlockSpec((2 * block, TILE), lambda i, *_: (0, i))] * count
    shapes = [jax.ShapeDtypeStruct((hidden, block), f32)] * count
    shapes += [jax.ShapeDtypeStruct((2 * block, hidden), f32)] * count
    return specs, shapes


def own_rest(where, nb, cb, hidden, d_gate, d_up, w_down, block):
    rows, width = nb.shape
    count = where.shape[0]
    half, ff = rows // 2, hidden.shape[1]
    specs, shapes = sum_specs(count, block, ff)
    col = pl.BlockSpec((rows, TILE), lambda i, *_: (0, i))
    part = jax.ShapeDtypeStruct((half, width), f32)
    out = pl.pallas_call(
        rest_kernel,
        grid_spec=pltpu.PrefetchScalarGridSpec(
            num_scalar_prefetch=1,
            grid=(ff // TILE,),
            in_specs=[
                whole((rows, width)),
                whole((rows, width)),
                col,
                col,
                col,
                pl.BlockSpec((TILE, width), lambda i, *_: (i, 0)),
            ],
            out_specs=[whole((half, width)), whole((half, width))] + specs,
            scratch_shapes=[
                pltpu.VMEM((count * block, rows), b16),
                pltpu.VMEM((rows, count * block), b16),
            ],
        ),
        out_shape=[part, part] + shapes,
        compiler_params=vmem(),
        name="own_rest",
    )(where, nb, cb, hidden, d_gate, d_up, w_down)
    return out[0], out[1], list(out[2:])


def group_kernel(n_pieces, c_pieces, count, where_ref, *refs):
    n_refs, refs = refs[:n_pieces], refs[n_pieces:]
    c_refs, refs = refs[:c_pieces], refs[c_pieces:]
    g_ref, wg_ref, wu_ref, wd_ref = refs[:4]
    before = refs[4 : 4 + 2 * count]
    sums = refs[4 + 2 * count : 4 + 4 * count]
    nb_ref, cb_ref, at_ref, cc_ref = refs[4 + 4 * count :]
    block = cc_ref.shape[1] // count

    @pl.when(pl.program_id(0) == 0)
    def _():
        at = 0
        for n_ref in n_refs:
            size = n_ref.shape[0]
            nb_ref[at : at + size, :] = (n_ref[...] * g_ref[...]).astype(b16)
            at += size
        at = 0
        for c_ref in c_refs:
            size = c_ref.shape[0]
            cb_ref[at : at + size, :] = (c_ref[...] * 0.5).astype(b16)
            at += size
        put_columns(at_ref, cc_ref, nb_ref, cb_ref, where_ref, count, block)

    hidden, d_gate, d_up = gated(nb_ref, cb_ref, wg_ref, wu_ref, wd_ref)
    put_grads(sums, at_ref, cc_ref, hidden, d_gate, d_up, block, before)


def group_feed(where, ns, cs, g, w_gate, w_up, w_down, before, block):
    width, ff = w_gate.shape
    count = where.shape[0]
    rows = sum(n.shape[0] for n in ns)
    specs, shapes = sum_specs(count, block, ff)
    return list(
        pl.pallas_call(
            functools.partial(group_kernel, len(ns), len(cs), count),
            grid_spec=pltpu.PrefetchScalarGridSpec(
                num_scalar_prefetch=1,
                grid=(ff // TILE,),
                in_specs=[whole(a.shape) for a in (*ns, *cs)]
                + [
                    whole((1, width)),
                    pl.BlockSpec((width, TILE), lambda i, *_: (0, i)),
                    pl.BlockSpec((width, TILE), lambda i, *_: (0, i)),
                    pl.BlockSpec((TILE, width), lambda i, *_: (i, 0)),
                ]
                + specs,
                out_specs=specs,
                scratch_shapes=[
                    pltpu.VMEM((rows, width), b16),
                    pltpu.VMEM((rows, width), b16),
                    pltpu.VMEM((count * block, rows), b16),
                    pltpu.VMEM((rows, count * block), b16),
                ],
            ),
            out_shape=shapes,
            compiler_params=vmem(),
            name="group_feed",
        )(where, *ns, *cs, g.reshape(1, -1), w_gate, w_up, w_down, *before)
    )


def sum_kernel(count, *refs):
    a_ref, b_refs, outs = refs[0], refs[1 : 1 + count], refs[1 + count :]
    size = a_ref.shape[0] // count
    for i, b_ref in enumerate(b_refs):
        at = slice(i * size, (i + 1) * size)
        total = a_ref[at, :] + b_ref[...]
        outs[0][at, :] = total
    pieces = outs[1:]
    for i, piece in enumerate(pieces):
        piece[...] = outs[0][i * piece.shape[0] : (i + 1) * piece.shape[0], :]


def sum_of(a, bs, split=0):
    shapes = [jax.ShapeDtypeStruct(a.shape, f32)]
    shapes += [jax.ShapeDtypeStruct((a.shape[0] // max(split, 1), a.shape[1]), f32)] * split
    return pl.pallas_call(
        functools.partial(sum_kernel, len(bs)),
        in_specs=[whole(x.shape) for x in (a, *bs)],
        out_specs=[whole(x.shape) for x in shapes],
        out_shape=shapes,
        grid=(1,),
        compiler_params=vmem(),
        name="sum_of",
    )(a, *bs)


def resid_kernel(x_at_ref, tok_ref, a_ref, b_ref, c_ref, r_ref, n_ref, quarter_ref, *pieces):
    size = pieces[0].shape[0]
    for i, piece in enumerate(pieces):
        at = slice(i * size, (i + 1) * size)
        part, first = (b_ref, 0) if i < len(pieces) // 2 else (c_ref, len(pieces) // 2)
        far = part[(i - first) * size : (i - first + 1) * size, :]
        resid = tok_ref[at, :].astype(f32) + (a_ref[at, :] + far)
        r_ref[at, :] = resid
        piece[...] = resid
        n_ref[at, :] = resid * lax.rsqrt(jnp.mean(resid * resid, axis=-1, keepdims=True) + EPS)
    small = quarter_ref.shape[0]
    quarter_ref[...] = n_ref[pl.ds(pl.multiple_of(x_at_ref[0] * small, small), small), :]


def resid_of(x_at, tok, a, b, c):
    rows, width = a.shape
    shapes = [(rows, width), (rows, width), (rows // 2, width)] + [(rows // PIECES, width)] * PIECES
    return pl.pallas_call(
        resid_kernel,
        grid_spec=pltpu.PrefetchScalarGridSpec(
            num_scalar_prefetch=1,
            grid=(1,),
            in_specs=[whole(a.shape)] * 2 + [whole(b.shape)] * 2,
            out_specs=[whole(s) for s in shapes],
        ),
        out_shape=[jax.ShapeDtypeStruct(s, f32) for s in shapes],
        compiler_params=vmem(),
        name="resid_of",
    )(x_at, tok, a, b, c)


def feed(normed, cot, w_gate, w_up, w_down):
    gate_pre = dot(normed, w_gate)
    up_pre = dot(normed, w_up)
    d_hidden = dot_nt(cot, w_down)
    sigmoid_g = jax.nn.sigmoid(gate_pre)
    act_gate = gate_pre * sigmoid_g
    hidden = (act_gate * up_pre).astype(b16)
    d_up = (d_hidden * act_gate).astype(b16)
    d_gate = (d_hidden * up_pre * (sigmoid_g * (1.0 + gate_pre * (1.0 - sigmoid_g)))).astype(b16)
    return hidden, d_gate, d_up


def plain_grads(where, normed, cot, parts, block):
    hidden, d_gate, d_up = parts
    takes = [functools.partial(lax.dynamic_slice_in_dim, start_index=w * block, slice_size=block, axis=1) for w in where]
    pair = jnp.concatenate([d_gate, d_up], axis=1)
    both = [dot_tn(take(normed), pair) for take in takes]
    ff = hidden.shape[1]
    return [dot_tn(hidden, take(cot)) for take in takes] + [jnp.concatenate([b[:, :ff], b[:, ff:]]) for b in both]


def plain_own_feed(r_a, r_b, cot, g, w_gate, w_up, w_down):
    resid = jnp.concatenate([r_a, *r_b])
    normed, unit, _ = rms_norm(resid, g)
    normed = normed.astype(b16)
    parts = feed(normed, cot, w_gate, w_up, w_down)
    total = dot_nt(parts[1], w_gate) + dot_nt(parts[2], w_up)
    half = r_a.shape[0]
    gain = jnp.sum(total * unit, axis=0, keepdims=True)
    return (normed, *parts, total[:half], *jnp.split(total[half:], PIECES), gain)


def plain_own_rest(where, nb, cb, hidden, d_gate, d_up, w_down, block):
    down = dot(hidden, w_down)
    half = nb.shape[0] // 2
    return down[:half], down[half:], plain_grads(where, nb, cb, (hidden, d_gate, d_up), block)


def plain_group_feed(where, ns, cs, g, w_gate, w_up, w_down, before, block):
    normed = (jnp.concatenate(ns) * g).astype(b16)
    cot = (jnp.concatenate(cs) * 0.5).astype(b16)
    parts = feed(normed, cot, w_gate, w_up, w_down)
    return [old + new for old, new in zip(before, plain_grads(where, normed, cot, parts, block))]


def rope_tables(length, width):
    half = width // 2
    inverse = THETA ** (-(jnp.arange(half).astype(f32) * 2.0 / width))
    angles = jnp.arange(length).astype(f32)[:, None] * inverse[None, :]
    angles = jnp.concatenate([angles, angles], axis=1)
    sign = jnp.where(jnp.arange(width) < half, -1.0, 1.0).astype(f32)
    return jnp.cos(angles), jnp.sin(angles) * sign[None, :]


def turn(values, cosine, sine):
    return values * cosine + pltpu.roll(values, values.shape[-1] // 2, 1) * sine


def turn_back(grads, cosine, sine):
    return grads * cosine + pltpu.roll(grads * sine, grads.shape[-1] // 2, 1)


def norm_of(values):
    inv = lax.rsqrt(jnp.mean(values * values, axis=-1, keepdims=True) + EPS)
    return values * inv, inv


def norm_back(scaled, unit, inv):
    return inv * (scaled - unit * jnp.mean(scaled * unit, axis=-1, keepdims=True))


def softmax_of(q_rot, k_rot):
    length, width = q_rot.shape
    scores = dot_nt(q_rot, k_rot) * (width**-0.5)
    at = lax.broadcasted_iota(jnp.int32, (length, length), 0)
    to = lax.broadcasted_iota(jnp.int32, (length, length), 1)
    scores = jnp.where(at >= to, scores, -1e30)
    grown = jnp.exp(scores - jnp.max(scores, axis=-1, keepdims=True))
    return grown * (1.0 / jnp.sum(grown, axis=-1, keepdims=True))


def attend_kernel(half, core_ref, tok_ref, g_ref, wq_ref, wk_ref, wv_ref, qg_ref, kg_ref, wo_ref, cos_ref, sin_ref, *outs):
    n_ref, q_ref, k_ref, v_ref, att_ref, wide_ref, mine_ref = outs[:7]
    width = qg_ref.shape[1]
    cosine, sine = cos_ref[...], sin_ref[...]
    unit, _ = norm_of(tok_ref[...].astype(f32))
    normed = (unit * g_ref[...]).astype(b16)
    n_ref[...] = normed
    query = dot(normed, wq_ref[...])
    keys = dot(normed, wk_ref[...])
    values = dot(normed, wv_ref[...]).astype(b16)
    q_ref[...] = query
    k_ref[...] = keys
    v_ref[...] = values
    kv_heads = keys.shape[1] // width
    share = query.shape[1] // keys.shape[1]
    for kv in range(kv_heads):
        at = slice(kv * width, (kv + 1) * width)
        k_unit, _ = norm_of(keys[:, at])
        k_rot = turn(k_unit * kg_ref[...], cosine, sine).astype(b16)
        for h in range(kv * share, (kv + 1) * share):
            to = slice(h * width, (h + 1) * width)
            q_unit, _ = norm_of(query[:, to])
            q_rot = turn(q_unit * qg_ref[...], cosine, sine).astype(b16)
            probs = softmax_of(q_rot, k_rot).astype(b16)
            att_ref[:, to] = dot(probs, values[:, at]).astype(b16)
    wide_ref[...] = att_ref[...].astype(f32) * 2.0
    mixed = dot(att_ref[...], wo_ref[...])

    @pl.when(pl.program_id(0) < half)
    def _():
        for i, ref in enumerate(outs[7:]):
            ref[...] = mixed[i * ref.shape[0] : (i + 1) * ref.shape[0]]

    @pl.when(pl.program_id(0) >= half)
    def _():
        mine_ref[...] = mixed


def attend(core, tokens, g, wq, wk, wv, qg, kg, wo, cosine, sine):
    rows, width = tokens.shape
    seqs = rows // SEQ_LEN
    half = seqs // 2

    def source(i, core_ref):
        mine = core_ref[0]
        return (jnp.where(i < half, (1 - mine) * half + i, mine * half + i - half), 0)

    def place(i, _):
        return ((i + half) % seqs, 0)

    def out(columns, dtype):
        return pl.BlockSpec((SEQ_LEN, columns), place), jax.ShapeDtypeStruct((rows, columns), dtype)

    nq, nk = wq.shape[1], wk.shape[1]
    outs = [out(width, b16), out(nq, f32), out(nk, f32), out(nk, b16), out(nq, b16), out(nq, f32)]
    part = jax.ShapeDtypeStruct((rows // 2, width), f32)
    piece = SEQ_LEN // PIECES
    return pl.pallas_call(
        functools.partial(attend_kernel, half),
        grid_spec=pltpu.PrefetchScalarGridSpec(
            num_scalar_prefetch=1,
            grid=(seqs,),
            in_specs=[pl.BlockSpec((SEQ_LEN, width), source)]
            + [whole(a.shape) for a in (g, wq, wk, wv, qg, kg, wo, cosine, sine)],
            out_specs=[o[0] for o in outs]
            + [
                pl.BlockSpec((SEQ_LEN, width), lambda i, _: (jnp.maximum(i - half, 0), 0)),
            ]
            + [pl.BlockSpec((piece, width), lambda i, _: (jnp.minimum(i, half - 1), 0))] * PIECES,
        ),
        out_shape=[o[1] for o in outs]
        + [part]
        + [jax.ShapeDtypeStruct((piece * half, width), f32)] * PIECES,
        compiler_params=vmem(),
        name="attend",
    )(core, tokens, g, wq, wk, wv, qg, kg, wo, cosine, sine)


def attend_back_kernel(half, core_ref, *refs):
    dnb_refs, rb_refs, refs = refs[:PIECES], refs[PIECES : 2 * PIECES], refs[2 * PIECES :]
    ins, outs = refs[:18], refs[18:]
    dna_ref, ra_ref, cot_ref, tok_ref, q_ref, k_ref, v_ref, att_ref = ins[:8]
    gm_ref, ga_ref, qg_ref, kg_ref, wq_ref, wk_ref, wv_ref, wo_ref, cos_ref, sin_ref = ins[8:]
    dr_ref, drm_ref, dqkv_ref, wide_ref, d1a_ref, ga_out, gq_out, gk_out = outs[:8]
    d1b_refs, (r_ref, dn_ref) = outs[8:-2], outs[-2:]
    step = pl.program_id(0)
    width = qg_ref.shape[1]
    cosine, sine = cos_ref[...], sin_ref[...]

    @pl.when(step == 0)
    def _():
        ga_out[...] = jnp.zeros_like(ga_out)
        gq_out[...] = jnp.zeros_like(gq_out)
        gk_out[...] = jnp.zeros_like(gk_out)

    mine = step < half

    @pl.when(mine)
    def _():
        r_ref[...] = ra_ref[...]
        dn_ref[...] = dna_ref[...]

    @pl.when(step >= half)
    def _():
        for i, (r_piece, dn_piece) in enumerate(zip(rb_refs, dnb_refs)):
            at = slice(i * r_piece.shape[0], (i + 1) * r_piece.shape[0])
            r_ref[at, :] = r_piece[...]
            dn_ref[at, :] = dn_piece[...]

    unit2, inv2 = norm_of(r_ref[...])
    scaled = dn_ref[...] * gm_ref[...]
    d_resid = cot_ref[...].astype(f32) + norm_back(scaled, unit2, inv2)
    d_resid_b = d_resid.astype(b16)
    dr_ref[...] = d_resid_b

    @pl.when(mine)
    def _():
        drm_ref[...] = d_resid

    d_att = dot_nt(d_resid_b, wo_ref[...]).astype(b16)
    nq, nk = q_ref.shape[1], k_ref.shape[1]
    share = nq // nk
    for kv in range(nk // width):
        at = slice(kv * width, (kv + 1) * width)
        k_unit, k_inv = norm_of(k_ref[:, at])
        k_rot = turn(k_unit * kg_ref[...], cosine, sine).astype(b16)
        values = v_ref[:, at]
        d_krot = d_values = 0.0
        for h in range(kv * share, (kv + 1) * share):
            to = slice(h * width, (h + 1) * width)
            q_unit, q_inv = norm_of(q_ref[:, to])
            q_rot = turn(q_unit * qg_ref[...], cosine, sine).astype(b16)
            probs = softmax_of(q_rot, k_rot)
            d_head = d_att[:, to]
            d_prob = dot_nt(d_head, values)
            delta = jnp.sum(d_head.astype(f32) * att_ref[:, to].astype(f32), axis=-1, keepdims=True)
            d_score = (probs * (d_prob - delta) * (width**-0.5)).astype(b16)
            d_krot += dot_tn(d_score, q_rot)
            d_values += dot_tn(probs.astype(b16), d_head)
            d_qn = turn_back(dot(d_score, k_rot), cosine, sine)
            gq_out[...] += jnp.sum(d_qn * q_unit, axis=0, keepdims=True)
            dqkv_ref[:, to] = norm_back(d_qn * qg_ref[...], q_unit, q_inv).astype(b16)
        d_kn = turn_back(d_krot, cosine, sine)
        gk_out[...] += jnp.sum(d_kn * k_unit, axis=0, keepdims=True)
        here = slice(nq + kv * width, nq + (kv + 1) * width)
        dqkv_ref[:, here] = norm_back(d_kn * kg_ref[...], k_unit, k_inv).astype(b16)
        here = slice(nq + nk + kv * width, nq + nk + (kv + 1) * width)
        dqkv_ref[:, here] = d_values.astype(b16)
    wide_ref[...] = dqkv_ref[...].astype(f32) * 2.0
    d_norm1 = (
        dot_nt(dqkv_ref[:, :nq], wq_ref[...])
        + dot_nt(dqkv_ref[:, nq : nq + nk], wk_ref[...])
        + dot_nt(dqkv_ref[:, nq + nk :], wv_ref[...])
    )
    unit1, _ = norm_of(tok_ref[...].astype(f32))
    ga_out[...] += jnp.sum(d_norm1 * unit1, axis=0, keepdims=True)

    @pl.when(mine)
    def _():
        d1a_ref[...] = d_norm1

    @pl.when(step >= half)
    def _():
        for i, ref in enumerate(d1b_refs):
            ref[...] = d_norm1[i * ref.shape[0] : (i + 1) * ref.shape[0]]


def attend_back(core, dn_a, dn_b, r_a, r_b, cot, tokens, q, k, v, att, gm, ga, qg, kg, wq, wk, wv, wo, cosine, sine):
    rows, width = tokens.shape
    seqs = rows // SEQ_LEN
    half = seqs // 2

    def source(i, core_ref):
        mine = core_ref[0]
        return (jnp.where(i < half, mine * half + i, (1 - mine) * half + i - half), 0)

    def low(i, _):
        return (jnp.minimum(i, half - 1), 0)

    def high(i, _):
        return (jnp.maximum(i - half, 0), 0)

    def same(i, _):
        return (i, 0)

    def block(columns, place):
        return pl.BlockSpec((SEQ_LEN, columns), place)

    nq, nk = wq.shape[1], wk.shape[1]
    part = jax.ShapeDtypeStruct((rows // 2, width), f32)
    consts = (gm, ga, qg, kg, wq, wk, wv, wo, cosine, sine)
    small = [(1, width), qg.shape, kg.shape]
    piece = SEQ_LEN // PIECES
    return pl.pallas_call(
        functools.partial(attend_back_kernel, half),
        grid_spec=pltpu.PrefetchScalarGridSpec(
            num_scalar_prefetch=1,
            grid=(seqs,),
            in_specs=[
                pl.BlockSpec((piece, width), high),
            ]
            * (2 * PIECES)
            + [
                block(width, low),
                block(width, low),
                block(width, same),
                block(width, source),
                block(nq, same),
                block(nk, same),
                block(nk, same),
                block(nq, same),
            ]
            + [whole(a.shape) for a in consts],
            out_specs=[
                block(width, same),
                block(width, low),
                block(nq + 2 * nk, same),
                block(nq + 2 * nk, same),
                block(width, low),
            ]
            + [whole(s) for s in small]
            + [pl.BlockSpec((piece, width), high)] * PIECES,
            scratch_shapes=[pltpu.VMEM((SEQ_LEN, width), f32)] * 2,
        ),
        out_shape=[
            jax.ShapeDtypeStruct((rows, width), b16),
            part,
            jax.ShapeDtypeStruct((rows, nq + 2 * nk), b16),
            jax.ShapeDtypeStruct((rows, nq + 2 * nk), f32),
            part,
        ]
        + [jax.ShapeDtypeStruct(s, f32) for s in small]
        + [jax.ShapeDtypeStruct((piece * half, width), f32)] * PIECES,
        compiler_params=vmem(),
        name="attend_back",
    )(core, *dn_b, *r_b, dn_a, r_a, cot, tokens, q, k, v, att, *consts)


def back_kernel(dr_ref, a_ref, b_ref, tok_ref, g_ref, out_ref, *pieces):
    size = pieces[0].shape[0]
    for i, piece in enumerate(pieces):
        at = slice(i * size, (i + 1) * size)
        unit, inv = norm_of(tok_ref[at, :].astype(f32))
        grads = dr_ref[at, :] + norm_back((a_ref[at, :] + b_ref[at, :]) * g_ref[...], unit, inv)
        out_ref[at, :] = grads
        piece[...] = grads


def back_of(dr, a, b, tok, g):
    rows, width = a.shape
    shapes = [(rows, width)] + [(rows // PIECES, width)] * PIECES
    return pl.pallas_call(
        back_kernel,
        grid=(1,),
        in_specs=[whole(x.shape) for x in (dr, a, b, tok, g)],
        out_specs=[whole(x) for x in shapes],
        out_shape=[jax.ShapeDtypeStruct(x, f32) for x in shapes],
        compiler_params=vmem(),
        name="back_of",
    )(dr, a, b, tok, g)


def few_kernel(normed, where_ref, a_ref, g_ref, out_ref, row_ref):
    block = out_ref.shape[1] // where_ref.shape[0]
    here = a_ref[...].astype(f32)
    if normed:
        here = (norm_of(here)[0] * g_ref[...]).astype(b16).astype(f32)
    row_ref[...] = here
    for j in range(where_ref.shape[0]):
        at = pl.ds(pl.multiple_of(where_ref[j] * block, 128), block)
        out_ref[:, j * block : (j + 1) * block] = row_ref[:, at]


def few_of(where, a, g, block, normed):
    half, width = a.shape[0] if normed else a.shape[0] // 2, a.shape[1]
    out = (half, where.shape[0] * block)
    return pl.pallas_call(
        functools.partial(few_kernel, normed),
        grid_spec=pltpu.PrefetchScalarGridSpec(
            num_scalar_prefetch=1,
            grid=(1,),
            in_specs=[whole((half, width)), whole(g.shape)],
            out_specs=whole(out),
            scratch_shapes=[pltpu.VMEM((half, width), f32)],
        ),
        out_shape=jax.ShapeDtypeStruct(out, f32),
        compiler_params=vmem(),
        name="few_of",
    )(where, a, g)


def plain_few_of(where, a, g, block, normed):
    half = a.shape[0] if normed else a.shape[0] // 2
    here = a[:half].astype(f32)
    if normed:
        here = rms_norm(here, g)[0].astype(b16).astype(f32)
    return jnp.concatenate([lax.dynamic_slice_in_dim(here, w * block, block, 1) for w in where], axis=1) * 2.0


def pair_kernel(inward, where_ref, a_ref, b_ref, few_a_ref, few_b_ref, wide_ref, out_ref, far_a_ref, far_b_ref):
    half = few_a_ref.shape[0]

    @pl.when(pl.program_id(0) == 0)
    def _():
        far_b_ref[...] = (wide_ref[...] * 0.5).astype(b16)

    far_a_ref[:half, :] = few_a_ref[...].astype(b16)
    far_a_ref[half:, :] = few_b_ref[...].astype(b16)
    if inward:
        out_ref[...] = dot_tn(a_ref[...], b_ref[...]) + dot_tn(far_a_ref[...], far_b_ref[...])
    else:
        out_ref[...] = dot_tn(b_ref[...], a_ref[...]) + dot_tn(far_b_ref[...], far_a_ref[...])


def pair_grads(where, first, a, b, few, wide, block, inward):
    rows, columns, count = a.shape[0], b.shape[1], where.shape[0]
    out = (block, columns) if inward else (columns, block)
    return pl.pallas_call(
        functools.partial(pair_kernel, inward),
        grid_spec=pltpu.PrefetchScalarGridSpec(
            num_scalar_prefetch=1,
            grid=(count,),
            in_specs=[pl.BlockSpec((rows, block), lambda j, at: (0, at[j])), whole((rows, columns))]
            + [pl.BlockSpec((rows // 2, block), lambda j, _: (0, first + j))] * 2
            + [whole((rows, columns))],
            out_specs=pl.BlockSpec(out, lambda j, _: (j, 0)),
            scratch_shapes=[pltpu.VMEM((rows, block), b16), pltpu.VMEM((rows, columns), b16)],
        ),
        out_shape=jax.ShapeDtypeStruct((count * out[0], out[1]), f32),
        compiler_params=vmem(),
        name="pair_grads",
    )(where, a, b, *few, wide)


def plain_pair_grads(where, first, a, b, few, wide, block, inward):
    far_a = (jnp.concatenate(few) * 0.5).astype(b16)
    far_b = (wide * 0.5).astype(b16)
    out = []
    for j, w in enumerate(where):
        near_a = lax.dynamic_slice_in_dim(a, w * block, block, 1)
        other = far_a[:, (first + j) * block : (first + j + 1) * block]
        if inward:
            out.append(dot_tn(near_a, b) + dot_tn(other, far_b))
        else:
            out.append(dot_tn(b, near_a) + dot_tn(far_b, other))
    return jnp.concatenate(out)


def tensor_masks():
    size = lax.axis_size("tensor")
    return [1 << i for i in range(1, size.bit_length() - 1)]


def scatter_sum(parts, masks):
    for mask in masks:
        half = len(parts) // 2
        received = [swap(p, "dp", mask) for p in parts[half:]]
        parts = [a + b for a, b in zip(parts[:half], received)]
    return parts[0]


def relative(masks):
    offsets = [0]
    for mask in reversed(masks):
        offsets = offsets + [o ^ mask for o in offsets]
    return offsets


def body(
    tokens,
    g_attn,
    w_query,
    w_key,
    w_value,
    q_gain,
    k_gain,
    w_out,
    g_mlp,
    w_gate,
    w_up,
    w_down,
    cotangent,
):
    rows, width = tokens.shape
    hd = q_gain.shape[0]
    cosine, sine = rope_tables(SEQ_LEN, hd)
    n_dp = lax.axis_size("dp")
    me = lax.axis_index("dp")
    core = lax.axis_index("tensor") % 2
    core_at = core.astype(jnp.int32).reshape(1)
    x_at = (lax.axis_index("tensor") // 2).astype(jnp.int32).reshape(1)
    half = rows // 2
    block = width // n_dp
    bits = [1 << i for i in range(n_dp.bit_length() - 1)]
    near, far = bits[0], bits[-1]
    middle = bits[1:-1]
    ga, gm, gq, gk = (g.reshape(1, -1) for g in (g_attn, g_mlp, q_gain, k_gain))
    seq = Sequence()

    def mine_of(a):
        return lax.dynamic_slice_in_dim(a, core * half, half, 0)

    def theirs_of(a):
        return lax.dynamic_slice_in_dim(a, (1 - core) * half, half, 0)

    def in_order(mine, theirs):
        out = jnp.zeros((rows,) + mine.shape[1:], mine.dtype)
        out = lax.dynamic_update_slice_in_dim(out, mine, core * half, 0)
        return lax.dynamic_update_slice_in_dim(out, theirs, (1 - core) * half, 0)

    def quarter_of(a):
        size = a.shape[0] // 2
        return lax.dynamic_slice_in_dim(a, (lax.axis_index("tensor") // 2) * size, size, 0)

    def one(value, count):
        return [value] if count == 1 else list(value)

    def pick(kernel, plain):
        return kernel if block % 128 == 0 else plain

    def at(offsets):
        return me ^ jnp.array(offsets, jnp.int32)

    def core_swap(a):
        return swap(a, "tensor", 1)

    def core_swaps(pieces):
        return [swap(a, "tensor", 1) for a in pieces]

    def x_swap(a):
        return swap(a, "tensor", 2)

    few = pick(few_of, plain_few_of)
    pair = pick(pair_grads, plain_pair_grads)
    rest = middle + [far]
    blocks = relative(rest)
    q = len(blocks) // 2
    rest_out = [near] + middle[1:] + [far]
    blocks_out = relative(rest_out)
    theirs_at, theirs_out = at([near ^ o for o in blocks]), at([middle[0] ^ o for o in blocks_out])

    cot_mine, cot_theirs = mine_of(cotangent), theirs_of(cotangent)
    cot_own = jnp.concatenate([cot_mine, cot_theirs])
    c0 = cot_mine.astype(f32) * 2.0
    c0, c0_quarter, tokens_then = seq(c0, quarter_of(c0), tokens)
    c1 = swap(c0, "dp", near)
    c2 = swap(c0_quarter, "dp", far)
    tok_mine = mine_of(tokens)
    normed1, query, keys, values, attended, att_wide, mixed_a, *mixed_b = seq(
        *attend(core_at, tokens_then, ga, w_query, w_key, w_value, gq, gk, w_out, cosine, sine)
    )
    mixed_got = seq(*core_swaps(mixed_b))
    mixed_chip, *mixed_split = seq(*sum_of(mixed_a, mixed_got, split=2))
    mixed_x = [x_swap(p) for p in mixed_split]
    c1, c2, *mixed_x = seq(c1, c2, *mixed_x)

    r_a, n0, n0_quarter, *r_split = seq(*resid_of(x_at, tok_mine, mixed_chip, *mixed_x))
    n1 = swap(n0, "dp", near)
    n2 = swap(n0_quarter, "dp", far)
    c2x = x_swap(c2)
    r_b = seq(*core_swaps(r_split))

    normed2, hidden, d_gate, d_up, dn_a, *dn_b, mlp_gain = seq(
        *pick(own_feed, plain_own_feed)(r_a, r_b, cot_own, gm, w_gate, w_up, w_down)
    )
    offsets = relative(middle)
    down_a, down_b, sums = pick(own_rest, plain_own_rest)(
        at(offsets), normed2, cot_own, hidden, d_gate, d_up, w_down, block
    )
    down_a, down_b, *both = seq(down_a, down_b, *sums, *dn_b)
    sums, dn_b = both[:-PIECES], both[-PIECES:]
    n2, c2x = seq(n2, c2x)
    n2x = x_swap(n2)
    n3 = swap(n2, "dp", near)
    n1, *dn_got = seq(n1, *core_swaps(dn_b))
    (dn_chip,) = sum_of(dn_a, dn_got)
    c2 = jnp.concatenate([c2, c2x])
    dn_chip, c2 = seq(dn_chip, c2)
    near_n = few(theirs_at, seq(tok_mine), ga, block, True)
    n1t, c1t, down_got = core_swaps((n1, c1, down_b))
    n1t, c1t, down_got, n2x, n3, dn_chip, c2, near_n = seq(n1t, c1t, down_got, n2x, n3, dn_chip, c2, near_n)
    dn_x = x_swap(dn_chip)
    c3 = swap(c2, "dp", near)

    def add_group(ns, cs, sums):
        group = pick(group_feed, plain_group_feed)
        return list(seq(*group(at(offsets), ns, cs, gm, w_gate, w_up, w_down, sums, block)))

    n2t, c2t = core_swaps((n2, c2))
    sums = add_group([n1, n1t], [c1, c1t], sums)
    n2t, c2t = seq(n2t, c2t)
    n2xt = seq(core_swap(n2x))
    sums = add_group([n2, n2x, n2t, n2xt], [c2, c2t], sums)
    dn_x, c3, n3 = seq(dn_x, c3, n3)

    n3x = x_swap(n3)
    dn_mine, *dn_split = seq(*sum_of(dn_chip, [dn_x], split=PIECES))
    *dn_theirs, c3, n3, near_n, att_wide = seq(*core_swaps(dn_split), c3, n3, near_n, att_wide)
    near_n = swap(near_n, "dp", near)
    near_att = swap(att_wide, "dp", middle[0])
    c3t, n3t = core_swaps((c3, n3))
    dr_b, dr_mine, d_qkv, d_wide, d1_a, gain_a, gain_q, gain_k, *d1_b = seq(
        *attend_back(
            core_at, dn_mine, dn_theirs, r_a, r_b, cot_own, tokens, query, keys, values, attended,
            gm, ga, gq, gk, w_query, w_key, w_value, w_out, cosine, sine,
        )
    )
    near_r = few(theirs_out, dr_b, gm, block, False)
    near_r, n3x, c3t, n3t, near_att, near_n = seq(near_r, n3x, c3t, n3t, near_att, near_n)
    near_d = swap(d_wide, "dp", near)
    near_r = swap(near_r, "dp", middle[0])
    gains = jnp.concatenate([gain_a[0], gain_q[0], gain_k[0], mlp_gain[0]])
    gains_got = x_swap(gains)
    n3xt = seq(core_swap(n3x))
    sums = add_group([n3, n3x, n3t, n3xt], [c3, c3t], sums)
    k = len(offsets)
    h = k // 2
    lists = [sums[i * k : (i + 1) * k] for i in range(2)]
    keep = [p[:h] for p in lists]
    send = [p[h:] for p in lists]

    def first_step(parts):
        return [swap(p, "dp", middle[0]) for p in parts]

    def finish(keep, got):
        return scatter_sum([a + b for a, b in zip(keep, got)], middle[1:])

    got = first_step(send[1])
    near_r, gains_got, *d1_b = seq(near_r, gains_got, *d1_b)
    gains = gains + gains_got
    near_nt, gains_got, *d1_got = seq(*core_swaps((near_n, gains, *d1_b)))
    gains = gains + gains_got
    gains_got = swap(gains, "dp", near)
    (d1_chip,), (down_chip,) = sum_of(d1_a, d1_got), sum_of(down_a, [down_got])
    d1_chip, down_chip = seq(d1_chip, down_chip)
    d1_x = x_swap(d1_chip)
    def ins(i):
        return pair(at(blocks[i * q : (i + 1) * q]), i * q, normed1, d_qkv, near_ns, near_d, block, True)

    def outs(i):
        return pair(at(blocks_out[i * q : (i + 1) * q]), i * q, dr_b, attended, near_rs, near_att, block, False)

    near_rs = [near_r, seq(core_swap(near_r))]
    out_1 = seq(outs(1))
    out_mid = swap(out_1, "dp", rest_out[0])
    near_d, near_nt = seq(near_d, near_nt)
    near_ns = [near_n, near_nt]
    in_1, down_chip, *got = seq(seq(ins(1)), down_chip, *got)
    down_x = x_swap(down_chip)
    in_mid = swap(in_1, "dp", rest[0])
    in_0, out_0 = seq(ins(0), outs(0))
    out_mid, gains_got = seq(out_mid, gains_got)
    gains = gains + gains_got
    gains_got = swap(gains, "dp", rest[0])
    summed_pair = finish(keep[1], got)
    if len(rest) == 2:
        summed_pair = seq(summed_pair)

    def split(a):
        return list(a.reshape(q, a.shape[0] // q, a.shape[1]))

    d1_x = seq(d1_x)
    gt_mine, *gt_split = seq(*back_of(dr_mine, d1_chip, d1_x, tok_mine, ga))
    gt_theirs = jnp.concatenate(seq(*core_swaps(gt_split)))
    grad_tokens = seq(in_order(gt_mine, gt_theirs))
    in_mid, gains_got, down_x, *send_down = seq(in_mid, gains_got, down_x, *send[0])
    got_down = first_step(send_down)
    gains = gains + gains_got
    gains_got = swap(gains, "dp", far)
    both = seq(*split(in_0 + in_mid), *split(out_0 + out_mid))
    if len(rest) == 2:
        cut = both[3].shape[0] // 2
        last = swap(jnp.concatenate([both[1], both[3][:cut], both[3][cut:]], axis=1), "dp", far)
    else:
        summed_qkv, summed_out = scatter_sum(both[:q], rest[1:]), scatter_sum(both[q:], rest_out[1:])
    down_mine, *down_split = seq(*sum_of(down_chip, [down_x], split=PIECES))
    down_theirs = seq(*core_swaps(down_split))
    down_theirs, r_theirs = jnp.concatenate(down_theirs), jnp.concatenate(r_b)
    output = seq(in_order((r_a + down_mine).astype(b16), (r_theirs + down_theirs).astype(b16)))
    gains = gains + gains_got
    for mask in rest[1:-1]:
        gains = gains + swap(gains, "dp", mask)
    if len(rest) == 2:
        last, *got_down = seq(last, *got_down)
        columns = both[0].shape[1]
        summed_qkv = both[0] + last[:, :columns]
        end = jnp.concatenate([last[:, columns : columns + block], last[:, columns + block :]])
        summed_out = both[2] + end
    summed_down = finish(keep[0], got_down)
    nq, nk = w_query.shape[1], w_key.shape[1]
    gains = gains + 0.0 * seq.token.astype(f32)
    return (
        output,
        grad_tokens,
        gains[:width],
        summed_qkv[:, :nq],
        summed_qkv[:, nq : nq + nk],
        summed_qkv[:, nq + nk :],
        gains[width : width + hd],
        gains[width + hd : width + 2 * hd],
        summed_out,
        gains[width + 2 * hd :],
        summed_pair[:block],
        summed_pair[block:],
        summed_down,
    )


def solution(mesh):
    in_specs = (
        P("dp", None),
        P(),
        P(None, "tensor"),
        P(None, "tensor"),
        P(None, "tensor"),
        P(),
        P(),
        P("tensor", None),
        P(),
        P(None, "tensor"),
        P(None, "tensor"),
        P("tensor", None),
        P("dp", None),
    )
    out_specs = (
        P("dp", None),
        P("dp", None),
        P(),
        P("dp", "tensor"),
        P("dp", "tensor"),
        P("dp", "tensor"),
        P(),
        P(),
        P("tensor", "dp"),
        P(),
        P("dp", "tensor"),
        P("dp", "tensor"),
        P("tensor", "dp"),
    )
    return jax.shard_map(body, mesh=mesh, in_specs=in_specs, out_specs=out_specs, check_vma=False)
```
